32 devices in a mesh: dp: 4 (over x, core), tensor: 8 (over z, y).
Axes of the slice: x: 2, y: 2, z: 4, core: 2. Of those that a mesh axis runs over, the one named last changes fastest.
Arguments:
- inputs: bfloat16 [2, 8192, 1024], P(None, ('dp', 'tensor')), may hold values from -6 to 6
- resets: int32 [2, 8192], P(None, ('dp', 'tensor')), may hold values 0 or 1
- cotangent: bfloat16 [2, 8192, 1024], P(None, ('dp', 'tensor')), may hold values from -6 to 6
- norm_gain: float32 [1024], replicated, may hold values from 0.5 to 1.5
- ema_alpha: float32 [1024, 16], replicated, may hold values from 0.02 to 0.2
- ema_damp: float32 [1024, 16], replicated, may hold values from 9.765625e-05 to 0.5
- ema_beta: float32 [1024, 16], replicated, may hold values from -4 to 4
- ema_eta: float32 [1024, 16], replicated, may hold values from -1.5 to 1.5
- ema_omega: float32 [1024], replicated, may hold values from -4 to 4
- w_gates: bfloat16 [1024, 2176], replicated, may hold values from -0.1875 to 0.1875
- b_gates: float32 [2176], replicated, may hold values from -3 to 3
- qk_gain: float32 [2, 128], replicated, may hold values from -4 to 4
- q_bias: float32 [128], replicated, may hold values from -3 to 3
- w_value: bfloat16 [1024, 2048], P(None, 'tensor'), may hold values from -0.1875 to 0.1875
- b_value: bfloat16 [2048], P('tensor'), may hold values from -3 to 3
- w_reset: bfloat16 [1024, 2048], P(None, 'tensor'), may hold values from -0.1875 to 0.1875
- b_reset: bfloat16 [2048], P('tensor'), may hold values from -3 to 3
- w_branch: bfloat16 [2048, 1024], P('tensor'), may hold values from -0.25 to 0.25
- ffn_gain: float32 [1024], replicated, may hold values from 0.5 to 1.5
- w_in: bfloat16 [1024, 4096], P(None, 'tensor'), may hold values from -0.1875 to 0.1875
- b_in: bfloat16 [4096], P('tensor'), may hold values from -3 to 3
- w_out: bfloat16 [4096, 1024], P('tensor'), may hold values from -0.09375 to 0.09375
- b_out: float32 [1024], replicated, may hold values from -3 to 3
Outputs:
- output: bfloat16 [2, 8192, 1024], P(None, ('dp', 'tensor'))
- grad_inputs: float32 [2, 8192, 1024], P(None, ('dp', 'tensor'))
- grad_norm_gain: float32 [1024], replicated
- grad_ema_alpha: float32 [1024, 16], replicated
- grad_ema_damp: float32 [1024, 16], replicated
- grad_ema_beta: float32 [1024, 16], replicated
- grad_ema_eta: float32 [1024, 16], replicated
- grad_ema_omega: float32 [1024], replicated
- grad_w_gates: float32 [1024, 2176], replicated
- grad_b_gates: float32 [2176], replicated
- grad_qk_gain: float32 [2, 128], replicated
- grad_q_bias: float32 [128], replicated
- grad_w_value: float32 [1024, 2048], P(None, 'tensor')
- grad_b_value: float32 [2048], P('tensor')
- grad_w_reset: float32 [1024, 2048], P(None, 'tensor')
- grad_b_reset: float32 [2048], P('tensor')
- grad_w_branch: float32 [2048, 1024], P('tensor')
- grad_ffn_gain: float32 [1024], replicated
- grad_w_in: float32 [1024, 4096], P(None, 'tensor')
- grad_b_in: float32 [4096], P('tensor')
- grad_w_out: float32 [4096, 1024], P('tensor')
- grad_b_out: float32 [1024], replicated
The draws below stay inside these ranges and needn't reach their ends.
Inputs may be any that keep to these rules, and one draw needn't show every extreme that they name: `resets`: 1 marks the first token of a document; the first token of every 2048-token segment starts a document whatever the mask says.
All inputs are finite; a program needn't handle non-finite values. No bound on the sum of `resets` on one device may be relied on, other than what follows from the above.
Results may differ from the reference program's by a relative error of at most 0.012.
The reference program's roundings to bfloat16 on the way count: a program that leaves them out, or rounds other values in their place, can miss the bound.
Values may be sent and summed in bfloat16 or wider, within the bound.
No kernel may reach another device: no remote copies, remote signals or barrier semaphores. Data moves between devices by JAX's collectives and lax.ppermute only.
A program may use at most 576 MiB of HBM per device.

```python
import math
from functools import partial
import jax
import jax.numpy as jnp
from jax import lax

D = 1024
Z = 128
V = 2048
H = 16
FF = 4096
BLOCK = 128
EMA_BLOCK = 32
MICRO = 2
SEG = 2048
TOKENS = 8192


def with_ends(values, rng, least, high):
    spot = [jax.random.randint(jax.random.fold_in(rng, axis), (), 0, length) for axis, length in enumerate(values.shape)]
    longest = values.shape.index(max(values.shape))
    next_to = spot[:longest] + [(spot[longest] + 1) % values.shape[longest]] + spot[longest + 1:]
    return values.at[tuple(spot)].set(least).at[tuple(next_to)].set(high)


def block_scale(own_key, dims, cuts, smallest, high):
    loudness, own = 1.0, jax.random.fold_in(own_key, 6)
    for dim, shards_of in cuts:
        heights = jnp.exp(jax.random.uniform(jax.random.fold_in(own, dim), (shards_of,), jnp.float32, smallest / len(cuts), high / len(cuts)))
        loudness = loudness * jnp.repeat(heights, dims[dim] // shards_of).reshape([-1 if axis == dim else 1 for axis in range(len(dims))])
    return loudness


def noise(key, shape, width, bound, split=(), kind=jnp.bfloat16):
    factor_of = block_scale(key, shape, split, -0.22, 0.18) if split else 1.0
    entries = jax.random.normal(key, shape, jnp.float32) * width * factor_of
    return jnp.minimum(jnp.maximum(entries, -bound), bound).astype(kind)


def setup_inputs(seed: int = 0) -> dict:
    keys = jax.random.split(jax.random.key(seed), 24)
    return {
        "inputs": noise(keys[0], (MICRO, TOKENS, D), 1.0, 6.0, ((1, 32),)),
        "resets": with_ends((jax.random.randint(keys[1], (MICRO, TOKENS), 0, SEG) < 2).astype(jnp.int32), jax.random.fold_in(keys[1], 1), 0, 1),
        "cotangent": noise(keys[2], (MICRO, TOKENS, D), 1.0, 6.0, ((1, 32),)),
        "norm_gain": jnp.clip(1.0 + 0.1 * jax.random.normal(keys[3], (D,), jnp.float32), 0.5, 1.5),
        "ema_alpha": jnp.clip(jnp.exp(jax.random.uniform(keys[4], (D, H), jnp.float32, math.log(0.02), math.log(0.2))), 0.02, 0.2),
        "ema_damp": jnp.clip(jnp.exp(jax.random.uniform(keys[5], (D, H), jnp.float32, math.log(9.765625145519152e-05), math.log(0.5))), 9.765625145519152e-05, 0.5),
        "ema_beta": noise(keys[6], (D, H), 1.0, 4.0, (), jnp.float32),
        "ema_eta": noise(keys[7], (D, H), H ** -0.5, 1.5, (), jnp.float32),
        "ema_omega": noise(keys[8], (D,), 1.0, 4.0, (), jnp.float32),
        "w_gates": noise(keys[9], (D, 2 * D + Z), D ** -0.5, 0.1875),
        "b_gates": noise(keys[10], (2 * D + Z,), 0.5, 3.0, (), jnp.float32),
        "qk_gain": noise(keys[11], (2, Z), 1.0, 4.0, (), jnp.float32),
        "q_bias": noise(keys[12], (Z,), 0.5, 3.0, (), jnp.float32),
        "w_value": noise(keys[13], (D, V), D ** -0.5, 0.1875, ((1, 8),)),
        "b_value": noise(keys[14], (V,), 0.5, 3.0, ((0, 8),)),
        "w_reset": noise(keys[15], (D, V), D ** -0.5, 0.1875, ((1, 8),)),
        "b_reset": noise(keys[16], (V,), 0.5, 3.0, ((0, 8),)),
        "w_branch": noise(keys[17], (V, D), (V // 4) ** -0.5, 0.25, ((0, 8),)),
        "ffn_gain": jnp.clip(1.0 + 0.1 * jax.random.normal(keys[18], (D,), jnp.float32), 0.5, 1.5),
        "w_in": noise(keys[19], (D, FF), D ** -0.5, 0.1875, ((1, 8),)),
        "b_in": noise(keys[20], (FF,), 0.5, 3.0, ((0, 8),)),
        "w_out": noise(keys[21], (FF, D), FF ** -0.5, 0.09375, ((0, 8),)),
        "b_out": noise(keys[22], (D,), 0.5, 3.0, (), jnp.float32),
    }


@jax.custom_vjp
def low(v):
    return lax.optimization_barrier(v.astype(jnp.bfloat16)).astype(jnp.float32)

@jax.custom_vjp
def low_back(v):
    return v

def low_keep(v):
    return (low(v), None)

def low_pass(kept, grad):
    return (grad,)

def back_keep(v):
    return (v, None)

def back_low(kept, grad):
    return (low(grad),)
low.defvjp(low_keep, low_pass)
low_back.defvjp(back_keep, back_low)
HIGHEST = lax.Precision.HIGHEST
EPSILON = 1e-06

def matmul(left_side, right_side):
    return jnp.dot(left_side, right_side, precision=HIGHEST)

def rms_scale(values, gain_row):
    return values * lax.rsqrt(lax.optimization_barrier(jnp.mean(values * values, axis=-1, keepdims=True)) + EPSILON) * gain_row

def ema_tables(rate_alpha, rate_damp, beta_in, eta_out, block_rows):
    log_decay = jnp.log(1.0 - rate_alpha * rate_damp)
    lag_steps = jnp.arange(block_rows).astype(rate_alpha.dtype)
    powers = jnp.exp(lag_steps[:, None, None] * log_decay[None])
    kernel = lax.optimization_barrier(jnp.sum(powers * (rate_alpha * beta_in * eta_out)[None], axis=-1))
    offsets = jnp.arange(block_rows)
    lag_index = offsets[:, None] - offsets[None, :]
    lower_mask = (lag_index >= 0).astype(rate_alpha.dtype)
    toeplitz = jnp.take(kernel, jnp.maximum(lag_index, 0), axis=0) * lower_mask[:, :, None]
    decay_rate = jnp.exp(log_decay)
    enter_table = powers * (decay_rate * eta_out)[None]
    leave_table = powers[::-1] * (rate_alpha * beta_in)[None]
    through = powers[-1] * decay_rate
    return (toeplitz, enter_table, leave_table, through)

def ema_block(tables, state_in, block_inputs):
    toeplitz, enter_table, leave_table, through = tables
    row_block, flag_block = block_inputs
    doc_index = jnp.cumsum(flag_block)
    offsets = jnp.arange(flag_block.shape[0])
    same_doc = ((doc_index[:, None] == doc_index[None, :]) & (offsets[:, None] >= offsets[None, :])).astype(row_block.dtype)
    before_reset = (doc_index == 0).astype(row_block.dtype)
    inner_sum = lax.optimization_barrier(jnp.sum(toeplitz * same_doc[:, :, None] * row_block[None, :, :], axis=1))
    outer_sum = before_reset[:, None] * lax.optimization_barrier(jnp.sum(enter_table * state_in[None], axis=-1))
    last_doc = (doc_index == doc_index[-1]).astype(row_block.dtype)
    keep_state = (doc_index[-1] == 0).astype(row_block.dtype)
    fresh_state = keep_state * through * state_in + lax.optimization_barrier(jnp.sum(leave_table * (row_block * last_doc[:, None])[:, :, None], axis=0))
    return (fresh_state, inner_sum + outer_sum)

def ema_run(normed, doc_flags, rate_alpha, rate_damp, beta_in, eta_out):
    tables = ema_tables(rate_alpha, rate_damp, beta_in, eta_out, EMA_BLOCK)
    start_state = jnp.zeros(rate_alpha.shape, normed.dtype)
    row_count = normed.shape[0]
    block_count = row_count // EMA_BLOCK
    final_state, smoothed = lax.scan(jax.checkpoint(partial(ema_block, tables)), start_state, (normed.reshape(block_count, EMA_BLOCK, -1), doc_flags.reshape(block_count, EMA_BLOCK)))
    return smoothed.reshape(row_count, -1)

def attend(query, key_rows, value, doc_flags):
    block_count = query.shape[0] // BLOCK
    doc_index = jnp.cumsum(doc_flags).reshape(block_count, BLOCK)
    offsets = jnp.arange(BLOCK)
    allowed = (doc_index[:, :, None] == doc_index[:, None, :]) & (offsets[:, None] >= offsets[None, :])[None]
    score_scale = query.shape[-1] ** (-0.5)
    scores = jnp.einsum('cik,cjk->cij', query.reshape(block_count, BLOCK, -1), key_rows.reshape(block_count, BLOCK, -1), precision=HIGHEST) * score_scale
    scores = jnp.where(allowed, scores, -1000000000.0)
    weights_soft = low(jax.nn.softmax(scores, axis=-1))
    result = jnp.einsum('cij,cjv->civ', weights_soft, value.reshape(block_count, BLOCK, -1), precision=HIGHEST)
    return result.reshape(query.shape[0], -1)

def forward(source, doc_flags, norm_gain, ema_alpha, ema_damp, ema_beta, ema_eta, ema_omega, w_gates, b_gates, qk_gain, q_bias, w_value, b_value, w_reset, b_reset, w_branch, ffn_gain, w_in, b_in, w_out, b_out):
    model_width = source.shape[-1]
    normed = rms_scale(source, norm_gain)
    smoothed = ema_run(normed, doc_flags, ema_alpha, ema_damp, ema_beta, ema_eta)
    blended = smoothed + ema_omega * normed
    mixed_low = low(jax.nn.silu(blended))
    normed_low = low(normed)
    gate_pre = low_back(matmul(mixed_low, w_gates) + b_gates)
    update = jax.nn.sigmoid(gate_pre[:, :model_width])
    direct = gate_pre[:, model_width:2 * model_width]
    shared = low(jax.nn.silu(gate_pre[:, 2 * model_width:]))
    query = low(shared * qk_gain[0] + q_bias)
    key_rows = low(shared * qk_gain[1])
    value = low(jax.nn.silu(low_back(matmul(normed_low, w_value) + b_value)))
    reset_gate = jax.nn.silu(low_back(matmul(mixed_low, w_reset) + b_reset))
    attended = low_back(attend(query, key_rows, value, doc_flags))
    gated = low(reset_gate * attended)
    branch = matmul(gated, w_branch)
    hidden = jax.nn.silu(direct + low_back(branch))
    mixed_out = update * hidden + (1.0 - update) * source
    ffn_normed = low(rms_scale(mixed_out, ffn_gain))
    pre_act = low_back(matmul(ffn_normed, w_in) + b_in)
    activ = low(jax.nn.silu(pre_act))
    return mixed_out + matmul(activ, w_out) + b_out

def reference(inputs, resets, cotangent, norm_gain, ema_alpha, ema_damp, ema_beta, ema_eta, ema_omega, w_gates, b_gates, qk_gain, q_bias, w_value, b_value, w_reset, b_reset, w_branch, ffn_gain, w_in, b_in, w_out, b_out):
    params = tuple((weight.astype(jnp.float32) for weight in (norm_gain, ema_alpha, ema_damp, ema_beta, ema_eta, ema_omega, w_gates, b_gates, qk_gain, q_bias, w_value, b_value, w_reset, b_reset, w_branch, ffn_gain, w_in, b_in, w_out, b_out)))
    seg_count = TOKENS // SEG
    model_width = inputs.shape[-1]
    positions = jnp.arange(SEG)

    def one_segment(totals, pieces):
        source_rows, reset_rows, grad_rows = pieces
        doc_flags = jnp.where(positions == 0, 1, reset_rows).astype(jnp.int32)

        def run_layer(values, *weights):
            return forward(values, doc_flags, *weights)
        result, pull_back = jax.vjp(run_layer, source_rows.astype(jnp.float32), *params)
        gradients = pull_back(grad_rows.astype(jnp.float32))
        fresh = tuple((total + grad_piece for total, grad_piece in zip(totals, gradients[1:])))
        return (fresh, (result.astype(jnp.bfloat16), gradients[0]))
    totals = tuple((jnp.zeros(weight.shape, jnp.float32) for weight in params))
    results = []
    input_grads = []
    for micro_index in range(MICRO):
        totals, (result_rows, grad_rows_in) = lax.scan(one_segment, totals, (inputs[micro_index].reshape(seg_count, SEG, model_width), resets[micro_index].reshape(seg_count, SEG), cotangent[micro_index].reshape(seg_count, SEG, model_width)))
        results.append(result_rows.reshape(TOKENS, model_width))
        input_grads.append(grad_rows_in.reshape(TOKENS, model_width))
    grad_norm_gain, grad_ema_alpha, grad_ema_damp, grad_ema_beta, grad_ema_eta, grad_ema_omega, grad_w_gates, grad_b_gates, grad_qk_gain, grad_q_bias, grad_w_value, grad_b_value, grad_w_reset, grad_b_reset, grad_w_branch, grad_ffn_gain, grad_w_in, grad_b_in, grad_w_out, grad_b_out = totals
    return (jnp.stack(results), jnp.stack(input_grads), grad_norm_gain, grad_ema_alpha, grad_ema_damp, grad_ema_beta, grad_ema_eta, grad_ema_omega, grad_w_gates, grad_b_gates, grad_qk_gain, grad_q_bias, grad_w_value, grad_b_value, grad_w_reset, grad_b_reset, grad_w_branch, grad_ffn_gain, grad_w_in, grad_b_in, grad_w_out, grad_b_out)
```

```python
from functools import partial

import jax
import jax.numpy as jnp
from jax import lax
from jax.experimental import pallas as pl
from jax.experimental.pallas import tpu as pltpu
from jax.sharding import PartitionSpec as P

BLOCK = 128
HIGHEST = lax.Precision.HIGHEST
EPSILON = 1e-06
AXES = ("dp", "tensor")
F32 = jnp.float32
BF16 = jnp.bfloat16


def dot_plain(a, b):
    return jnp.dot(a, b, preferred_element_type=F32)


def dot_against(a, b):
    return lax.dot_general(a, b, (((1,), (1,)), ((), ())), preferred_element_type=F32)


def dot_over_rows(a, b):
    return lax.dot_general(a, b, (((0,), (0,)), ((), ())), preferred_element_type=F32)


def rounded(v):
    return lax.reduce_precision(v, exponent_bits=8, mantissa_bits=7)


def silu_slope(v):
    s = jax.nn.sigmoid(v)
    return s * (1.0 + v * (1.0 - s))


class Grid:
    def __init__(self):
        dp, tensor = lax.axis_size("dp"), lax.axis_size("tensor")
        self.size = {"x": dp // 2, "c": 2, "z": 4, "y": tensor // 4}
        d, t = lax.axis_index("dp"), lax.axis_index("tensor")
        self.at = {"x": d // 2, "c": d % 2, "z": t // self.size["y"], "y": t % self.size["y"]}

    def send(self, value, digit, shift, wrap=True):
        n = self.size
        pairs = []
        for x in range(n["x"]):
            for c in range(n["c"]):
                for z in range(n["z"]):
                    for y in range(n["y"]):
                        here = {"x": x, "c": c, "z": z, "y": y}
                        there = dict(here)
                        there[digit] = here[digit] + shift
                        if not wrap and not 0 <= there[digit] < n[digit]:
                            continue
                        there[digit] %= n[digit]
                        pairs.append(tuple(
                            ((k["x"] * n["c"] + k["c"]) * n["z"] + k["z"]) * n["y"] + k["y"]
                            for k in (here, there)
                        ))
        return lax.ppermute(value, AXES, pairs)


def ema_step(state, row, keep, decay, feed):
    return [(s * keep) * q + f * row for s, q, f in zip(state, decay, feed)]


def row_of(ref, base, r):
    return ref[pl.ds(base + r, 8, stride=8), :]


def spread(ref, block, values):
    for j in range(8):
        ref[pl.ds(pl.multiple_of(block * 64, 64) + 8 * j, 8), :] = values[:, j * 128 : (j + 1) * 128]


def collect(ref, block):
    return jnp.concatenate(
        [ref[pl.ds(pl.multiple_of(block * 64, 64) + 8 * j, 8), :] for j in range(8)], axis=1
    )


def norm_kernel(flags, x_ref, gain_ref, decay_ref, feed_ref, normed_ref, low_ref, final_ref):
    micros, rows = flags.shape
    heads = decay_ref.shape[0]

    def norm_block(b, carry):
        at = pl.ds(pl.multiple_of(b * 16, 16), 16)
        x = x_ref[at, :].astype(F32)
        n = x * lax.rsqrt(jnp.mean(x * x, axis=-1, keepdims=True) + EPSILON) * gain_ref[...]
        low_ref[at, :] = n.astype(BF16)
        spread(normed_ref, 2 * b, n[:8])
        spread(normed_ref, 2 * b + 1, n[8:])
        return carry

    lax.fori_loop(0, micros * rows // 16, norm_block, 0)
    for m in range(micros):
        for h0 in range(0, heads, 8):
            decay = [decay_ref[h0 + h] for h in range(8)]
            feed = [feed_ref[h0 + h] for h in range(8)]

            def block(b, state, m=m, decay=decay, feed=feed):
                base = pl.multiple_of((m * (rows // 8) + b) * 64, 64)
                for r in range(8):
                    keep = (1 - flags[m, b * 8 + r]).astype(F32)
                    state = ema_step(state, row_of(normed_ref, base, r), keep, decay, feed)
                return state

            state = lax.fori_loop(0, rows // 8, block, [jnp.zeros((8, 128), F32)] * 8)
            for h in range(8):
                final_ref[m, h0 + h] = state[h]


def blend_kernel(
    flags, normed_ref, start_ref, decay_ref, feed_ref, out_ref, omega_ref, blended_ref, low_ref, acc_ref
):
    micros, rows = flags.shape
    heads = decay_ref.shape[0]
    omega = omega_ref[...]
    for m in range(micros):
        for h0 in range(0, heads, 8):
            decay = [decay_ref[h0 + h] for h in range(8)]
            feed = [feed_ref[h0 + h] for h in range(8)]
            tell = [out_ref[h0 + h] for h in range(8)]

            def block(b, state, m=m, h0=h0, decay=decay, feed=feed, tell=tell):
                base = pl.multiple_of((m * (rows // 8) + b) * 64, 64)
                for r in range(8):
                    keep = (1 - flags[m, b * 8 + r]).astype(F32)
                    row = row_of(normed_ref, base, r)
                    state = ema_step(state, row, keep, decay, feed)
                    told = [s * t for s, t in zip(state, tell)]
                    while len(told) > 1:
                        told = [told[i] + told[i + 1] for i in range(0, len(told), 2)]
                    at = pl.ds(base + r, 8, stride=8)
                    if h0 == 0:
                        acc_ref[at, :] = told[0] + omega * row
                    else:
                        acc_ref[at, :] = acc_ref[at, :] + told[0]
                return state

            lax.fori_loop(0, rows // 8, block, [start_ref[m, h0 + h] for h in range(8)])

    def finish(b, carry):
        at = pl.ds(pl.multiple_of(b * 16, 16), 16)
        v = jnp.concatenate([collect(acc_ref, 2 * b), collect(acc_ref, 2 * b + 1)], axis=0)
        blended_ref[at, :] = v
        low_ref[at, :] = (v / (1.0 + jnp.exp(-v))).astype(BF16)
        return carry

    lax.fori_loop(0, micros * rows // 16, finish, 0)


def back_first_kernel(flags, grad_ref, decay_ref, tell_ref, left_ref, rows_ref):
    micros, rows = flags.shape
    heads = decay_ref.shape[0]

    def lay(b, carry):
        spread(rows_ref, b, grad_ref[pl.ds(pl.multiple_of(b * 8, 8), 8), :])
        return carry

    lax.fori_loop(0, micros * rows // 8, lay, 0)
    for m in range(micros):
        for h0 in range(0, heads, 8):
            decay = [decay_ref[h0 + h] for h in range(8)]
            tell = [tell_ref[h0 + h] for h in range(8)]

            def block(i, left, m=m, decay=decay, tell=tell):
                b = rows // 8 - 1 - i
                base = pl.multiple_of((m * (rows // 8) + b) * 64, 64)
                for r in reversed(range(8)):
                    keep = (1 - flags[m, b * 8 + r]).astype(F32)
                    row = row_of(rows_ref, base, r)
                    left = [((t * row + k) * keep) * q for k, q, t in zip(left, decay, tell)]
                return left

            left = lax.fori_loop(0, rows // 8, block, [jnp.zeros((8, 128), F32)] * 8)
            for h in range(8):
                left_ref[m, h0 + h] = left[h]


def back_kernel(
    flags, normed_ref, rows_ref, start_ref, right_ref, decay_ref, feed_ref, tell_ref,
    grad_ref, eta_ref, one_ref, two_ref, states, acc_ref,
):
    micros, rows = flags.shape
    heads = decay_ref.shape[0]
    group = 4
    for m in range(micros):
        for h0 in range(0, heads, group):
            decay = [decay_ref[h0 + h] for h in range(group)]
            feed = [feed_ref[h0 + h] for h in range(group)]
            tell = [tell_ref[h0 + h] for h in range(group)]

            def ahead(b, state, m=m, decay=decay, feed=feed):
                base = pl.multiple_of((m * (rows // 8) + b) * 64, 64)
                for r in range(8):
                    keep = (1 - flags[m, b * 8 + r]).astype(F32)
                    for h in range(group):
                        states[b * 8 + r, h] = state[h]
                    state = ema_step(state, row_of(normed_ref, base, r), keep, decay, feed)
                return state

            last = lax.fori_loop(0, rows // 8, ahead, [start_ref[m, h0 + h] for h in range(group)])

            def back(i, carry, m=m, h0=h0, decay=decay, feed=feed, tell=tell):
                left, after, eta, one, two = carry
                b = rows // 8 - 1 - i
                base = pl.multiple_of((m * (rows // 8) + b) * 64, 64)
                for r in reversed(range(8)):
                    keep = (1 - flags[m, b * 8 + r]).astype(F32)
                    g = row_of(rows_ref, base, r)
                    x = row_of(normed_ref, base, r)
                    before = [states[b * 8 + r, h] for h in range(group)]
                    eta = [e + s * g for e, s in zip(eta, after)]
                    now = [t * g + k for t, k in zip(tell, left)]
                    one = [o + n * x for o, n in zip(one, now)]
                    kept = [n * keep for n in now]
                    two = [w + k * s for w, k, s in zip(two, kept, before)]
                    left = [k * q for k, q in zip(kept, decay)]
                    gn = [n * f for n, f in zip(now, feed)]
                    while len(gn) > 1:
                        gn = [gn[i] + gn[i + 1] for i in range(0, len(gn), 2)]
                    at = pl.ds(base + r, 8, stride=8)
                    if h0 == 0:
                        acc_ref[at, :] = gn[0]
                    else:
                        acc_ref[at, :] = acc_ref[at, :] + gn[0]
                    after = before
                return left, after, eta, one, two

            zero = [jnp.zeros((8, 128), F32)] * group
            if m == 0:
                sums = (zero, zero, zero)
            else:
                sums = tuple([ref[h0 + h] for h in range(group)] for ref in (eta_ref, one_ref, two_ref))
            right = [right_ref[m, h0 + h] for h in range(group)]
            _, _, eta, one, two = lax.fori_loop(0, rows // 8, back, (right, last, *sums))
            for h in range(group):
                eta_ref[h0 + h] = eta[h]
                one_ref[h0 + h] = one[h]
                two_ref[h0 + h] = two[h]

    def finish(b, carry):
        grad_ref[pl.ds(pl.multiple_of(b * 8, 8), 8), :] = collect(acc_ref, b)
        return carry

    lax.fori_loop(0, micros * rows // 8, finish, 0)


def call(kernel, outs, scratch, smem, *arrays):
    return pl.pallas_call(
        kernel,
        out_shape=outs,
        in_specs=[pl.BlockSpec(memory_space=pltpu.SMEM)] * smem
        + [pl.BlockSpec(memory_space=pltpu.VMEM)] * (len(arrays) - smem),
        out_specs=jax.tree.map(lambda _: pl.BlockSpec(memory_space=pltpu.VMEM), outs),
        scratch_shapes=scratch,
    )(*arrays)


def scan_carry(grid, local, clear, whole, reverse):
    sign = -1 if reverse else 1
    micros, heads = local.shape[:2]
    flag = jnp.broadcast_to(clear[:, None, None, None], (micros, 1, 8, 128))
    pack = jnp.concatenate([local, flag], axis=1)
    n = grid.size["y"]
    near = [pack] + [grid.send(pack, "y", sign * r) for r in range(1, n)]
    stack = jnp.stack(near)
    at = grid.at["y"] if not reverse else n - 1 - grid.at["y"]
    ordered = [lax.dynamic_index_in_dim(stack, (at - a) % n, 0, False) for a in range(n)]
    inner = jnp.zeros_like(local)
    through = jnp.ones((micros, 1, 8, 128), F32)
    mine, reach = inner, through
    power = jnp.ones_like(whole)
    mine_power = power
    for a in range(n):
        mine = jnp.where(at == a, inner, mine)
        reach = jnp.where(at == a, through, reach)
        mine_power = jnp.where(at == a, power, mine_power)
        inner = ordered[a][:, :heads] + ordered[a][:, heads:] * whole * inner
        through = through * ordered[a][:, heads:]
        power = power * whole
    pack = jnp.concatenate([inner, through], axis=1)
    entering = jnp.zeros_like(local)
    factor = jnp.ones((micros, 1, 8, 128), F32)
    scale = jnp.ones_like(whole)
    for k in range(1, grid.size["z"]):
        got = grid.send(pack, "z", sign * k, wrap=False)
        entering = entering + factor * scale * got[:, :heads]
        factor = factor * got[:, heads:]
        scale = scale * power
    return mine + reach * mine_power * entering


def gather_units(grid, seed, split_x):
    parts = {(0, 0): {(0, 0): seed}}
    for k in range(1, grid.size["z"]):
        parts[k, 0] = {(0, 0): grid.send(seed, "z", k)}
    for kz in range(grid.size["z"]):
        for k in range(1, grid.size["y"]):
            parts[kz, k] = {(0, 0): grid.send(parts[kz, 0][0, 0], "y", k)}
    if split_x:
        for key in parts:
            parts[key][0, 1] = grid.send(parts[key][0, 0], "x", 1)
    for key in parts:
        for kx in range(2 if split_x else 1):
            parts[key][1, kx] = grid.send(parts[key][0, kx], "c", 1)
    return parts


def in_order(parts):
    return [parts[key][sub] for key in sorted(parts) for sub in sorted(parts[key])]


def scatter_sum(grid, value, stages):
    for digit, axis, relative in stages:
        n = grid.size[digit]
        at = grid.at[digit]

        def part(r, value=value, axis=axis, relative=relative, n=n, at=at):
            if relative:
                return lax.index_in_dim(value, r, axis, True)
            return lax.dynamic_slice_in_dim(value, (at - r) % n, 1, axis)

        total = part(0).astype(F32)
        for r in range(1, n):
            total = total + grid.send(part(r), digit, -r).astype(F32)
        value = total.astype(BF16)
    return value


def local(
    inputs, resets, cotangent, norm_gain, ema_alpha, ema_damp, ema_beta, ema_eta, ema_omega,
    w_gates, b_gates, qk_gain, q_bias, w_value, b_value, w_reset, b_reset, w_branch, ffn_gain,
    w_in, b_in, w_out, b_out,
):
    grid = Grid()
    size, at = grid.size, grid.at
    micros, rows, width = inputs.shape
    total = micros * rows
    heads = ema_alpha.shape[1]
    rank = lax.axis_index("tensor")
    units_v, units_f = w_value.shape[1], w_in.shape[1]
    n_tensor = lax.axis_size("tensor")
    split_x = size["x"] == 2

    half_v = units_v // 2
    part_f = units_f // (4 if split_x else 2)
    off_v = at["c"] * half_v
    off_f = (at["c"] * 2 + at["x"] if split_x else at["c"]) * part_f
    cols = lambda w, o, n: lax.dynamic_slice_in_dim(w, o, n, 1)
    rws = lambda w, o, n: lax.dynamic_slice_in_dim(w, o, n, 0)
    seed_vr = jnp.concatenate([cols(w_value, off_v, half_v), cols(w_reset, off_v, half_v)], axis=0)
    got_vr = in_order(gather_units(grid, seed_vr, False))
    got_b = in_order(gather_units(grid, rws(w_branch, off_v, half_v), False))
    got_i = in_order(gather_units(grid, cols(w_in, off_f, part_f), split_x))
    got_o = in_order(gather_units(grid, rws(w_out, off_f, part_f), split_x))
    all_value = jnp.concatenate([p[:width] for p in got_vr], axis=1)
    all_reset = jnp.concatenate([p[width:] for p in got_vr], axis=1)
    all_branch = jnp.concatenate(got_b, axis=0)
    all_in = jnp.concatenate(got_i, axis=1)
    all_out = jnp.concatenate(got_o, axis=0)

    table = lax.all_gather(
        jnp.concatenate([b_value, b_reset, b_in])[None], "tensor", axis=0, tiled=True
    ).astype(F32)
    zs = [(at["z"] - k) % size["z"] for k in range(size["z"])]
    ys = [(at["y"] - k) % size["y"] for k in range(size["y"])]
    owners = jnp.stack([z * size["y"] + y for z in zs for y in ys])
    subs_v = jnp.stack([at["c"], 1 - at["c"]])
    subs_f = (
        jnp.stack([c * 2 + x for c in (at["c"], 1 - at["c"]) for x in (at["x"], 1 - at["x"])])
        if split_x
        else subs_v
    )
    place_v = (owners[:, None] * 2 + subs_v[None]).reshape(-1)
    n_f = 4 if split_x else 2
    place_f = (owners[:, None] * n_f + subs_f[None]).reshape(-1)
    bias_v = jnp.take(table[:, :units_v].reshape(-1, half_v), place_v, axis=0).reshape(1, -1)
    bias_r = jnp.take(table[:, units_v : 2 * units_v].reshape(-1, half_v), place_v, axis=0).reshape(1, -1)
    bias_i = jnp.take(table[:, 2 * units_v :].reshape(-1, part_f), place_f, axis=0).reshape(1, -1)

    offsets = rank * rows + jnp.arange(rows)
    flags = jnp.where(offsets[None] == 0, 1, resets).astype(jnp.int32)
    tile = lambda a: a.T.reshape(heads, 8, 128)
    decay = tile(1.0 - ema_alpha * ema_damp)
    feed = tile(ema_alpha * ema_beta)
    tell = tile(ema_eta)
    whole = jnp.exp(rows * jnp.log(decay))[None]
    clear = (jnp.sum(flags, axis=1) == 0).astype(F32)
    source_low = inputs.reshape(total, width)
    laid = jax.ShapeDtypeStruct((total * 8, 128), F32)
    wide = jax.ShapeDtypeStruct((total, width), F32)
    wide_low = jax.ShapeDtypeStruct((total, width), BF16)
    states = jax.ShapeDtypeStruct((micros, heads, 8, 128), F32)
    sums = jax.ShapeDtypeStruct((heads, 8, 128), F32)
    normed_laid, normed_low, final = call(
        norm_kernel, (laid, wide_low, states), [], 1,
        flags, source_low, norm_gain[None], decay, feed,
    )
    start = scan_carry(grid, final, clear, whole, False)
    blended, mixed_low = call(
        blend_kernel, (wide, wide_low), [pltpu.VMEM((total * 8, 128), F32)], 1,
        flags, normed_laid, start, decay, feed, tell, ema_omega.reshape(8, 128),
    )

    source = source_low.astype(F32)
    scale_in = lax.rsqrt(jnp.mean(source * source, axis=-1, keepdims=True) + EPSILON)
    gate_pre = dot_plain(mixed_low, w_gates) + b_gates
    update = jax.nn.sigmoid(gate_pre[:, :width])
    direct = gate_pre[:, width : 2 * width]
    shared_pre = gate_pre[:, 2 * width :]
    shared = rounded(jax.nn.silu(shared_pre))
    query = (shared * qk_gain[0] + q_bias).astype(BF16)
    key = (shared * qk_gain[1]).astype(BF16)
    blocks = total // BLOCK
    doc = jnp.cumsum(flags.reshape(blocks, BLOCK), axis=1)
    order = jnp.arange(BLOCK)
    allowed = (doc[:, :, None] == doc[:, None, :]) & (order[:, None] >= order[None, :])[None]
    score_scale = query.shape[-1] ** (-0.5)
    query_b, key_b = query.reshape(blocks, BLOCK, -1), key.reshape(blocks, BLOCK, -1)
    scores = jnp.einsum("cik,cjk->cij", query_b, key_b, preferred_element_type=F32) * score_scale
    scores = jnp.where(allowed, scores, -1000000000.0)
    probs = jax.nn.softmax(scores, axis=-1)
    probs_low = probs.astype(BF16)

    value_pre = dot_plain(normed_low, all_value) + bias_v
    value_low = jax.nn.silu(value_pre).astype(BF16)
    reset_pre = dot_plain(mixed_low, all_reset) + bias_r
    reset_gate = jax.nn.silu(reset_pre)
    value_b = value_low.reshape(blocks, BLOCK, -1)
    attended = jnp.einsum(
        "cij,cjv->civ", probs_low, value_b, preferred_element_type=F32
    ).reshape(total, -1)
    gated_low = (reset_gate * attended).astype(BF16)
    branch = dot_plain(gated_low, all_branch)
    pre_hidden = direct + branch
    hidden = jax.nn.silu(pre_hidden)
    mixed_out = update * hidden + (1.0 - update) * source
    scale_mid = lax.rsqrt(jnp.mean(mixed_out * mixed_out, axis=-1, keepdims=True) + EPSILON)
    ffn_low = (mixed_out * scale_mid * ffn_gain).astype(BF16)
    pre_act = dot_plain(ffn_low, all_in) + bias_i
    activ_low = jax.nn.silu(pre_act).astype(BF16)
    grad_low = cotangent.reshape(total, width)
    grad_out = grad_low.astype(F32)
    feed_out = dot_plain(activ_low, all_out)
    output = (mixed_out + feed_out + b_out).astype(BF16)

    n_z, n_y, n_x = size["z"], size["y"], size["x"]

    def sum_f(d, order):
        if split_x:
            d = d.reshape(n_z, n_y, 2, 2, part_f, width)
        else:
            d = d.reshape(n_z, n_y, 2, n_x, part_f // n_x, width)
        kinds = {"c": ("c", 2, True), "x": ("x", 3, split_x), "y": ("y", 1, True), "z": ("z", 0, True)}
        d = scatter_sum(grid, d, [kinds[k] for k in order])
        d = d.reshape(-1, width)
        everyone = lax.all_gather(d, "dp", axis=0, tiled=False)
        everyone = everyone.reshape(n_x, 2, -1, width).transpose(1, 0, 2, 3)
        return everyone.reshape(units_f, width).astype(F32)

    def sum_v(d, order):
        d = d.reshape(n_z, n_y, 2, n_x, half_v // n_x, width)
        kinds = {"c": ("c", 2, True), "x": ("x", 3, False), "y": ("y", 1, True), "z": ("z", 0, True)}
        d = scatter_sum(grid, d, [kinds[k] for k in order])
        d = d.reshape(-1, width)
        everyone = lax.all_gather(d, "dp", axis=0, tiled=False)
        everyone = everyone.reshape(n_x, 2, -1, width).transpose(1, 0, 2, 3)
        return everyone.reshape(units_v, width).astype(F32)

    grad_w_out = sum_f(dot_over_rows(activ_low, grad_low).astype(BF16), "cxyz")
    grad_act = dot_against(grad_low, all_out)
    grad_pre_low = (grad_act * silu_slope(pre_act)).astype(BF16)
    grad_w_in = sum_f(dot_over_rows(grad_pre_low, ffn_low).astype(BF16), "cyxz").T
    sum_b_in = jnp.sum(rounded(grad_act * silu_slope(pre_act)), axis=0)
    grad_ffn = dot_against(grad_pre_low, all_in)

    scaled = mixed_out * scale_mid
    sum_ffn_gain = jnp.sum(grad_ffn * scaled, axis=0)
    inner = grad_ffn * ffn_gain
    grad_mixed = (
        grad_out + scale_mid * (inner - scaled * jnp.mean(inner * scaled, axis=-1, keepdims=True))
    )
    grad_source = grad_mixed * (1.0 - update)
    grad_update_pre = grad_mixed * (hidden - source) * update * (1.0 - update)
    grad_hidden_pre = grad_mixed * update * silu_slope(pre_hidden)
    grad_hidden_low = grad_hidden_pre.astype(BF16)
    grad_gated = dot_against(grad_hidden_low, all_branch)
    grad_w_branch = sum_v(dot_over_rows(gated_low, grad_hidden_low).astype(BF16), "cxyz")
    grad_attended_low = (grad_gated * reset_gate).astype(BF16)
    grad_reset_low = (grad_gated * attended * silu_slope(reset_pre)).astype(BF16)
    grad_w_reset = sum_v(dot_over_rows(grad_reset_low, mixed_low).astype(BF16), "cyxz").T
    sum_b_reset = jnp.sum(rounded(grad_gated * attended * silu_slope(reset_pre)), axis=0)
    grad_b = grad_attended_low.reshape(blocks, BLOCK, -1)
    grad_probs = jnp.einsum("civ,cjv->cij", grad_b, value_b, preferred_element_type=F32)
    grad_value = jnp.einsum(
        "cij,civ->cjv", probs_low, grad_b, preferred_element_type=F32
    ).reshape(total, -1)
    grad_value_low = (grad_value * silu_slope(value_pre)).astype(BF16)
    grad_w_value = sum_v(dot_over_rows(grad_value_low, normed_low).astype(BF16), "cxyz").T
    sum_b_value = jnp.sum(rounded(grad_value * silu_slope(value_pre)), axis=0)
    grad_scores = (
        probs * (grad_probs - jnp.sum(grad_probs * probs, axis=-1, keepdims=True)) * score_scale
    )
    grad_query = jnp.einsum(
        "cij,cjk->cik", grad_scores, key_b.astype(F32), precision=HIGHEST
    ).reshape(total, -1)
    grad_key = jnp.einsum(
        "cij,cik->cjk", grad_scores, query_b.astype(F32), precision=HIGHEST
    ).reshape(total, -1)
    sum_qk = jnp.stack([jnp.sum(grad_query * shared, axis=0), jnp.sum(grad_key * shared, axis=0)])
    sum_q_bias = jnp.sum(grad_query, axis=0)
    grad_shared_pre = (grad_query * qk_gain[0] + grad_key * qk_gain[1]) * silu_slope(shared_pre)
    grad_gates = rounded(
        jnp.concatenate([grad_update_pre, grad_hidden_pre, grad_shared_pre], axis=1)
    )
    grad_gates_low = grad_gates.astype(BF16)
    sum_b_gates = jnp.sum(grad_gates, axis=0)
    d_gates = dot_over_rows(mixed_low, grad_gates_low).astype(BF16)
    n_all = n_x * 2 * n_tensor
    d_gates = d_gates.reshape(n_x, 2, n_z, n_y, width // n_all, -1)
    d_gates = scatter_sum(
        grid, d_gates, [("c", 1, False), ("y", 3, False), ("x", 0, False), ("z", 2, False)]
    ).reshape(width // n_all, -1)
    grad_w_gates = lax.all_gather(d_gates, AXES, axis=0, tiled=True).astype(F32)
    grad_mixed_in = dot_against(grad_reset_low, all_reset) + dot_against(grad_gates_low, w_gates)
    grad_blended = grad_mixed_in * silu_slope(blended)
    left, grad_laid = call(
        back_first_kernel, (states, laid), [], 1, flags, grad_blended, decay, tell
    )
    right = scan_carry(grid, left, clear, whole, True)
    grad_normed_ema, sum_eta, sum_one, sum_two = call(
        back_kernel, (wide, sums, sums, sums),
        [pltpu.VMEM((rows, 4, 8, 128), F32), pltpu.VMEM((total * 8, 128), F32)], 1,
        flags, normed_laid, grad_laid, start, right, decay, feed, tell,
    )
    grad_normed = (
        dot_against(grad_value_low, all_value) + grad_blended * ema_omega + grad_normed_ema
    )
    scaled_in = source * scale_in
    normed = scaled_in * norm_gain
    sum_omega = jnp.sum(grad_blended * normed, axis=0)
    sum_norm_gain = jnp.sum(grad_normed * scaled_in, axis=0)
    inner = grad_normed * norm_gain
    grad_inputs = grad_source + scale_in * (
        inner - scaled_in * jnp.mean(inner * scaled_in, axis=-1, keepdims=True)
    )

    put = lambda v, place: jnp.zeros((place.size, v.size // place.size), F32).at[place].set(
        v.reshape(place.size, -1)
    ).reshape(-1)
    pieces = [
        sum_eta.reshape(-1), sum_one.reshape(-1), sum_two.reshape(-1),
        sum_norm_gain, sum_omega, sum_b_gates, sum_qk.reshape(-1), sum_q_bias, sum_ffn_gain,
        jnp.sum(grad_out, axis=0),
        put(sum_b_value, place_v), put(sum_b_reset, place_v), put(sum_b_in, place_f),
    ]
    packed = lax.psum(jnp.concatenate(pieces).reshape(-1, 128), AXES).reshape(-1)
    cut, at_piece = [], 0
    for p in pieces:
        cut.append(packed[at_piece : at_piece + p.size])
        at_piece += p.size
    untile = lambda v: v.reshape(heads, width).T
    eta, one, two = (untile(v) for v in cut[:3])
    own = lambda v, n: lax.dynamic_slice_in_dim(v, rank * n, n, 0)
    return (
        output.reshape(inputs.shape),
        grad_inputs.reshape(inputs.shape),
        cut[3],
        ema_beta * one - ema_damp * two,
        -ema_alpha * two,
        ema_alpha * one,
        eta,
        cut[4],
        grad_w_gates,
        cut[5],
        cut[6].reshape(2, -1),
        cut[7],
        grad_w_value,
        own(cut[10], units_v),
        grad_w_reset,
        own(cut[11], units_v),
        grad_w_branch,
        cut[8],
        grad_w_in,
        own(cut[12], units_f),
        grad_w_out,
        cut[9],
    )


def solution(mesh):
    rows = P(None, AXES, None)
    col, row, vec, rep = P(None, "tensor"), P("tensor", None), P("tensor"), P()
    return jax.shard_map(
        local,
        mesh=mesh,
        in_specs=(
            rows, P(None, AXES), rows, rep, rep, rep, rep, rep, rep, rep, rep, rep, rep,
            col, vec, col, vec, row, rep, col, vec, row, rep,
        ),
        out_specs=(
            rows, rows, rep, rep, rep, rep, rep, rep, rep, rep, rep, rep,
            col, vec, col, vec, row, rep, col, vec, row, rep,
        ),
        check_vma=False,
    )
```

```python
from functools import partial

import jax
import jax.numpy as jnp
from jax import lax
from jax.experimental import pallas as pl
from jax.experimental.pallas import tpu as pltpu
from jax.sharding import PartitionSpec as P

BLOCK = 128
HIGHEST = lax.Precision.HIGHEST
EPSILON = 1e-06
AXES = ("dp", "tensor")
F32 = jnp.float32
BF16 = jnp.bfloat16


def dot_plain(a, b):
    return jnp.dot(a, b, preferred_element_type=F32)


def dot_against(a, b):
    return lax.dot_general(a, b, (((1,), (1,)), ((), ())), preferred_element_type=F32)


def dot_over_rows(a, b):
    return lax.dot_general(a, b, (((0,), (0,)), ((), ())), preferred_element_type=F32)


def rounded(v):
    return lax.reduce_precision(v, exponent_bits=8, mantissa_bits=7)


def silu_slope(v):
    s = jax.nn.sigmoid(v)
    return s * (1.0 + v * (1.0 - s))


class Grid:
    def __init__(self):
        dp, tensor = lax.axis_size("dp"), lax.axis_size("tensor")
        self.count = dp * tensor
        self.index = lax.axis_index("dp") * tensor + lax.axis_index("tensor")
        masks = lambda n, first: [first << k for k in range(n.bit_length() - 1)]
        self.tensor = masks(tensor, 1)
        self.core, *self.xs = masks(dp, tensor)

    def bit(self, mask):
        return (self.index // mask) % 2

    def swap(self, value, mask):
        return lax.ppermute(value, AXES, [(i, i ^ mask) for i in range(self.count)])


def ema_step(state, row, keep, decay, feed):
    return [(s * keep) * q + f * row for s, q, f in zip(state, decay, feed)]


def row_of(ref, base, r):
    return ref[pl.ds(base + r, 8, stride=8), :]


def spread(ref, block, values):
    for j in range(8):
        ref[pl.ds(pl.multiple_of(block * 64, 64) + 8 * j, 8), :] = values[:, j * 128 : (j + 1) * 128]


def collect(ref, block):
    return jnp.concatenate(
        [ref[pl.ds(pl.multiple_of(block * 64, 64) + 8 * j, 8), :] for j in range(8)], axis=1
    )


def norm_kernel(flags, x_ref, gain_ref, decay_ref, feed_ref, normed_ref, low_ref, final_ref):
    micros, rows = flags.shape
    heads = decay_ref.shape[0]

    def norm_block(b, carry):
        at = pl.ds(pl.multiple_of(b * 16, 16), 16)
        x = x_ref[at, :].astype(F32)
        n = x * lax.rsqrt(jnp.mean(x * x, axis=-1, keepdims=True) + EPSILON) * gain_ref[...]
        low_ref[at, :] = n.astype(BF16)
        spread(normed_ref, 2 * b, n[:8])
        spread(normed_ref, 2 * b + 1, n[8:])
        return carry

    lax.fori_loop(0, micros * rows // 16, norm_block, 0)
    for m in range(micros):
        for h0 in range(0, heads, 8):
            decay = [decay_ref[h0 + h] for h in range(8)]
            feed = [feed_ref[h0 + h] for h in range(8)]

            def block(b, state, m=m, decay=decay, feed=feed):
                base = pl.multiple_of((m * (rows // 8) + b) * 64, 64)
                for r in range(8):
                    keep = (1 - flags[m, b * 8 + r]).astype(F32)
                    state = ema_step(state, row_of(normed_ref, base, r), keep, decay, feed)
                return state

            state = lax.fori_loop(0, rows // 8, block, [jnp.zeros((8, 128), F32)] * 8)
            for h in range(8):
                final_ref[m, h0 + h] = state[h]


def blend_kernel(
    flags, normed_ref, start_ref, decay_ref, feed_ref, out_ref, omega_ref, blended_ref, low_ref, acc_ref
):
    micros, rows = flags.shape
    heads = decay_ref.shape[0]
    omega = omega_ref[...]
    for m in range(micros):
        for h0 in range(0, heads, 8):
            decay = [decay_ref[h0 + h] for h in range(8)]
            feed = [feed_ref[h0 + h] for h in range(8)]
            tell = [out_ref[h0 + h] for h in range(8)]

            def block(b, state, m=m, h0=h0, decay=decay, feed=feed, tell=tell):
                base = pl.multiple_of((m * (rows // 8) + b) * 64, 64)
                for r in range(8):
                    keep = (1 - flags[m, b * 8 + r]).astype(F32)
                    row = row_of(normed_ref, base, r)
                    state = ema_step(state, row, keep, decay, feed)
                    told = [s * t for s, t in zip(state, tell)]
                    while len(told) > 1:
                        told = [told[i] + told[i + 1] for i in range(0, len(told), 2)]
                    at = pl.ds(base + r, 8, stride=8)
                    if h0 == 0:
                        acc_ref[at, :] = told[0] + omega * row
                    else:
                        acc_ref[at, :] = acc_ref[at, :] + told[0]
                return state

            lax.fori_loop(0, rows // 8, block, [start_ref[m, h0 + h] for h in range(8)])

    def finish(b, carry):
        at = pl.ds(pl.multiple_of(b * 16, 16), 16)
        v = jnp.concatenate([collect(acc_ref, 2 * b), collect(acc_ref, 2 * b + 1)], axis=0)
        blended_ref[at, :] = v
        low_ref[at, :] = (v / (1.0 + jnp.exp(-v))).astype(BF16)
        return carry

    lax.fori_loop(0, micros * rows // 16, finish, 0)


def shared_kernel(
    before, flags, gp0_ref, gp1_ref, probs_ref, query_ref, key_ref, shared_ref, pre_ref, gain_ref, gates_ref, weight_ref,
    mix0_ref, mix1_ref, blended_ref, decay_ref, tell_ref,
    rows_ref, left_ref, low_ref, sums_ref,
):
    b = pl.program_id(0)
    width = mix0_ref.shape[-1]
    probs = probs_ref[0]
    grad_probs = gp0_ref[0] + gp1_ref[0]
    scale = query_ref.shape[-1] ** (-0.5)
    grad_scores = probs * (grad_probs - jnp.sum(grad_probs * probs, axis=-1, keepdims=True)) * scale
    exact = partial(lax.dot_general, precision=HIGHEST, preferred_element_type=F32)
    grad_query = exact(grad_scores, key_ref[...].astype(F32), (((1,), (0,)), ((), ())))
    grad_key = exact(grad_scores, query_ref[...].astype(F32), (((0,), (0,)), ((), ())))
    shared = shared_ref[...]
    pre = pre_ref[...]
    grad_pre = (grad_query * gain_ref[0:1] + grad_key * gain_ref[1:2]) * slope(pre, sigmoid(pre))
    low = grad_pre.astype(BF16)
    low_ref[...] = low
    total = lambda v: jnp.sum(v, axis=0, keepdims=True)
    part = jnp.concatenate(
        [
            total(grad_query * shared), total(grad_key * shared), total(grad_query), total(low.astype(F32)),
            jnp.zeros((4, low.shape[-1]), F32),
        ]
    )
    add_to(sums_ref, part)
    mixed = (
        mix0_ref[...]
        + mix1_ref[...]
        + dot_nt(gates_ref[...], weight_ref[:, : 2 * width])
        + dot_nt(low, weight_ref[:, 2 * width :])
    )
    v = blended_ref[...]
    grad = mixed * slope(v, sigmoid(v))
    for i in range(BLOCK // 8):
        spread(rows_ref, b * (BLOCK // 8) + i, grad[8 * i : 8 * i + 8])

    @pl.when(b == pl.num_programs(0) - 1)
    def _():
        micros, rows = flags.shape
        heads = decay_ref.shape[0]
        for m in range(micros):
            for h0 in range(0, heads, 8):
                decay = [decay_ref[h0 + h] for h in range(8)]
                tell = [tell_ref[h0 + h] for h in range(8)]

                def block(i, left, m=m, decay=decay, tell=tell):
                    b = rows // 8 - 1 - i
                    base = pl.multiple_of((m * (rows // 8) + b) * 64, 64)
                    for r in reversed(range(8)):
                        keep = (1 - flags[m, b * 8 + r]).astype(F32)
                        row = row_of(rows_ref, base, r)
                        left = [((t * row + k) * keep) * q for k, q, t in zip(left, decay, tell)]
                    return left

                left = lax.fori_loop(0, rows // 8, block, [jnp.zeros((8, 128), F32)] * 8)
                for h in range(8):
                    left_ref[m, h0 + h] = left[h]


def run_shared(token, flags, gp0, gp1, probs, query, key, shared, pre, gain, gates, weight, mix0, mix1, blended, decay, tell):
    total, width = mix0.shape
    z = query.shape[1]
    rows = lambda n: pl.BlockSpec((BLOCK, n), lambda b: (b, 0))
    pair = pl.BlockSpec((1, BLOCK, BLOCK), lambda b: (b, 0, 0))
    whole = lambda a: pl.BlockSpec(a.shape, lambda b: (0,) * a.ndim)
    micros, heads = flags.shape[0], decay.shape[0]
    return pl.pallas_call(
        shared_kernel,
        grid=(total // BLOCK,),
        in_specs=[
            pl.BlockSpec(memory_space=pl.ANY), pl.BlockSpec(memory_space=pltpu.SMEM), pair, pair, pair, rows(z), rows(z), rows(z), rows(z), whole(gain),
            rows(2 * width), whole(weight), rows(width), rows(width), rows(width), whole(decay), whole(tell),
        ],
        out_specs=[
            pl.BlockSpec((total * 8, 128), lambda b: (0, 0)),
            pl.BlockSpec((micros, heads, 8, 128), lambda b: (0, 0, 0, 0)),
            rows(z),
            pl.BlockSpec((8, z), lambda b: (0, 0)),
        ],
        out_shape=[
            shape_of(total * 8, 128), shape_of(micros, heads, 8, 128), shape_of(total, z, dtype=BF16), shape_of(8, z),
        ],
        cost_estimate=cost(200),
    )(token, flags, gp0, gp1, probs, query, key, shared, pre, gain, gates, weight, mix0, mix1, blended, decay, tell)


def back_kernel(
    m, before, flags, normed_ref, rows_ref, start_ref, right_ref, decay_ref, feed_ref, tell_ref, omega_ref,
    add0_ref, add1_ref, source_ref, base_ref, gain_ref,
    grad_ref, eta_ref, one_ref, two_ref, omega_out, gain_out, token_ref, states, acc_ref,
):
    rows = flags.shape[1]
    heads = decay_ref.shape[0]
    group = 4
    omega = omega_ref[...]
    zero = jnp.zeros((8, 128), F32)
    token_ref[...] = zero
    for h0 in range(0, heads, group):
        decay = [decay_ref[h0 + h] for h in range(group)]
        feed = [feed_ref[h0 + h] for h in range(group)]
        tell = [tell_ref[h0 + h] for h in range(group)]

        def ahead(b, state, decay=decay, feed=feed):
            base = pl.multiple_of(b * 64, 64)
            for r in range(8):
                keep = (1 - flags[m, b * 8 + r]).astype(F32)
                for h in range(group):
                    states[b * 8 + r, h] = state[h]
                state = ema_step(state, row_of(normed_ref, base, r), keep, decay, feed)
            return state

        last = lax.fori_loop(0, rows // 8, ahead, [start_ref[0, h0 + h] for h in range(group)])

        def back(i, carry, h0=h0, decay=decay, feed=feed, tell=tell):
            left, after_state, eta, one, two, with_omega = carry
            b = rows // 8 - 1 - i
            base = pl.multiple_of(b * 64, 64)
            for r in reversed(range(8)):
                keep = (1 - flags[m, b * 8 + r]).astype(F32)
                g = row_of(rows_ref, base, r)
                x = row_of(normed_ref, base, r)
                earlier = [states[b * 8 + r, h] for h in range(group)]
                eta = [e + s * g for e, s in zip(eta, after_state)]
                now = [t * g + k for t, k in zip(tell, left)]
                one = [o + n * x for o, n in zip(one, now)]
                kept = [n * keep for n in now]
                two = [w + k * s for w, k, s in zip(two, kept, earlier)]
                left = [k * q for k, q in zip(kept, decay)]
                gn = [n * f for n, f in zip(now, feed)]
                while len(gn) > 1:
                    gn = [gn[i] + gn[i + 1] for i in range(0, len(gn), 2)]
                at = pl.ds(base + r, 8, stride=8)
                if h0 == 0:
                    acc_ref[at, :] = gn[0] + omega * g
                    with_omega = with_omega + g * x
                else:
                    acc_ref[at, :] = acc_ref[at, :] + gn[0]
                after_state = earlier
            return left, after_state, eta, one, two, with_omega

        right = [right_ref[0, h0 + h] for h in range(group)]
        nothing = [zero] * group
        _, _, eta, one, two, with_omega = lax.fori_loop(
            0, rows // 8, back, (right, last, nothing, nothing, nothing, zero)
        )
        if h0 == 0:
            omega_out[...] = with_omega
        for h in range(group):
            eta_ref[h0 + h] = eta[h]
            one_ref[h0 + h] = one[h]
            two_ref[h0 + h] = two[h]

    def finish(b, gained):
        at = pl.ds(pl.multiple_of(b * 16, 16), 16)
        x = source_ref[at, :].astype(F32)
        scale = lax.rsqrt(jnp.mean(x * x, axis=-1, keepdims=True) + EPSILON)
        scaled = x * scale
        grad = jnp.concatenate([collect(acc_ref, 2 * b), collect(acc_ref, 2 * b + 1)], axis=0)
        grad = grad + add0_ref[at, :] + add1_ref[at, :]
        own = grad * scaled
        gained = gained + own[:8] + own[8:]
        inner = grad * gain_ref[...]
        mean = jnp.mean(inner * scaled, axis=-1, keepdims=True)
        grad_ref[at, :] = base_ref[at, :] + scale * (inner - scaled * mean)
        return gained

    width = source_ref.shape[-1]
    gain_out[...] = lax.fori_loop(0, rows // 16, finish, jnp.zeros((8, width), F32))


def run_back(m, token, flags, laid, grads, start, right, decay, feed, tell, omega, add0, add1, source, base, gain):
    rows, heads = flags.shape[1], decay.shape[0]
    width = source.shape[1]
    whole = lambda a: pl.BlockSpec(a.shape, lambda i: (0,) * a.ndim)
    tall = pl.BlockSpec((rows * 8, 128), lambda i: (m, 0))
    carry = pl.BlockSpec((1, heads, 8, 128), lambda i: (m, 0, 0, 0))
    wide = pl.BlockSpec((rows, width), lambda i: (m, 0))
    sums = pl.BlockSpec((heads, 8, 128), lambda i: (0, 0, 0))
    return pl.pallas_call(
        partial(back_kernel, m),
        grid=(1,),
        in_specs=[
            pl.BlockSpec(memory_space=pl.ANY), pl.BlockSpec(memory_space=pltpu.SMEM), tall, tall, carry, carry,
            whole(decay), whole(feed), whole(tell), whole(omega), wide, wide, wide, wide, whole(gain),
        ],
        out_specs=[
            pl.BlockSpec((rows, width), lambda i: (0, 0)), sums, sums, sums,
            pl.BlockSpec((8, 128), lambda i: (0, 0)), pl.BlockSpec((8, width), lambda i: (0, 0)),
            pl.BlockSpec((8, 128), lambda i: (0, 0)),
        ],
        out_shape=[
            jax.ShapeDtypeStruct((rows, width), F32),
            *[jax.ShapeDtypeStruct((heads, 8, 128), F32)] * 3,
            jax.ShapeDtypeStruct((8, 128), F32),
            jax.ShapeDtypeStruct((8, width), F32),
            jax.ShapeDtypeStruct((8, 128), F32),
        ],
        scratch_shapes=[pltpu.VMEM((rows, 4, 8, 128), F32), pltpu.VMEM((rows * 8, 128), F32)],
        cost_estimate=cost(200),
    )(token, flags, laid, grads, start, right, decay, feed, tell, omega, add0, add1, source, base, gain)


def dot_tn(a, b):
    return lax.dot_general(a, b, (((0,), (0,)), ((), ())), preferred_element_type=F32)


def dot_nt(a, b):
    return lax.dot_general(a, b, (((1,), (1,)), ((), ())), preferred_element_type=F32)


def dot_nn(a, b):
    return lax.dot_general(a, b, (((1,), (0,)), ((), ())), preferred_element_type=F32)


def sigmoid(v):
    return 1.0 / (1.0 + jnp.exp(-v))


def slope(v, s):
    return s * (1.0 + v * (1.0 - s))


def add_to(ref, value, first_ref=None):
    first = pl.program_id(0) == 0

    @pl.when(first)
    def _():
        ref[...] = value if first_ref is None else first_ref[...] + value

    @pl.when(jnp.logical_not(first))
    def _():
        ref[...] = ref[...] + value


def put_sides(ref, lead, v):
    half = v.shape[-1] // 2
    v = v.astype(BF16)
    ref[0, lead] = v[:, :half]
    ref[1, lead] = v[:, half:]


def value_kernel(
    piece, normed_ref, mixed_ref, probs_ref, wv_ref, wr_ref, wb_ref, bv_ref, br_ref, sum_ref,
    value_ref, reset_ref, attended_ref, gated_ref, out_ref,
):
    value_pre = dot_nt(normed_ref[...], flat(wv_ref)) + bv_ref[...]
    value_ref[...] = value_pre
    value = (value_pre * sigmoid(value_pre)).astype(BF16)
    blocks = probs_ref.shape[0]
    attended = jnp.concatenate(
        [dot_nn(probs_ref[b], value[b * BLOCK : (b + 1) * BLOCK]) for b in range(blocks)], axis=0
    )
    attended_ref[...] = attended
    reset_pre = dot_nt(mixed_ref[...], flat(wr_ref)) + br_ref[...]
    reset_ref[...] = reset_pre
    gated = (reset_pre * sigmoid(reset_pre) * attended).astype(BF16)
    gated_ref[...] = gated
    add_to(out_ref, dot_nn(gated, flat(wb_ref)), sum_ref)


def value_back_kernel(
    piece, grad_ref, normed_ref, mixed_ref, probs_ref, wv_ref, wr_ref, wb_ref,
    value_ref, reset_ref, attended_ref, gated_ref,
    d_ref, sum_r_ref, sum_v_ref, mixed_out, normed_out, probs_out,
):
    grad = grad_ref[...]
    grad_gated = dot_nt(grad, flat(wb_ref))
    put_sides(d_ref, 0, dot_tn(gated_ref[...], grad))
    reset_pre = reset_ref[...]
    s = sigmoid(reset_pre)
    grad_attended = (grad_gated * (reset_pre * s)).astype(BF16)
    grad_reset = (grad_gated * attended_ref[...] * slope(reset_pre, s)).astype(BF16)
    sum_r_ref[...] = jnp.sum(grad_reset.astype(F32), axis=0, keepdims=True)
    mixed = mixed_ref[...]
    put_sides(d_ref, 1, dot_tn(grad_reset, mixed))
    add_to(mixed_out, dot_nn(grad_reset, flat(wr_ref)))
    value_pre = value_ref[...]
    s = sigmoid(value_pre)
    value = (value_pre * s).astype(BF16)
    blocks = probs_ref.shape[0]
    grad_value, grad_probs = [], []
    for b in range(blocks):
        rows = slice(b * BLOCK, (b + 1) * BLOCK)
        grad_probs.append(dot_nt(grad_attended[rows], value[rows])[None])
        grad_value.append(dot_tn(probs_ref[b], grad_attended[rows]))
    add_to(probs_out, jnp.concatenate(grad_probs, axis=0))
    grad_value = (jnp.concatenate(grad_value, axis=0) * slope(value_pre, s)).astype(BF16)
    sum_v_ref[...] = jnp.sum(grad_value.astype(F32), axis=0, keepdims=True)
    put_sides(d_ref, 2, dot_tn(grad_value, normed_ref[...]))
    add_to(normed_out, dot_nn(grad_value, flat(wv_ref)))


def inner_kernel(piece, ffn_ref, grad_ref, wi_ref, bi_ref, pre_ref, activ_ref, do_ref):
    wi = flat(wi_ref)
    pre = dot_nt(ffn_ref[...], wi) + bi_ref[...]
    pre_ref[...] = pre
    activ = (pre * sigmoid(pre)).astype(BF16)
    activ_ref[...] = activ
    put_sides(do_ref, 0, dot_tn(activ, grad_ref[...]))


def outer_kernel(
    piece, ffn_ref, grad_ref, wi_ref, wo_ref, pre_ref, activ_ref, sum_o_ref, sum_f_ref,
    di_ref, sum_i_ref, out_ref, ffn_out,
):
    wi = flat(wi_ref)
    wo = flat(wo_ref)
    add_to(out_ref, dot_nn(activ_ref[...], wo), sum_o_ref)
    pre = pre_ref[...]
    grad = (dot_nt(grad_ref[...], wo) * slope(pre, sigmoid(pre))).astype(BF16)
    sum_i_ref[...] = jnp.sum(grad.astype(F32), axis=0, keepdims=True)
    put_sides(di_ref, 0, dot_tn(grad, ffn_ref[...]))
    add_to(ffn_out, dot_nn(grad, wi), sum_f_ref)


UNITS = 512


def cost(micros):
    return pl.CostEstimate(flops=int(micros * SCALE * 1.15e9), bytes_accessed=int(micros * SCALE * 3.3e6), transcendentals=0)


SCALE = 1.0


def shape_of(*dims, dtype=F32):
    return jax.ShapeDtypeStruct(dims, dtype)


def middle(gate_ref, branch_ref, source_ref):
    width = source_ref.shape[-1]
    update = sigmoid(gate_ref[:, :width])
    pre = gate_ref[:, width : 2 * width] + branch_ref[...]
    s = sigmoid(pre)
    return source_ref[...].astype(F32), update, pre, s


def middle_kernel(gate_ref, branch_ref, source_ref, gain_ref, mixed_ref, ffn_ref):
    source, update, pre, s = middle(gate_ref, branch_ref, source_ref)
    mixed = update * (pre * s) + (1.0 - update) * source
    mixed_ref[...] = mixed
    scale = lax.rsqrt(jnp.mean(mixed * mixed, axis=-1, keepdims=True) + EPSILON)
    ffn_ref[...] = (mixed * scale * gain_ref[...]).astype(BF16)


def column_sums(v):
    return jnp.sum(v.reshape(-1, 8, v.shape[-1]), axis=0)


def middle_back_kernel(
    before, gate_ref, branch_ref, source_ref, gain_ref, bias_ref, mixed_ref, feed_ref, grad_ref, ffn_ref,
    out_ref, base_ref, gates_ref, sum_gain_ref, sum_out_ref, sum_gates_ref,
):
    width = source_ref.shape[-1]
    source, update, pre, s = middle(gate_ref, branch_ref, source_ref)
    mixed = mixed_ref[...]
    out_ref[...] = (mixed + feed_ref[...] + bias_ref[...]).astype(BF16)
    scale = lax.rsqrt(jnp.mean(mixed * mixed, axis=-1, keepdims=True) + EPSILON)
    scaled = mixed * scale
    grad_out = grad_ref[...].astype(F32)
    grad_ffn = ffn_ref[...]
    add_to(sum_out_ref, column_sums(grad_out))
    add_to(sum_gain_ref, column_sums(grad_ffn * scaled))
    gained = grad_ffn * gain_ref[...]
    grad = grad_out + scale * (gained - scaled * jnp.mean(gained * scaled, axis=-1, keepdims=True))
    base_ref[...] = grad * (1.0 - update)
    grad_update = (grad * (pre * s - source) * update * (1.0 - update)).astype(BF16)
    grad_hidden = (grad * update * slope(pre, s)).astype(BF16)
    gates_ref[:, :width] = grad_update
    gates_ref[:, width:] = grad_hidden
    add_to(
        sum_gates_ref,
        jnp.concatenate([column_sums(grad_update.astype(F32)), column_sums(grad_hidden.astype(F32))], axis=1),
    )


def run_middle(gate, branch, source, gain):
    total, width = source.shape
    rows = lambda n: pl.BlockSpec((BLOCK, n), lambda i: (i, 0))
    line = pl.BlockSpec((1, width), lambda i: (0, 0))
    return pl.pallas_call(
        middle_kernel,
        grid=(total // BLOCK,),
        in_specs=[rows(gate.shape[1]), rows(width), rows(width), line],
        out_specs=[rows(width), rows(width)],
        out_shape=[shape_of(total, width), shape_of(total, width, dtype=BF16)],
        cost_estimate=cost(5),
    )(gate, branch, source, gain[None])


def run_middle_back(token, gate, branch, source, gain, bias, mixed, feed, grad, ffn):
    total, width = source.shape
    rows = lambda n: pl.BlockSpec((BLOCK, n), lambda i: (i, 0))
    line = pl.BlockSpec((1, width), lambda i: (0, 0))
    few = lambda n: pl.BlockSpec((8, n), lambda i: (0, 0))
    wide = rows(width)
    return pl.pallas_call(
        middle_back_kernel,
        grid=(total // BLOCK,),
        in_specs=[
            pl.BlockSpec(memory_space=pl.ANY), rows(gate.shape[1]), wide, wide, line, line, wide, wide, wide, wide
        ],
        out_specs=[wide, wide, rows(2 * width), few(width), few(width), few(2 * width)],
        out_shape=[
            shape_of(total, width, dtype=BF16), shape_of(total, width), shape_of(total, 2 * width, dtype=BF16),
            shape_of(8, width), shape_of(8, width), shape_of(8, 2 * width),
        ],
        cost_estimate=cost(1),
    )(token, gate, branch, source, gain[None], bias[None], mixed, feed, grad, ffn)


def gates_kernel(piece, before, mixed_ref, gates_ref, d_ref):
    grad = dot_tn(mixed_ref[...], gates_ref[...]).astype(BF16)
    half = grad.shape[-1] // 2
    d_ref[0] = grad[:, :half].reshape(d_ref.shape[1:])
    d_ref[1] = grad[:, half:].reshape(d_ref.shape[1:])


def run_gates(which, token, mixed, gates):
    total, width = mixed.shape
    n = which.shape[0]
    block = width // (2 * n)
    return pl.pallas_call(
        gates_kernel,
        grid_spec=pltpu.PrefetchScalarGridSpec(
            num_scalar_prefetch=1,
            grid=(n,),
            in_specs=[
                pl.BlockSpec(memory_space=pl.ANY),
                pl.BlockSpec((total, block), lambda i, p: (0, p[i])),
                pl.BlockSpec(gates.shape, lambda i, p: (0, 0)),
            ],
            out_specs=pl.BlockSpec((2, 1, block, width), lambda i, p: (0, 0, i, 0)),
        ),
        out_shape=shape_of(2, 1, n * block, width, dtype=BF16),
        cost_estimate=cost(1),
    )(which, token, mixed, gates)


class Pieces:
    def __init__(self, gathered, which, tensor, part_f, part_v):
        self.gathered, self.which, self.tensor = gathered, which, tensor
        self.part_f, self.part_v = part_f, part_v
        self.width = gathered.shape[-1]

    def units(self, part):
        return self.which.shape[0] * self.tensor * part

    def block(self, part):
        return min(UNITS, self.tensor * part)

    def spec(self, part, row):
        step = self.block(part) // part
        per = self.tensor // step
        return pl.BlockSpec(
            (step, part, self.width), lambda i, p: (p[i // per] * per + i % per, row // part, 0)
        )

    @property
    def w_in(self):
        return self.spec(self.part_f, 0)

    @property
    def w_out(self):
        return self.spec(self.part_f, self.part_f)

    def v(self, k):
        return self.spec(self.part_v, 2 * self.part_f + k * self.part_v)


def flat(ref):
    return ref[...].reshape(-1, ref.shape[-1])


def blocked(kernel, micros, pieces, steps, token, in_specs, out_specs, out_shape, *arrays):
    def body(piece, before, *refs):
        kernel(piece, *refs)

    return pl.pallas_call(
        body,
        grid_spec=pltpu.PrefetchScalarGridSpec(
            num_scalar_prefetch=1,
            grid=(steps,),
            in_specs=[pl.BlockSpec(memory_space=pl.ANY), *in_specs],
            out_specs=out_specs,
        ),
        out_shape=out_shape,
        cost_estimate=cost(micros),
    )(pieces.which, token, *arrays)


def block_specs(total, width, block, lead):
    full = pl.BlockSpec((total, width), lambda i, p: (0, 0))
    cols = pl.BlockSpec((total, block), lambda i, p: (0, i))
    line = pl.BlockSpec((1, block), lambda i, p: (0, i))
    grads = pl.BlockSpec((2, lead, block, width // 2), lambda i, p: (0, 0, i, 0))
    return full, cols, line, grads


def run_value(pieces, token, normed, mixed, probs, bv, br, before):
    total, width = normed.shape
    units, block = pieces.units(pieces.part_v), pieces.block(pieces.part_v)
    full, cols, line, grads = block_specs(total, width, block, 3)
    pairs = pl.BlockSpec(probs.shape, lambda i, p: (0, 0, 0))
    g = pieces.gathered
    return blocked(
        value_kernel, 200, pieces, units // block, token,
        [full, full, pairs, pieces.v(0), pieces.v(1), pieces.v(2), line, line, full],
        [cols, cols, cols, cols, full],
        [shape_of(total, units)] * 3 + [shape_of(total, units, dtype=BF16), shape_of(total, width)],
        normed, mixed, probs, g, g, g, bv, br, before,
    )


def run_value_back(pieces, micros, token, grad, normed, mixed, probs, kept):
    total, width = normed.shape
    units, block = pieces.units(pieces.part_v), pieces.block(pieces.part_v)
    full, cols, line, grads = block_specs(total, width, block, 3)
    pairs = pl.BlockSpec(probs.shape, lambda i, p: (0, 0, 0))
    g = pieces.gathered
    return blocked(
        value_back_kernel, micros, pieces, units // block, token,
        [
            pl.BlockSpec((total, width), lambda i, p: (0, 1)), full, full, pairs,
            pieces.v(0), pieces.v(1), pieces.v(2), cols, cols, cols, cols,
        ],
        [grads, line, line, full, full, pairs],
        [shape_of(2, 3, units, width // 2, dtype=BF16)]
        + [shape_of(1, units)] * 2
        + [shape_of(total, width)] * 2
        + [shape_of(*probs.shape)],
        grad, normed, mixed, probs, g, g, g, *kept,
    )


def run_inner(pieces, token, ffn, grad, bias):
    total, width = ffn.shape
    units, block = pieces.units(pieces.part_f), pieces.block(pieces.part_f)
    full, cols, line, grads = block_specs(total, width, block, 1)
    return blocked(
        inner_kernel, 200, pieces, units // block, token,
        [full, full, pieces.w_in, line],
        [cols, cols, grads],
        [shape_of(total, units), shape_of(total, units, dtype=BF16), shape_of(2, 1, units, width // 2, dtype=BF16)],
        ffn, grad, pieces.gathered, bias,
    )


def run_outer(pieces, token, ffn, grad, pre, activ, before_out, before_ffn):
    total, width = ffn.shape
    units, block = pieces.units(pieces.part_f), pieces.block(pieces.part_f)
    full, cols, line, grads = block_specs(total, width, block, 1)
    return blocked(
        outer_kernel, 200, pieces, units // block, token,
        [full, full, pieces.w_in, pieces.w_out, cols, cols, full, full],
        [grads, line, full, full],
        [shape_of(2, 1, units, width // 2, dtype=BF16), shape_of(1, units), shape_of(total, width), shape_of(total, width)],
        ffn, grad, pieces.gathered, pieces.gathered, pre, activ, before_out, before_ffn,
    )


def call(kernel, outs, scratch, smem, *arrays):
    return pl.pallas_call(
        kernel,
        out_shape=outs,
        in_specs=[pl.BlockSpec(memory_space=pltpu.SMEM)] * smem
        + [pl.BlockSpec(memory_space=pltpu.VMEM)] * (len(arrays) - smem),
        out_specs=jax.tree.map(lambda _: pl.BlockSpec(memory_space=pltpu.VMEM), outs),
        scratch_shapes=scratch,
        cost_estimate=cost(12),
    )(*arrays)


def scan_carry(grid, local, clear, whole, reverse):
    micros, heads = local.shape[:2]
    clear = jnp.broadcast_to(clear[:, None, None, None], (micros, 1, 8, 128))
    entering = jnp.zeros_like(local)
    reach = jnp.ones_like(local)
    total = local
    for mask in grid.tensor:
        got = grid.swap(jnp.concatenate([total, clear], axis=1), mask)
        got_total, got_clear = got[:, :heads], got[:, heads:]
        later = grid.bit(mask) == (0 if reverse else 1)
        entering = jnp.where(later, entering + reach * got_total, entering)
        reach = jnp.where(later, reach * got_clear * whole, reach)
        total = jnp.where(
            later, total + clear * whole * got_total, got_total + got_clear * whole * total
        )
        clear = clear * got_clear
        whole = whole * whole
    return entering


def after(values, *others):
    return lax.optimization_barrier((values, others))[0]


class Term:
    def __init__(self, array, labels, fixed):
        self.array, self.labels, self.fixed = array, labels, fixed


class Reduce:
    def __init__(self, grid, high, dims, still=()):
        self.grid, self.dims, self.still = grid, list(dims), still
        self.labels = ["side", "lead", *self.dims, "u", "h"]
        xs, (lo, *hi) = grid.xs[::-1], grid.tensor
        self.orders = [[*xs, lo], [lo, *xs]], hi[::-1]
        self.step = -1
        self.high = self.view(high)
        self.raw = [grid.swap(self.high, grid.core)]

    def view(self, v):
        n = len(self.dims)
        return v.reshape(*v.shape[:2], *[2] * n, v.shape[2] >> n, v.shape[3])

    @property
    def steps(self):
        return len(self.orders[0][0]) + len(self.orders[1])

    def add_low(self, low):
        self.low = self.view(low)

    def take(self):
        if self.step < 0:
            self.sides = [[Term(a, self.labels, {"side": s}) for a in (self.low, self.raw[0])] for s in (0, 1)]
            self.left = [list(self.dims), list(self.dims)]
        else:
            for s in (0, 1):
                for t in self.sides[s]:
                    if self.masks[s] in t.labels:
                        t.fixed[self.masks[s]] = 0
                self.left[s] = [d for d in self.left[s] if d != self.masks[s]]
                if len(self.raw) == 2:
                    self.sides[s].append(Term(self.raw[s], ["lead", *self.left[s], "u", "h"], {}))
                else:
                    self.sides[s].append(Term(self.raw[0], ["lead", *self.left[s], "u", "hh"], {"hh": s}))
        self.step += 1

    def wanted(self):
        (first, second), hi = self.orders
        k = self.step
        if k == self.steps:
            return [(self.sides[s], {}, self.left[s]) for s in (0, 1)], True
        self.masks = [first[k], second[k]] if k < len(first) else [hi[k - len(first)]] * 2
        return [
            (self.sides[s], {self.masks[s]: 1}, [d for d in self.left[s] if d != self.masks[s]]) for s in (0, 1)
        ], k >= len(first)

    def start(self, sends):
        if len(sends) == 2:
            self.raw = [self.grid.swap(v, m) for v, m in zip(sends, self.masks)]
        else:
            self.raw = [self.grid.swap(sends[0], self.masks[0])]


def place_of(grid, still, fixed, name, sel):
    if name in still:
        masks = [*grid.tensor, *grid.xs]
        return sel[2 * masks.index(name) + fixed[name]]
    return fixed[name]


def picked(grid, still, term, extra, sel):
    v = term.array
    fixed = {**term.fixed, **extra}
    for axis in reversed(range(len(term.labels))):
        name = term.labels[axis]
        if name == "hh":
            half = v.shape[-1] // 2
            v = v[..., fixed[name] * half : (fixed[name] + 1) * half]
        elif name in fixed:
            v = lax.dynamic_index_in_dim(v, place_of(grid, still, fixed, name, sel), axis, False)
    return v.astype(F32)


def point(grid, gates, *sums):
    for r in sums:
        r.take()
    outs, tasks = [], []
    for r in sums:
        sides, joined = r.wanted()
        for terms, fixed, left in sides:
            tasks.append((r, terms, fixed, left))
        shapes = []
        for terms, fixed, left in sides:
            low = r.low.shape
            shapes.append((low[1], *[2] * len(left), *low[-2:]))
        if joined:
            outs.append((*shapes[0][:-1], 2 * shapes[0][-1]))
        else:
            outs.extend(shapes)
    sel = grid.sel
    fits = all(len(r.dims) <= 4 and r.low.shape[-2] % 32 == 0 for r in sums)
    if fits:
        *values, token = run_point(grid, gates, tasks, outs, sel)
    else:
        values = []
        sides = [
            sum(picked(grid, r.still, t, {k: v for k, v in fixed.items() if k in t.labels}, sel) for t in terms).astype(BF16)
            for r, terms, fixed, left in tasks
        ]
        for shape in outs:
            v = sides.pop(0)
            values.append(v if v.shape == shape else jnp.concatenate([v, sides.pop(0)], axis=-1))
        token = after(jnp.zeros((8, 128), F32), [g[(0,) * g.ndim] for g in gates])
    done = []
    for r in sums:
        if r.step == r.steps:
            done.append(values.pop(0))
        else:
            n = 2 if r.step < len(r.orders[0][0]) else 1
            r.start(values[:n])
            values = values[n:]
    return (token, *done) if done else token


def run_point(grid, gates, tasks, outs, sel):
    parts = 2
    arrays, specs, layout = [], [], []
    for r, terms, extra, left in tasks:
        mine = []
        for t in terms:
            fixed = {**t.fixed, **{k: v for k, v in extra.items() if k in t.labels}}
            block = []
            for name, size in zip(t.labels, t.array.shape):
                if name == "hh":
                    block.append(size // 2)
                elif name == "u":
                    block.append(size // parts)
                else:
                    block.append(None if name in fixed else size)

            def index(i, p, t=t, fixed=fixed, r=r):
                return tuple(
                    i if name == "u" else place_of(grid, r.still, fixed, name, p) if name in fixed else 0
                    for name in t.labels
                )

            mine.append(len(arrays))
            arrays.append(t.array)
            specs.append(pl.BlockSpec(tuple(block), index))
        layout.append(mine)
    out_specs = []
    for shape in outs:
        block = (*shape[:-2], shape[-2] // parts, shape[-1])
        out_specs.append(pl.BlockSpec(block, lambda i, p, n=len(shape): (*[0] * (n - 2), i, 0)))
    out_specs.append(pl.BlockSpec((8, 128), lambda i, p: (0, 0)))

    def body(p, *refs):
        refs = refs[len(gates) :]
        ins, results = refs[: len(arrays)], refs[len(arrays) :]
        queue = list(layout)
        for ref in results[:-1]:
            first = 0
            while first < ref.shape[-1]:
                mine = queue.pop(0)
                total = ins[mine[0]][...].astype(F32)
                for k in mine[1:]:
                    total = total + ins[k][...].astype(F32)
                ref[..., first : first + total.shape[-1]] = total.astype(BF16)
                first += total.shape[-1]
        results[-1][...] = jnp.zeros((8, 128), F32)

    return pl.pallas_call(
        body,
        grid_spec=pltpu.PrefetchScalarGridSpec(
            num_scalar_prefetch=1,
            grid=(parts,),
            in_specs=[pl.BlockSpec(memory_space=pl.ANY)] * len(gates) + specs,
            out_specs=out_specs,
        ),
        out_shape=[shape_of(*shape, dtype=BF16) for shape in outs] + [shape_of(8, 128)],
        cost_estimate=cost(1),
    )(sel, *gates, *arrays)


def ends(result):
    return result if isinstance(result, tuple) else (result,)


def finish(grid, gates, r, value=None):
    while value is None:
        out = point(grid, gates, r)
        value = out[1] if isinstance(out, tuple) else None
    return value


def share_units(grid, part):
    held = part[None]
    masks = [*grid.xs, grid.core]
    for mask in masks:
        held = jnp.concatenate([held, grid.swap(held, mask)], axis=0)
    n = held.shape[0]
    held = held.astype(F32)
    for k, mask in enumerate(masks):
        held = held.reshape(n >> (k + 1), 2, -1, *part.shape)
        held = jnp.where(grid.bit(mask) == 1, held[:, ::-1], held)
    held = held.reshape(n, *part.shape).transpose(1, 0, 2, 3)
    return held.reshape(part.shape[0], -1, part.shape[-1])


def place_kernel(turned, bits, own_ref, x_ref, c_ref, *outs):
    swap_c, swap_x = bits[0] == 1, bits[1] == 1
    for k, turn in enumerate(turned):
        rows = []
        for own, other in ((own_ref[k], x_ref[k]), (c_ref[0, k], c_ref[1, k])):
            own, other = own.astype(F32), other.astype(F32)
            rows.append(jnp.concatenate([jnp.where(swap_x, other, own), jnp.where(swap_x, own, other)], axis=0))
        v = jnp.concatenate(
            [jnp.where(swap_c, rows[1], rows[0]), jnp.where(swap_c, rows[0], rows[1])], axis=0
        )
        outs[k][...] = v.T if turn else v


def share_and_place(grid, parts, turned, zero):
    results = []
    for part, turns in zip(parts, turned):
        if zero is not None:
            part = part + zero
        lead, units, width = part.shape
        if len(grid.xs) > 1 or units % 16:
            rows = share_units(grid, part)
            results.append([r.T if t else r for r, t in zip(rows, turns)])
            continue
        from_x = grid.swap(part, grid.xs[0])
        from_c = grid.swap(jnp.stack([part, from_x]), grid.core)
        results.append(
            pl.pallas_call(
                partial(place_kernel, turns),
                in_specs=[pl.BlockSpec(memory_space=pltpu.SMEM)] + [pl.BlockSpec(memory_space=pltpu.VMEM)] * 3,
                out_specs=[pl.BlockSpec(memory_space=pltpu.VMEM)] * lead,
                out_shape=[shape_of(*((width, 4 * units) if t else (4 * units, width))) for t in turns],
                cost_estimate=cost(5),
            )(jnp.stack([grid.bit(grid.core), grid.bit(grid.xs[0])]).astype(jnp.int32), part, from_x, from_c)
        )
    return results


def join_kernel(left_ref, right_ref, out_ref):
    n = left_ref.shape[1]
    out_ref[:, :n] = left_ref[...].astype(F32)
    out_ref[:, n:] = right_ref[...].astype(F32)


def join(left, right):
    rows, n = left.shape
    block = 256
    return pl.pallas_call(
        join_kernel,
        grid=(rows // block,),
        in_specs=[pl.BlockSpec((block, n), lambda i: (i, 0)), pl.BlockSpec((block, right.shape[1]), lambda i: (i, 0))],
        out_specs=pl.BlockSpec((block, n + right.shape[1]), lambda i: (i, 0)),
        out_shape=shape_of(rows, n + right.shape[1]),
        cost_estimate=cost(5),
    )(left, right)


def sum_flat(grid, v, part):
    held = v.reshape(-1, 128)
    n = held.shape[0]
    parts = part.astype(BF16)
    masks = [grid.core, *grid.xs, *grid.tensor]
    for mask in masks:
        low = held.astype(BF16)
        got = grid.swap(jnp.concatenate([low, parts]), mask)
        held = low.astype(F32) + got[:n].astype(F32)
        parts = jnp.concatenate([parts, got[n:]])
    parts = parts.reshape(*[2] * len(masks), *part.shape)
    order = masks[::-1]
    for axis, mask in enumerate(order):
        parts = jnp.where(grid.bit(mask) == 1, jnp.flip(parts, axis), parts)
    want = [*grid.xs[::-1], grid.core, *grid.tensor[::-1]]
    parts = parts.transpose(*[order.index(m) for m in want], len(order), len(order) + 1)
    return held.reshape(-1), parts.reshape(-1, part.shape[-1])


def padded(v, size):
    return jnp.concatenate([v, jnp.zeros(-v.size % size, F32)])


def local(
    inputs, resets, cotangent, norm_gain, ema_alpha, ema_damp, ema_beta, ema_eta, ema_omega,
    w_gates, b_gates, qk_gain, q_bias, w_value, b_value, w_reset, b_reset, w_branch, ffn_gain,
    w_in, b_in, w_out, b_out,
):
    grid = Grid()
    micros, rows, width = inputs.shape
    total = micros * rows
    heads = ema_alpha.shape[1]
    rank = lax.axis_index("tensor")
    units_v, units_f = w_value.shape[1], w_in.shape[1]
    n_x = 1 << len(grid.xs)
    split_x = n_x == 2
    core, x_at = grid.bit(grid.core), lax.axis_index("dp") // 2

    half_v, half_f = units_v // 2, units_f // 2

    def chunks(w, half, axis, whole):
        size = half // n_x
        picks = range(n_x) if whole else range(1)
        return jnp.concatenate(
            [lax.dynamic_slice_in_dim(w, core * half + (x_at ^ r) * size, size, axis) for r in picks],
            axis=axis,
        )

    n_tensor = lax.axis_size("tensor")
    part_f, part_v = half_f // n_x, half_v // n_x
    own = lambda w, half, axis: chunks(w, half, axis, False)
    bias = jnp.concatenate([own(b_value, half_v, 0), own(b_reset, half_v, 0), own(b_in, half_f, 0)])
    bias = jnp.zeros((8, width), BF16).at[0, : bias.size].set(bias)
    seed = jnp.concatenate(
        [
            own(w_in, half_f, 1).T, own(w_out, half_f, 0), own(w_value, half_v, 1).T,
            own(w_reset, half_v, 1).T, own(w_branch, half_v, 0), bias,
        ]
    )
    gathered = lax.all_gather(seed, AXES, axis=0)
    which = [
        jnp.stack([(x_at ^ r) * 2 + c for r in range(n_x)]).astype(jnp.int32) for c in (core, 1 - core)
    ]
    pieces = [Pieces(gathered, w, n_tensor, part_f, part_v) for w in which]
    table = gathered[:, 2 * part_f + 3 * part_v].astype(F32).reshape(2 * n_x, n_tensor, width)
    tables = [jnp.stack([lax.dynamic_index_in_dim(table, w[r], 0, False) for r in range(n_x)]) for w in which]
    bias_v = [t[..., :part_v].reshape(1, -1) for t in tables]
    bias_r = [t[..., part_v : 2 * part_v].reshape(1, -1) for t in tables]
    bias_i = [t[..., 2 * part_v : 2 * part_v + part_f].reshape(1, -1) for t in tables]
    dims = [*grid.xs[::-1], *grid.tensor[::-1]]
    still = grid.tensor

    def in_place(low, high):
        d = [grid.core, *dims]
        v = jnp.stack([low, high]).reshape(*[2] * len(d), -1)
        for axis, mask in enumerate(d):
            if mask not in still:
                v = jnp.where(grid.bit(mask) == 1, jnp.flip(v, axis), v)
        want = [*grid.tensor[::-1], grid.core, *grid.xs[::-1]]
        return v.transpose(*[d.index(m) for m in want], len(d)).reshape(-1)

    offsets = rank * rows + jnp.arange(rows)
    flags = jnp.where(offsets[None] == 0, 1, resets).astype(jnp.int32)
    sel = jnp.stack([grid.bit(m) ^ i for m in [*grid.tensor, *grid.xs] for i in (0, 1)]).astype(jnp.int32)
    places = [jnp.stack([2 * x + c for x in range(n_x)]).astype(jnp.int32) for c in (core, 1 - core)]
    flags, grid.sel, places, which = lax.optimization_barrier((flags, sel, places, which))
    for p, w in zip(pieces, which):
        p.which = w
    tile = lambda a: a.T.reshape(heads, 8, 128)
    decay = tile(1.0 - ema_alpha * ema_damp)
    feed = tile(ema_alpha * ema_beta)
    tell = tile(ema_eta)
    whole = jnp.exp(rows * jnp.log(decay))[None]
    clear = (jnp.sum(flags, axis=1) == 0).astype(F32)
    source_low = inputs.reshape(total, width)
    laid = jax.ShapeDtypeStruct((total * 8, 128), F32)
    wide = jax.ShapeDtypeStruct((total, width), F32)
    wide_low = jax.ShapeDtypeStruct((total, width), BF16)
    states = jax.ShapeDtypeStruct((micros, heads, 8, 128), F32)
    sums = jax.ShapeDtypeStruct((heads, 8, 128), F32)
    normed_laid, normed_low, final = call(
        norm_kernel, (laid, wide_low, states), [], 1,
        flags, source_low, norm_gain[None], decay, feed,
    )
    start = scan_carry(grid, final, clear, whole, False)
    blended, mixed_low = call(
        blend_kernel, (wide, wide_low), [pltpu.VMEM((total * 8, 128), F32)], 1,
        flags, normed_laid, start, decay, feed, tell, ema_omega.reshape(8, 128),
    )

    source = source_low.astype(F32)
    gate_pre = dot_plain(mixed_low, w_gates) + b_gates
    update = jax.nn.sigmoid(gate_pre[:, :width])
    direct = gate_pre[:, width : 2 * width]
    shared_pre = gate_pre[:, 2 * width :]
    shared = rounded(jax.nn.silu(shared_pre))
    query = (shared * qk_gain[0] + q_bias).astype(BF16)
    key = (shared * qk_gain[1]).astype(BF16)
    blocks = total // BLOCK
    doc = jnp.cumsum(flags.reshape(blocks, BLOCK), axis=1)
    order = jnp.arange(BLOCK)
    allowed = (doc[:, :, None] == doc[:, None, :]) & (order[:, None] >= order[None, :])[None]
    score_scale = query.shape[-1] ** (-0.5)
    query_b, key_b = query.reshape(blocks, BLOCK, -1), key.reshape(blocks, BLOCK, -1)
    scores = jnp.einsum("cik,cjk->cij", query_b, key_b, preferred_element_type=F32) * score_scale
    scores = jnp.where(allowed, scores, -1000000000.0)
    probs = jax.nn.softmax(scores, axis=-1)
    probs_low = probs.astype(BF16)

    sums_b = jnp.zeros((total, width), F32)
    kept = [None, None]
    for k in (0, 1):
        *kept[k], sums_b = run_value(pieces[k], bias_v[k], normed_low, mixed_low, probs_low, bias_v[k], bias_r[k], sums_b)
    branch = sums_b
    mixed_out, ffn_low = run_middle(gate_pre, branch, source_low, ffn_gain)
    grad_low = cotangent.reshape(total, width)

    inner = [None, None]
    inner[1] = run_inner(pieces[1], bias_i[1], ffn_low, grad_low, bias_i[1])
    r_out = Reduce(grid, inner[1][2], dims, still)
    inner[0] = run_inner(pieces[0], inner[1][1], ffn_low, grad_low, bias_i[0])
    r_out.add_low(inner[0][2])
    token = point(grid, [], r_out)
    feed_out = jnp.zeros((total, width), F32)
    sum_in = [None, None]
    d_high, sum_in[1], feed_out, grad_ffn = run_outer(
        pieces[1], token, ffn_low, grad_low, inner[1][0], inner[1][1], feed_out, feed_out
    )
    r_in = Reduce(grid, d_high, dims, still)
    token = point(grid, [sum_in[1]], r_out)
    d_low, sum_in[0], feed_out, grad_ffn = run_outer(
        pieces[0], token, ffn_low, grad_low, inner[0][0], inner[0][1], feed_out, grad_ffn
    )
    r_in.add_low(d_low)
    token = point(grid, [], r_out, r_in)
    output, grad_source, grad_gates_low, sum_ffn_gain, sum_out, sum_gates = run_middle_back(
        token, gate_pre, branch, source_low, ffn_gain, b_out, mixed_out, feed_out, grad_low, grad_ffn
    )
    bits = [*grid.xs[::-1], grid.core, *grid.tensor[::-1]]
    dims_g = [m for m in bits if m != grid.core]
    if width // (2 * n_x) % 128 == 0:
        d_gates = [None, None]
        d_gates[1] = run_gates(places[1], sum_gates, mixed_low, grad_gates_low)
        r_gates = Reduce(grid, d_gates[1], dims_g, dims_g)
        d_gates[0] = run_gates(places[0], d_gates[1], mixed_low, grad_gates_low)
        r_gates.add_low(d_gates[0])
        token = d_gates[0]
    else:
        c_axis = bits.index(grid.core)
        d_gates = [
            dot_over_rows(mixed_low, side).astype(BF16).reshape(*[2] * len(bits), -1, width)
            for side in (grad_gates_low[:, :width], grad_gates_low[:, width:])
        ]
        half_of = lambda i: jnp.stack(
            [lax.dynamic_index_in_dim(d, i, c_axis, False).reshape(1, width // 2, width) for d in d_gates]
        )
        r_gates = Reduce(grid, half_of(1 - core), dims_g, dims_g)
        r_gates.add_low(half_of(core))
        token = sum_gates

    def run_vb(k, token):
        return run_value_back(pieces[k], 200 if k == 0 else 1, token, grad_gates_low, normed_low, mixed_low, probs_low, kept[k])

    back = [None, None]
    back[1] = run_vb(1, token)
    r_v = Reduce(grid, back[1][0], dims, still)
    token = point(grid, [back[1][1]], r_out, r_in, r_gates)
    back[0] = run_vb(0, token)
    r_v.add_low(back[0][0])
    token = point(grid, [back[0][1]], r_v, r_gates, r_in)
    grad_laid, left, grad_shared_low, sums_shared = run_shared(
        token, flags, back[0][5], back[1][5], probs, query, key, shared, shared_pre, qk_gain, grad_gates_low, w_gates,
        back[0][3], back[1][3], blended, decay, tell,
    )
    token = point(grid, [left], r_gates, r_in)
    left = left + token[0, 0]
    d_shared = dot_over_rows(mixed_low, grad_shared_low + token[0, 0].astype(BF16))
    d_shared = d_shared.reshape(*[2] * len(bits), -1, d_shared.shape[-1])

    def fold(v, mask):
        axis, here = bits.index(mask), grid.bit(mask)
        got = grid.swap(lax.dynamic_slice_in_dim(v, 1 - here, 1, axis).astype(BF16), mask)
        return lax.dynamic_slice_in_dim(v, here, 1, axis) + got.astype(F32)

    right = scan_carry(grid, left, clear, whole, True)
    t_first, *t_rest = grid.tensor
    for mask in [grid.core, *grid.xs, t_first]:
        d_shared = fold(d_shared, mask)
    token = point(grid, [right], r_v, r_gates)
    d_shared = fold(d_shared + token[0, 0], t_rest[0])
    column = shape_of(8, 128)
    results = []
    for m in range(micros):
        part = slice(m * rows, (m + 1) * rows)
        laid_part = slice(m * rows * 8, (m + 1) * rows * 8)
        results.append(
            run_back(
                m, token, flags, normed_laid, grad_laid, start, right, decay, feed, tell, ema_omega.reshape(8, 128),
                back[0][4], back[1][4], source_low, grad_source, norm_gain[None],
            )
        )
        if m == 0:
            token, *done = ends(point(grid, [results[0][1]], r_gates, r_in, r_out, r_v))
            d_shared = d_shared + token[0, 0]
            for mask in t_rest[1:]:
                d_shared = fold(d_shared, mask)
    done_gates = finish(grid, [token], r_gates, *done[:1])
    done_in = finish(grid, [token], r_in, *done[1:2])
    done_out = finish(grid, [token], r_out, *done[2:])
    token_v = point(grid, [results[-1][1]], r_v)
    done_v = finish(grid, [token_v], r_v)
    grad_w_out, grad_w_in = share_and_place(grid, [done_out, done_in], [(False,), (True,)], None)
    (grad_w_out,), (grad_w_in,) = grad_w_out, grad_w_in
    grad_w_gates = lax.all_gather(
        done_gates.reshape(width // grid.count, 2 * width), AXES, axis=0, tiled=True
    )

    z = token_v[0, 0]
    spread_in = lambda k: in_place(back[0][k] + z, back[1][k] + z)
    early = [
        jnp.concatenate([jnp.sum(sum_gates + z, axis=0), sums_shared[3] + z]), sums_shared[:2].reshape(-1) + z,
        sums_shared[2] + z, jnp.sum(sum_ffn_gain + z, axis=0), jnp.sum(sum_out + z, axis=0),
        spread_in(2), spread_in(1), in_place(sum_in[0] + z, sum_in[1] + z),
    ]
    sum_eta, sum_one, sum_two, sum_omega, sum_norm_gain = (
        sum(r[k] + z for r in results) for k in range(1, 6)
    )
    late = [
        sum_eta.reshape(-1), sum_one.reshape(-1), sum_two.reshape(-1), jnp.sum(sum_norm_gain, axis=0), sum_omega.reshape(-1)
    ]

    def cut_like(v, parts):
        out, first = [], 0
        for p in parts:
            out.append(v[first : first + p.size])
            first += p.size
        return out

    small = padded(jnp.concatenate(early), 128)
    summed, d_shared = sum_flat(
        grid, padded(jnp.concatenate([jnp.concatenate(late), small]), 2048), d_shared.reshape(width // grid.count, -1)
    )
    grad_w_gates = join(grad_w_gates, d_shared)
    last = cut_like(summed, late)
    cut = cut_like(summed[sum(p.size for p in late) :], early)
    ((grad_w_branch, grad_w_reset, grad_w_value),) = share_and_place(grid, [done_v], [(False, True, True)], None)
    untile = lambda v: v.reshape(heads, width).T
    eta, one, two = (untile(v) for v in last[:3])
    mine = lambda v, n: lax.dynamic_slice_in_dim(v, rank * n, n, 0)
    return (
        output.reshape(inputs.shape),
        jnp.stack([r[0] + z for r in results]),
        last[3],
        ema_beta * one - ema_damp * two,
        -ema_alpha * two,
        ema_alpha * one,
        eta,
        last[4],
        grad_w_gates,
        cut[0],
        cut[1].reshape(2, -1),
        cut[2],
        grad_w_value,
        mine(cut[5], units_v),
        grad_w_reset,
        mine(cut[6], units_v),
        grad_w_branch,
        cut[3],
        grad_w_in,
        mine(cut[7], units_f),
        grad_w_out,
        cut[4],
    )


def solution(mesh):
    rows = P(None, AXES, None)
    col, row, vec, rep = P(None, "tensor"), P("tensor", None), P("tensor"), P()
    return jax.shard_map(
        local,
        mesh=mesh,
        in_specs=(
            rows, P(None, AXES), rows, rep, rep, rep, rep, rep, rep, rep, rep, rep, rep,
            col, vec, col, vec, row, rep, col, vec, row, rep,
        ),
        out_specs=(
            rows, rows, rep, rep, rep, rep, rep, rep, rep, rep, rep, rep,
            col, vec, col, vec, row, rep, col, vec, row, rep,
        ),
        check_vma=False,
    )
```

```python
from functools import partial

import jax
import jax.numpy as jnp
from jax import lax
from jax.experimental import pallas as pl
from jax.experimental.pallas import tpu as pltpu
from jax.sharding import PartitionSpec as P

BLOCK = 128
HIGHEST = lax.Precision.HIGHEST
EPSILON = 1e-06
AXES = ("dp", "tensor")
F32 = jnp.float32
BF16 = jnp.bfloat16


def dot_plain(a, b):
    return jnp.dot(a, b, preferred_element_type=F32)


def dot_against(a, b):
    return lax.dot_general(a, b, (((1,), (1,)), ((), ())), preferred_element_type=F32)


def dot_over_rows(a, b):
    return lax.dot_general(a, b, (((0,), (0,)), ((), ())), preferred_element_type=F32)


def rounded(v):
    return lax.reduce_precision(v, exponent_bits=8, mantissa_bits=7)


def silu_slope(v):
    s = jax.nn.sigmoid(v)
    return s * (1.0 + v * (1.0 - s))


class Grid:
    def __init__(self):
        dp, tensor = lax.axis_size("dp"), lax.axis_size("tensor")
        self.count = dp * tensor
        self.index = lax.axis_index("dp") * tensor + lax.axis_index("tensor")
        masks = lambda n, first: [first << k for k in range(n.bit_length() - 1)]
        self.tensor = masks(tensor, 1)
        self.core, *self.xs = masks(dp, tensor)

    def bit(self, mask):
        return (self.index // mask) % 2

    def swap(self, value, mask):
        return lax.ppermute(value, AXES, [(i, i ^ mask) for i in range(self.count)])


def ema_step(state, row, keep, decay, feed):
    return [(s * keep) * q + f * row for s, q, f in zip(state, decay, feed)]


def row_of(ref, base, r):
    return ref[pl.ds(base + r, 8, stride=8), :]


def spread(ref, block, values):
    for j in range(8):
        ref[pl.ds(pl.multiple_of(block * 64, 64) + 8 * j, 8), :] = values[:, j * 128 : (j + 1) * 128]


def collect(ref, block):
    return jnp.concatenate(
        [ref[pl.ds(pl.multiple_of(block * 64, 64) + 8 * j, 8), :] for j in range(8)], axis=1
    )


def norm_kernel(flags, x_ref, gain_ref, decay_ref, feed_ref, normed_ref, low_ref, final_ref):
    micros, rows = flags.shape
    heads = decay_ref.shape[0]

    def norm_block(b, carry):
        at = pl.ds(pl.multiple_of(b * 16, 16), 16)
        x = x_ref[at, :].astype(F32)
        n = x * lax.rsqrt(jnp.mean(x * x, axis=-1, keepdims=True) + EPSILON) * gain_ref[...]
        low_ref[at, :] = n.astype(BF16)
        spread(normed_ref, 2 * b, n[:8])
        spread(normed_ref, 2 * b + 1, n[8:])
        return carry

    lax.fori_loop(0, micros * rows // 16, norm_block, 0)
    for m in range(micros):
        for h0 in range(0, heads, 8):
            decay = [decay_ref[h0 + h] for h in range(8)]
            feed = [feed_ref[h0 + h] for h in range(8)]

            def block(b, state, m=m, decay=decay, feed=feed):
                base = pl.multiple_of((m * (rows // 8) + b) * 64, 64)
                for r in range(8):
                    keep = (1 - flags[m, b * 8 + r]).astype(F32)
                    state = ema_step(state, row_of(normed_ref, base, r), keep, decay, feed)
                return state

            state = lax.fori_loop(0, rows // 8, block, [jnp.zeros((8, 128), F32)] * 8)
            for h in range(8):
                final_ref[m, h0 + h] = state[h]


def blend_kernel(
    flags, normed_ref, start_ref, decay_ref, feed_ref, out_ref, omega_ref, blended_ref, low_ref, acc_ref
):
    micros, rows = flags.shape
    heads = decay_ref.shape[0]
    omega = omega_ref[...]
    for m in range(micros):
        for h0 in range(0, heads, 8):
            decay = [decay_ref[h0 + h] for h in range(8)]
            feed = [feed_ref[h0 + h] for h in range(8)]
            tell = [out_ref[h0 + h] for h in range(8)]

            def block(b, state, m=m, h0=h0, decay=decay, feed=feed, tell=tell):
                base = pl.multiple_of((m * (rows // 8) + b) * 64, 64)
                for r in range(8):
                    keep = (1 - flags[m, b * 8 + r]).astype(F32)
                    row = row_of(normed_ref, base, r)
                    state = ema_step(state, row, keep, decay, feed)
                    told = [s * t for s, t in zip(state, tell)]
                    while len(told) > 1:
                        told = [told[i] + told[i + 1] for i in range(0, len(told), 2)]
                    at = pl.ds(base + r, 8, stride=8)
                    if h0 == 0:
                        acc_ref[at, :] = told[0] + omega * row
                    else:
                        acc_ref[at, :] = acc_ref[at, :] + told[0]
                return state

            lax.fori_loop(0, rows // 8, block, [start_ref[m, h0 + h] for h in range(8)])

    def finish(b, carry):
        at = pl.ds(pl.multiple_of(b * 16, 16), 16)
        v = jnp.concatenate([collect(acc_ref, 2 * b), collect(acc_ref, 2 * b + 1)], axis=0)
        blended_ref[at, :] = v
        low_ref[at, :] = (v / (1.0 + jnp.exp(-v))).astype(BF16)
        return carry

    lax.fori_loop(0, micros * rows // 16, finish, 0)


def shared_kernel(
    before, flags, gp0_ref, gp1_ref, probs_ref, query_ref, key_ref, shared_ref, pre_ref, gain_ref, gates_ref, weight_ref,
    mix0_ref, mix1_ref, blended_ref, decay_ref, tell_ref,
    rows_ref, left_ref, low_ref, sums_ref,
):
    b = pl.program_id(0)
    width = mix0_ref.shape[-1]
    probs = probs_ref[0]
    grad_probs = gp0_ref[0] + gp1_ref[0]
    scale = query_ref.shape[-1] ** (-0.5)
    grad_scores = probs * (grad_probs - jnp.sum(grad_probs * probs, axis=-1, keepdims=True)) * scale
    exact = partial(lax.dot_general, precision=HIGHEST, preferred_element_type=F32)
    grad_query = exact(grad_scores, key_ref[...].astype(F32), (((1,), (0,)), ((), ())))
    grad_key = exact(grad_scores, query_ref[...].astype(F32), (((0,), (0,)), ((), ())))
    shared = shared_ref[...]
    pre = pre_ref[...]
    grad_pre = (grad_query * gain_ref[0:1] + grad_key * gain_ref[1:2]) * slope(pre, sigmoid(pre))
    low = grad_pre.astype(BF16)
    low_ref[...] = low
    total = lambda v: jnp.sum(v, axis=0, keepdims=True)
    part = jnp.concatenate(
        [
            total(grad_query * shared), total(grad_key * shared), total(grad_query), total(low.astype(F32)),
            jnp.zeros((4, low.shape[-1]), F32),
        ]
    )
    add_to(sums_ref, part)
    mixed = (
        mix0_ref[...]
        + mix1_ref[...]
        + dot_nt(gates_ref[...], weight_ref[:, : 2 * width])
        + dot_nt(low, weight_ref[:, 2 * width :])
    )
    v = blended_ref[...]
    grad = mixed * slope(v, sigmoid(v))
    for i in range(BLOCK // 8):
        spread(rows_ref, b * (BLOCK // 8) + i, grad[8 * i : 8 * i + 8])

    @pl.when(b == pl.num_programs(0) - 1)
    def _():
        micros, rows = flags.shape
        heads = decay_ref.shape[0]
        for m in range(micros):
            for h0 in range(0, heads, 8):
                decay = [decay_ref[h0 + h] for h in range(8)]
                tell = [tell_ref[h0 + h] for h in range(8)]

                def block(i, left, m=m, decay=decay, tell=tell):
                    b = rows // 8 - 1 - i
                    base = pl.multiple_of((m * (rows // 8) + b) * 64, 64)
                    for r in reversed(range(8)):
                        keep = (1 - flags[m, b * 8 + r]).astype(F32)
                        row = row_of(rows_ref, base, r)
                        left = [((t * row + k) * keep) * q for k, q, t in zip(left, decay, tell)]
                    return left

                left = lax.fori_loop(0, rows // 8, block, [jnp.zeros((8, 128), F32)] * 8)
                for h in range(8):
                    left_ref[m, h0 + h] = left[h]


def run_shared(token, flags, gp0, gp1, probs, query, key, shared, pre, gain, gates, weight, mix0, mix1, blended, decay, tell):
    total, width = mix0.shape
    z = query.shape[1]
    rows = lambda n: pl.BlockSpec((BLOCK, n), lambda b: (b, 0))
    pair = pl.BlockSpec((1, BLOCK, BLOCK), lambda b: (b, 0, 0))
    whole = lambda a: pl.BlockSpec(a.shape, lambda b: (0,) * a.ndim)
    micros, heads = flags.shape[0], decay.shape[0]
    return pl.pallas_call(
        shared_kernel,
        grid=(total // BLOCK,),
        in_specs=[
            pl.BlockSpec(memory_space=pl.ANY), pl.BlockSpec(memory_space=pltpu.SMEM), pair, pair, pair, rows(z), rows(z), rows(z), rows(z), whole(gain),
            rows(2 * width), whole(weight), rows(width), rows(width), rows(width), whole(decay), whole(tell),
        ],
        out_specs=[
            pl.BlockSpec((total * 8, 128), lambda b: (0, 0)),
            pl.BlockSpec((micros, heads, 8, 128), lambda b: (0, 0, 0, 0)),
            rows(z),
            pl.BlockSpec((8, z), lambda b: (0, 0)),
        ],
        out_shape=[
            shape_of(total * 8, 128), shape_of(micros, heads, 8, 128), shape_of(total, z, dtype=BF16), shape_of(8, z),
        ],
        cost_estimate=cost(200),
    )(token, flags, gp0, gp1, probs, query, key, shared, pre, gain, gates, weight, mix0, mix1, blended, decay, tell)


def back_kernel(
    m, before, flags, normed_ref, rows_ref, start_ref, right_ref, decay_ref, feed_ref, tell_ref, omega_ref,
    add0_ref, add1_ref, source_ref, base_ref, gain_ref,
    grad_ref, eta_ref, one_ref, two_ref, omega_out, gain_out, token_ref, states, acc_ref,
):
    rows = flags.shape[1]
    heads = decay_ref.shape[0]
    group = 4
    omega = omega_ref[...]
    zero = jnp.zeros((8, 128), F32)
    token_ref[...] = zero
    for h0 in range(0, heads, group):
        decay = [decay_ref[h0 + h] for h in range(group)]
        feed = [feed_ref[h0 + h] for h in range(group)]
        tell = [tell_ref[h0 + h] for h in range(group)]

        def ahead(b, state, decay=decay, feed=feed):
            base = pl.multiple_of(b * 64, 64)
            for r in range(8):
                keep = (1 - flags[m, b * 8 + r]).astype(F32)
                for h in range(group):
                    states[b * 8 + r, h] = state[h]
                state = ema_step(state, row_of(normed_ref, base, r), keep, decay, feed)
            return state

        last = lax.fori_loop(0, rows // 8, ahead, [start_ref[0, h0 + h] for h in range(group)])

        def back(i, carry, h0=h0, decay=decay, feed=feed, tell=tell):
            left, after_state, eta, one, two, with_omega = carry
            b = rows // 8 - 1 - i
            base = pl.multiple_of(b * 64, 64)
            for r in reversed(range(8)):
                keep = (1 - flags[m, b * 8 + r]).astype(F32)
                g = row_of(rows_ref, base, r)
                x = row_of(normed_ref, base, r)
                earlier = [states[b * 8 + r, h] for h in range(group)]
                eta = [e + s * g for e, s in zip(eta, after_state)]
                now = [t * g + k for t, k in zip(tell, left)]
                one = [o + n * x for o, n in zip(one, now)]
                kept = [n * keep for n in now]
                two = [w + k * s for w, k, s in zip(two, kept, earlier)]
                left = [k * q for k, q in zip(kept, decay)]
                gn = [n * f for n, f in zip(now, feed)]
                while len(gn) > 1:
                    gn = [gn[i] + gn[i + 1] for i in range(0, len(gn), 2)]
                at = pl.ds(base + r, 8, stride=8)
                if h0 == 0:
                    acc_ref[at, :] = gn[0] + omega * g
                    with_omega = with_omega + g * x
                else:
                    acc_ref[at, :] = acc_ref[at, :] + gn[0]
                after_state = earlier
            return left, after_state, eta, one, two, with_omega

        right = [right_ref[0, h0 + h] for h in range(group)]
        nothing = [zero] * group
        _, _, eta, one, two, with_omega = lax.fori_loop(
            0, rows // 8, back, (right, last, nothing, nothing, nothing, zero)
        )
        if h0 == 0:
            omega_out[...] = with_omega
        for h in range(group):
            eta_ref[h0 + h] = eta[h]
            one_ref[h0 + h] = one[h]
            two_ref[h0 + h] = two[h]

    def finish(b, gained):
        at = pl.ds(pl.multiple_of(b * 16, 16), 16)
        x = source_ref[at, :].astype(F32)
        scale = lax.rsqrt(jnp.mean(x * x, axis=-1, keepdims=True) + EPSILON)
        scaled = x * scale
        grad = jnp.concatenate([collect(acc_ref, 2 * b), collect(acc_ref, 2 * b + 1)], axis=0)
        grad = grad + add0_ref[at, :] + add1_ref[at, :]
        own = grad * scaled
        gained = gained + own[:8] + own[8:]
        inner = grad * gain_ref[...]
        mean = jnp.mean(inner * scaled, axis=-1, keepdims=True)
        grad_ref[at, :] = base_ref[at, :] + scale * (inner - scaled * mean)
        return gained

    width = source_ref.shape[-1]
    gain_out[...] = lax.fori_loop(0, rows // 16, finish, jnp.zeros((8, width), F32))


def run_back(m, token, flags, laid, grads, start, right, decay, feed, tell, omega, add0, add1, source, base, gain):
    rows, heads = flags.shape[1], decay.shape[0]
    width = source.shape[1]
    whole = lambda a: pl.BlockSpec(a.shape, lambda i: (0,) * a.ndim)
    tall = pl.BlockSpec((rows * 8, 128), lambda i: (m, 0))
    carry = pl.BlockSpec((1, heads, 8, 128), lambda i: (m, 0, 0, 0))
    wide = pl.BlockSpec((rows, width), lambda i: (m, 0))
    sums = pl.BlockSpec((heads, 8, 128), lambda i: (0, 0, 0))
    return pl.pallas_call(
        partial(back_kernel, m),
        grid=(1,),
        in_specs=[
            pl.BlockSpec(memory_space=pl.ANY), pl.BlockSpec(memory_space=pltpu.SMEM), tall, tall, carry, carry,
            whole(decay), whole(feed), whole(tell), whole(omega), wide, wide, wide, wide, whole(gain),
        ],
        out_specs=[
            pl.BlockSpec((rows, width), lambda i: (0, 0)), sums, sums, sums,
            pl.BlockSpec((8, 128), lambda i: (0, 0)), pl.BlockSpec((8, width), lambda i: (0, 0)),
            pl.BlockSpec((8, 128), lambda i: (0, 0)),
        ],
        out_shape=[
            jax.ShapeDtypeStruct((rows, width), F32),
            *[jax.ShapeDtypeStruct((heads, 8, 128), F32)] * 3,
            jax.ShapeDtypeStruct((8, 128), F32),
            jax.ShapeDtypeStruct((8, width), F32),
            jax.ShapeDtypeStruct((8, 128), F32),
        ],
        scratch_shapes=[pltpu.VMEM((rows, 4, 8, 128), F32), pltpu.VMEM((rows * 8, 128), F32)],
        cost_estimate=cost(200),
    )(token, flags, laid, grads, start, right, decay, feed, tell, omega, add0, add1, source, base, gain)


def dot_tn(a, b):
    return lax.dot_general(a, b, (((0,), (0,)), ((), ())), preferred_element_type=F32)


def dot_nt(a, b):
    return lax.dot_general(a, b, (((1,), (1,)), ((), ())), preferred_element_type=F32)


def dot_nn(a, b):
    return lax.dot_general(a, b, (((1,), (0,)), ((), ())), preferred_element_type=F32)


def sigmoid(v):
    return 1.0 / (1.0 + jnp.exp(-v))


def slope(v, s):
    return s * (1.0 + v * (1.0 - s))


def add_to(ref, value, first_ref=None):
    first = pl.program_id(0) == 0

    @pl.when(first)
    def _():
        ref[...] = value if first_ref is None else first_ref[...] + value

    @pl.when(jnp.logical_not(first))
    def _():
        ref[...] = ref[...] + value


def put_sides(ref, lead, v):
    half = v.shape[-1] // 2
    v = v.astype(BF16)
    ref[0, lead] = v[:, :half]
    ref[1, lead] = v[:, half:]


def value_kernel(
    piece, normed_ref, mixed_ref, probs_ref, wv_ref, wr_ref, wb_ref, bv_ref, br_ref,
    value_ref, reset_ref, attended_ref, gated_ref, out_ref,
):
    value_pre = dot_nt(normed_ref[...], flat(wv_ref)) + bv_ref[...]
    value_ref[...] = value_pre
    value = (value_pre * sigmoid(value_pre)).astype(BF16)
    blocks = probs_ref.shape[0]
    attended = jnp.concatenate(
        [dot_nn(probs_ref[b], value[b * BLOCK : (b + 1) * BLOCK]) for b in range(blocks)], axis=0
    )
    attended_ref[...] = attended
    reset_pre = dot_nt(mixed_ref[...], flat(wr_ref)) + br_ref[...]
    reset_ref[...] = reset_pre
    gated = (reset_pre * sigmoid(reset_pre) * attended).astype(BF16)
    gated_ref[...] = gated
    add_to(out_ref, dot_nn(gated, flat(wb_ref)))


def value_back_kernel(
    piece, grad_ref, normed_ref, mixed_ref, probs_ref, wv_ref, wr_ref, wb_ref,
    value_ref, reset_ref, attended_ref, gated_ref,
    d_ref, sum_r_ref, sum_v_ref, mixed_out, normed_out, probs_out,
):
    grad = grad_ref[...]
    grad_gated = dot_nt(grad, flat(wb_ref))
    put_sides(d_ref, 0, dot_tn(gated_ref[...], grad))
    reset_pre = reset_ref[...]
    s = sigmoid(reset_pre)
    grad_attended = (grad_gated * (reset_pre * s)).astype(BF16)
    grad_reset = (grad_gated * attended_ref[...] * slope(reset_pre, s)).astype(BF16)
    sum_r_ref[...] = jnp.sum(grad_reset.astype(F32), axis=0, keepdims=True)
    mixed = mixed_ref[...]
    put_sides(d_ref, 1, dot_tn(grad_reset, mixed))
    add_to(mixed_out, dot_nn(grad_reset, flat(wr_ref)))
    value_pre = value_ref[...]
    s = sigmoid(value_pre)
    value = (value_pre * s).astype(BF16)
    blocks = probs_ref.shape[0]
    grad_value, grad_probs = [], []
    for b in range(blocks):
        rows = slice(b * BLOCK, (b + 1) * BLOCK)
        grad_probs.append(dot_nt(grad_attended[rows], value[rows])[None])
        grad_value.append(dot_tn(probs_ref[b], grad_attended[rows]))
    add_to(probs_out, jnp.concatenate(grad_probs, axis=0))
    grad_value = (jnp.concatenate(grad_value, axis=0) * slope(value_pre, s)).astype(BF16)
    sum_v_ref[...] = jnp.sum(grad_value.astype(F32), axis=0, keepdims=True)
    put_sides(d_ref, 2, dot_tn(grad_value, normed_ref[...]))
    add_to(normed_out, dot_nn(grad_value, flat(wv_ref)))


def inner_kernel(piece, ffn_ref, grad_ref, wi_ref, bi_ref, pre_ref, activ_ref, do_ref):
    wi = flat(wi_ref)
    pre = dot_nt(ffn_ref[...], wi) + bi_ref[...]
    pre_ref[...] = pre
    activ = (pre * sigmoid(pre)).astype(BF16)
    activ_ref[...] = activ
    put_sides(do_ref, 0, dot_tn(activ, grad_ref[...]))


def outer_kernel(
    piece, ffn_ref, grad_ref, wi_ref, wo_ref, pre_ref, activ_ref, *rest
):
    *sums, di_ref, sum_i_ref, out_ref, ffn_out = rest
    sum_o_ref, sum_f_ref = sums if sums else (None, None)
    wi = flat(wi_ref)
    wo = flat(wo_ref)
    add_to(out_ref, dot_nn(activ_ref[...], wo), sum_o_ref)
    pre = pre_ref[...]
    grad = (dot_nt(grad_ref[...], wo) * slope(pre, sigmoid(pre))).astype(BF16)
    sum_i_ref[...] = jnp.sum(grad.astype(F32), axis=0, keepdims=True)
    put_sides(di_ref, 0, dot_tn(grad, ffn_ref[...]))
    add_to(ffn_out, dot_nn(grad, wi), sum_f_ref)


UNITS = 512


def cost(micros):
    return pl.CostEstimate(flops=int(micros * SCALE * 1.15e9), bytes_accessed=int(micros * SCALE * 3.3e6), transcendentals=0)


SCALE = 1.0


def shape_of(*dims, dtype=F32):
    return jax.ShapeDtypeStruct(dims, dtype)


def middle(gate_ref, branch_ref, source_ref):
    width = source_ref.shape[-1]
    update = sigmoid(gate_ref[:, :width])
    pre = gate_ref[:, width : 2 * width] + branch_ref[...]
    s = sigmoid(pre)
    return source_ref[...].astype(F32), update, pre, s


def middle_kernel(gate_ref, branch_ref, source_ref, gain_ref, mixed_ref, ffn_ref):
    source, update, pre, s = middle(gate_ref, branch_ref, source_ref)
    mixed = update * (pre * s) + (1.0 - update) * source
    mixed_ref[...] = mixed
    scale = lax.rsqrt(jnp.mean(mixed * mixed, axis=-1, keepdims=True) + EPSILON)
    ffn_ref[...] = (mixed * scale * gain_ref[...]).astype(BF16)


def column_sums(v):
    return jnp.sum(v.reshape(-1, 8, v.shape[-1]), axis=0)


def middle_back_kernel(
    before, gate_ref, branch_ref, source_ref, gain_ref, bias_ref, mixed_ref, feed_ref, grad_ref, ffn_ref,
    out_ref, base_ref, gates_ref, sum_gain_ref, sum_out_ref, sum_gates_ref,
):
    width = source_ref.shape[-1]
    source, update, pre, s = middle(gate_ref, branch_ref, source_ref)
    mixed = mixed_ref[...]
    out_ref[...] = (mixed + feed_ref[...] + bias_ref[...]).astype(BF16)
    scale = lax.rsqrt(jnp.mean(mixed * mixed, axis=-1, keepdims=True) + EPSILON)
    scaled = mixed * scale
    grad_out = grad_ref[...].astype(F32)
    grad_ffn = ffn_ref[...]
    add_to(sum_out_ref, column_sums(grad_out))
    add_to(sum_gain_ref, column_sums(grad_ffn * scaled))
    gained = grad_ffn * gain_ref[...]
    grad = grad_out + scale * (gained - scaled * jnp.mean(gained * scaled, axis=-1, keepdims=True))
    base_ref[...] = grad * (1.0 - update)
    grad_update = (grad * (pre * s - source) * update * (1.0 - update)).astype(BF16)
    grad_hidden = (grad * update * slope(pre, s)).astype(BF16)
    gates_ref[:, :width] = grad_update
    gates_ref[:, width:] = grad_hidden
    add_to(
        sum_gates_ref,
        jnp.concatenate([column_sums(grad_update.astype(F32)), column_sums(grad_hidden.astype(F32))], axis=1),
    )


def run_middle(gate, branch, source, gain):
    total, width = source.shape
    rows = lambda n: pl.BlockSpec((BLOCK, n), lambda i: (i, 0))
    line = pl.BlockSpec((1, width), lambda i: (0, 0))
    return pl.pallas_call(
        middle_kernel,
        grid=(total // BLOCK,),
        in_specs=[rows(gate.shape[1]), rows(width), rows(width), line],
        out_specs=[rows(width), rows(width)],
        out_shape=[shape_of(total, width), shape_of(total, width, dtype=BF16)],
        cost_estimate=cost(5),
    )(gate, branch, source, gain[None])


def run_middle_back(token, gate, branch, source, gain, bias, mixed, feed, grad, ffn):
    total, width = source.shape
    rows = lambda n: pl.BlockSpec((BLOCK, n), lambda i: (i, 0))
    line = pl.BlockSpec((1, width), lambda i: (0, 0))
    few = lambda n: pl.BlockSpec((8, n), lambda i: (0, 0))
    wide = rows(width)
    return pl.pallas_call(
        middle_back_kernel,
        grid=(total // BLOCK,),
        in_specs=[
            pl.BlockSpec(memory_space=pl.ANY), rows(gate.shape[1]), wide, wide, line, line, wide, wide, wide, wide
        ],
        out_specs=[wide, wide, rows(2 * width), few(width), few(width), few(2 * width)],
        out_shape=[
            shape_of(total, width, dtype=BF16), shape_of(total, width), shape_of(total, 2 * width, dtype=BF16),
            shape_of(8, width), shape_of(8, width), shape_of(8, 2 * width),
        ],
        cost_estimate=cost(1),
    )(token, gate, branch, source, gain[None], bias[None], mixed, feed, grad, ffn)


def gates_kernel(piece, before, mixed_ref, gates_ref, d_ref):
    grad = dot_tn(mixed_ref[...], gates_ref[...]).astype(BF16)
    half = grad.shape[-1] // 2
    d_ref[0] = grad[:, :half].reshape(d_ref.shape[1:])
    d_ref[1] = grad[:, half:].reshape(d_ref.shape[1:])


def run_gates(which, token, mixed, gates):
    total, width = mixed.shape
    n = which.shape[0]
    block = width // (2 * n)
    return pl.pallas_call(
        gates_kernel,
        grid_spec=pltpu.PrefetchScalarGridSpec(
            num_scalar_prefetch=1,
            grid=(n,),
            in_specs=[
                pl.BlockSpec(memory_space=pl.ANY),
                pl.BlockSpec((total, block), lambda i, p: (0, p[i])),
                pl.BlockSpec(gates.shape, lambda i, p: (0, 0)),
            ],
            out_specs=pl.BlockSpec((2, 1, block, width), lambda i, p: (0, 0, i, 0)),
        ),
        out_shape=shape_of(2, 1, n * block, width, dtype=BF16),
        cost_estimate=cost(1),
    )(which, token, mixed, gates)


class Pieces:
    def __init__(self, gathered, outer, which, tensor, part_f, part_v):
        self.gathered, self.outer, self.which, self.tensor = gathered, outer, which, tensor
        self.part_f, self.part_v = part_f, part_v
        self.width = gathered.shape[-1]

    def units(self, part):
        return self.which.shape[0] * self.tensor * part

    def block(self, part):
        return min(UNITS, self.tensor * part)

    def spec(self, part, row):
        step = self.block(part) // part
        per = self.tensor // step
        return pl.BlockSpec(
            (step, part, self.width), lambda i, p: (p[i // per] * per + i % per, row // part, 0)
        )

    @property
    def w_in(self):
        return self.spec(self.part_f, 0)

    @property
    def w_out(self):
        return self.spec(self.part_f, 0)

    def v(self, k):
        return self.spec(self.part_v, self.part_f + k * self.part_v)


def flat(ref):
    return ref[...].reshape(-1, ref.shape[-1])


def blocked(kernel, micros, pieces, steps, token, in_specs, out_specs, out_shape, *arrays):
    def body(piece, before, *refs):
        kernel(piece, *refs)

    return pl.pallas_call(
        body,
        grid_spec=pltpu.PrefetchScalarGridSpec(
            num_scalar_prefetch=1,
            grid=(steps,),
            in_specs=[pl.BlockSpec(memory_space=pl.ANY), *in_specs],
            out_specs=out_specs,
        ),
        out_shape=out_shape,
        cost_estimate=cost(micros),
    )(pieces.which, token, *arrays)


def block_specs(total, width, block, lead):
    full = pl.BlockSpec((total, width), lambda i, p: (0, 0))
    cols = pl.BlockSpec((total, block), lambda i, p: (0, i))
    line = pl.BlockSpec((1, block), lambda i, p: (0, i))
    grads = pl.BlockSpec((2, lead, block, width // 2), lambda i, p: (0, 0, i, 0))
    return full, cols, line, grads


def run_value(pieces, token, normed, mixed, probs, bv, br):
    total, width = normed.shape
    units, block = pieces.units(pieces.part_v), pieces.block(pieces.part_v)
    full, cols, line, grads = block_specs(total, width, block, 3)
    pairs = pl.BlockSpec(probs.shape, lambda i, p: (0, 0, 0))
    g = pieces.gathered
    return blocked(
        value_kernel, 200, pieces, units // block, token,
        [full, full, pairs, pieces.v(0), pieces.v(1), pieces.v(2), line, line],
        [cols, cols, cols, cols, full],
        [shape_of(total, units)] * 3 + [shape_of(total, units, dtype=BF16), shape_of(total, width)],
        normed, mixed, probs, g, g, g, bv, br,
    )


def run_value_back(pieces, k, micros, token, grad, normed, mixed, probs, kept):
    total, width = normed.shape
    units, block = pieces.units(pieces.part_v), pieces.block(pieces.part_v)
    full, cols, line, grads = block_specs(total, width, block, 3)
    pairs = pl.BlockSpec(probs.shape, lambda i, p: (0, 0, 0))
    g = pieces.gathered
    return blocked(
        value_back_kernel, micros, pieces, units // block, token,
        [
            pl.BlockSpec((total, width), lambda i, p: (0, 1)), full, full, pairs,
            pieces.v(0), pieces.v(1), pieces.v(2), *[pl.BlockSpec((total, block), lambda i, p: (0, k * (units // block) + i))] * 4,
        ],
        [grads, line, line, full, full, pairs],
        [shape_of(2, 3, units, width // 2, dtype=BF16)]
        + [shape_of(1, units)] * 2
        + [shape_of(total, width)] * 2
        + [shape_of(*probs.shape)],
        grad, normed, mixed, probs, g, g, g, *kept,
    )


def run_inner(pieces, token, ffn, grad, bias):
    total, width = ffn.shape
    units, block = pieces.units(pieces.part_f), pieces.block(pieces.part_f)
    full, cols, line, grads = block_specs(total, width, block, 1)
    return blocked(
        inner_kernel, 200, pieces, units // block, token,
        [full, full, pieces.w_in, line],
        [cols, cols, grads],
        [shape_of(total, units), shape_of(total, units, dtype=BF16), shape_of(2, 1, units, width // 2, dtype=BF16)],
        ffn, grad, pieces.gathered, bias,
    )


def run_outer(pieces, token, ffn, grad, pre, activ, *before):
    total, width = ffn.shape
    units, block = pieces.units(pieces.part_f), pieces.block(pieces.part_f)
    full, cols, line, grads = block_specs(total, width, block, 1)
    return blocked(
        outer_kernel, 200, pieces, units // block, token,
        [full, full, pieces.w_in, pieces.w_out, cols, cols, *[full] * len(before)],
        [grads, line, full, full],
        [shape_of(2, 1, units, width // 2, dtype=BF16), shape_of(1, units), shape_of(total, width), shape_of(total, width)],
        ffn, grad, pieces.gathered, pieces.outer, pre, activ, *before,
    )


def call(kernel, outs, scratch, smem, *arrays):
    return pl.pallas_call(
        kernel,
        out_shape=outs,
        in_specs=[pl.BlockSpec(memory_space=pltpu.SMEM)] * smem
        + [pl.BlockSpec(memory_space=pltpu.VMEM)] * (len(arrays) - smem),
        out_specs=jax.tree.map(lambda _: pl.BlockSpec(memory_space=pltpu.VMEM), outs),
        scratch_shapes=scratch,
        cost_estimate=cost(12),
    )(*arrays)


def scan_carry(grid, local, clear, whole, reverse):
    micros, heads = local.shape[:2]
    clear = jnp.broadcast_to(clear[:, None, None, None], (micros, 1, 8, 128))
    entering = jnp.zeros_like(local)
    reach = jnp.ones_like(local)
    total = local
    for mask in grid.tensor:
        got = grid.swap(jnp.concatenate([total, clear], axis=1), mask)
        got_total, got_clear = got[:, :heads], got[:, heads:]
        later = grid.bit(mask) == (0 if reverse else 1)
        entering = jnp.where(later, entering + reach * got_total, entering)
        reach = jnp.where(later, reach * got_clear * whole, reach)
        total = jnp.where(
            later, total + clear * whole * got_total, got_total + got_clear * whole * total
        )
        clear = clear * got_clear
        whole = whole * whole
    return entering


def after(values, *others):
    return lax.optimization_barrier((values, others))[0]


class Term:
    def __init__(self, array, labels, fixed):
        self.array, self.labels, self.fixed = array, labels, fixed


class Reduce:
    def __init__(self, grid, high, dims, still=()):
        self.grid, self.dims, self.still = grid, list(dims), still
        self.labels = ["side", "lead", *self.dims, "u", "h"]
        xs, (lo, *hi) = grid.xs[::-1], grid.tensor
        self.orders = [[*xs, lo], [lo, *xs]], hi[::-1]
        self.step = -1
        self.high = self.view(high)
        self.raw = [grid.swap(self.high, grid.core)]

    def view(self, v):
        n = len(self.dims)
        return v.reshape(*v.shape[:2], *[2] * n, v.shape[2] >> n, v.shape[3])

    @property
    def steps(self):
        return len(self.orders[0][0]) + len(self.orders[1])

    def add_low(self, low):
        self.low = self.view(low)

    def take(self):
        if self.step < 0:
            self.sides = [[Term(a, self.labels, {"side": s}) for a in (self.low, self.raw[0])] for s in (0, 1)]
            self.left = [list(self.dims), list(self.dims)]
        else:
            for s in (0, 1):
                for t in self.sides[s]:
                    if self.masks[s] in t.labels:
                        t.fixed[self.masks[s]] = 0
                self.left[s] = [d for d in self.left[s] if d != self.masks[s]]
                if len(self.raw) == 2:
                    self.sides[s].append(Term(self.raw[s], ["lead", *self.left[s], "u", "h"], {}))
                else:
                    self.sides[s].append(Term(self.raw[0], ["lead", *self.left[s], "u", "hh"], {"hh": s}))
        self.step += 1

    def wanted(self):
        (first, second), hi = self.orders
        k = self.step
        if k == self.steps:
            return [(self.sides[s], {}, self.left[s]) for s in (0, 1)], True
        self.masks = [first[k], second[k]] if k < len(first) else [hi[k - len(first)]] * 2
        return [
            (self.sides[s], {self.masks[s]: 1}, [d for d in self.left[s] if d != self.masks[s]]) for s in (0, 1)
        ], k >= len(first)

    def start(self, sends):
        if len(sends) == 2:
            self.raw = [self.grid.swap(v, m) for v, m in zip(sends, self.masks)]
        else:
            self.raw = [self.grid.swap(sends[0], self.masks[0])]


def place_of(grid, still, fixed, name, sel):
    if name in still:
        masks = [*grid.tensor, *grid.xs]
        return sel[2 * masks.index(name) + fixed[name]]
    return fixed[name]


def picked(grid, still, term, extra, sel):
    v = term.array
    fixed = {**term.fixed, **extra}
    for axis in reversed(range(len(term.labels))):
        name = term.labels[axis]
        if name == "hh":
            half = v.shape[-1] // 2
            v = v[..., fixed[name] * half : (fixed[name] + 1) * half]
        elif name in fixed:
            v = lax.dynamic_index_in_dim(v, place_of(grid, still, fixed, name, sel), axis, False)
    return v.astype(F32)


def point(grid, gates, *sums, behind=None):
    for r in sums:
        r.take()
    outs, tasks = [], []
    for r in sums:
        sides, joined = r.wanted()
        for terms, fixed, left in sides:
            tasks.append((r, terms, fixed, left))
        shapes = []
        for terms, fixed, left in sides:
            low = r.low.shape
            shapes.append((low[1], *[2] * len(left), *low[-2:]))
        if joined:
            outs.append((*shapes[0][:-1], 2 * shapes[0][-1]))
        else:
            outs.extend(shapes)
    pair = [
        k for k in range(len(sums) - 1)
        if 0 < len(sums[k].orders[0][0]) <= sums[k].step < sums[k].steps
        and sums[k].step == sums[k + 1].step and sums[k].low.shape == sums[k + 1].low.shape
    ]
    sel = grid.sel
    fits = all(len(r.dims) <= 4 and r.low.shape[-2] % 32 == 0 for r in sums)
    if fits:
        *values, token = run_point(grid, gates, tasks, outs, sel)
    else:
        values = []
        sides = [
            sum(picked(grid, r.still, t, {k: v for k, v in fixed.items() if k in t.labels}, sel) for t in terms).astype(BF16)
            for r, terms, fixed, left in tasks
        ]
        for shape in outs:
            v = sides.pop(0)
            values.append(v if v.shape == shape else jnp.concatenate([v, sides.pop(0)], axis=-1))
        token = after(jnp.zeros((8, 128), F32), [g[(0,) * g.ndim] for g in gates])
    if behind is not None:
        values, behind = lax.optimization_barrier((values, behind))
    done, skip = [], False
    for k, r in enumerate(sums):
        if skip:
            skip = False
            continue
        if r.step == r.steps:
            done.append(values.pop(0))
        elif k in pair:
            both = grid.swap(jnp.concatenate(values[:2]), r.masks[0])
            n = values[0].shape[0]
            r.raw, sums[k + 1].raw = [both[:n]], [both[n:]]
            values, skip = values[2:], True
        else:
            n = 2 if r.step < len(r.orders[0][0]) else 1
            r.start(values[:n])
            values = values[n:]
    if behind is not None:
        return token, behind
    return (token, *done) if done else token


def run_point(grid, gates, tasks, outs, sel):
    parts = 2
    arrays, specs, layout = [], [], []
    for r, terms, extra, left in tasks:
        mine = []
        for t in terms:
            fixed = {**t.fixed, **{k: v for k, v in extra.items() if k in t.labels}}
            block = []
            for name, size in zip(t.labels, t.array.shape):
                if name == "hh":
                    block.append(size // 2)
                elif name == "u":
                    block.append(size // parts)
                else:
                    block.append(None if name in fixed else size)

            def index(i, p, t=t, fixed=fixed, r=r):
                return tuple(
                    i if name == "u" else place_of(grid, r.still, fixed, name, p) if name in fixed else 0
                    for name in t.labels
                )

            mine.append(len(arrays))
            arrays.append(t.array)
            specs.append(pl.BlockSpec(tuple(block), index))
        layout.append(mine)
    out_specs = []
    for shape in outs:
        block = (*shape[:-2], shape[-2] // parts, shape[-1])
        out_specs.append(pl.BlockSpec(block, lambda i, p, n=len(shape): (*[0] * (n - 2), i, 0)))
    out_specs.append(pl.BlockSpec((8, 128), lambda i, p: (0, 0)))

    def body(p, *refs):
        refs = refs[len(gates) :]
        ins, results = refs[: len(arrays)], refs[len(arrays) :]
        queue = list(layout)
        for ref in results[:-1]:
            first = 0
            while first < ref.shape[-1]:
                mine = queue.pop(0)
                total = ins[mine[0]][...].astype(F32)
                for k in mine[1:]:
                    total = total + ins[k][...].astype(F32)
                ref[..., first : first + total.shape[-1]] = total.astype(BF16)
                first += total.shape[-1]
        results[-1][...] = jnp.zeros((8, 128), F32)

    return pl.pallas_call(
        body,
        grid_spec=pltpu.PrefetchScalarGridSpec(
            num_scalar_prefetch=1,
            grid=(parts,),
            in_specs=[pl.BlockSpec(memory_space=pl.ANY)] * len(gates) + specs,
            out_specs=out_specs,
        ),
        out_shape=[shape_of(*shape, dtype=BF16) for shape in outs] + [shape_of(8, 128)],
        cost_estimate=cost(1),
    )(sel, *gates, *arrays)


def ends(result):
    return result if isinstance(result, tuple) else (result,)


def finish(grid, gates, r, value=None):
    while value is None:
        out = point(grid, gates, r)
        value = out[1] if isinstance(out, tuple) else None
    return value


def share_units(grid, part):
    held = part[None]
    masks = [*grid.xs, grid.core]
    for mask in masks:
        held = jnp.concatenate([held, grid.swap(held, mask)], axis=0)
    n = held.shape[0]
    held = held.astype(F32)
    for k, mask in enumerate(masks):
        held = held.reshape(n >> (k + 1), 2, -1, *part.shape)
        held = jnp.where(grid.bit(mask) == 1, held[:, ::-1], held)
    held = held.reshape(n, *part.shape).transpose(1, 0, 2, 3)
    return held.reshape(part.shape[0], -1, part.shape[-1])


def place_kernel(turned, bits, own_ref, x_ref, c_ref, *outs):
    swap_c, swap_x = bits[0] == 1, bits[1] == 1
    outs[-1][...] = jnp.zeros((8, 128), F32)
    for k, turn in enumerate(turned):
        rows = []
        for own, other in ((own_ref[k], x_ref[k]), (c_ref[0, k], c_ref[1, k])):
            own, other = own.astype(F32), other.astype(F32)
            rows.append(jnp.concatenate([jnp.where(swap_x, other, own), jnp.where(swap_x, own, other)], axis=0))
        v = jnp.concatenate(
            [jnp.where(swap_c, rows[1], rows[0]), jnp.where(swap_c, rows[0], rows[1])], axis=0
        )
        outs[k][...] = v.T if turn else v


def share_and_place(grid, parts, turned, zero):
    results = []
    for part, turns in zip(parts, turned):
        if zero is not None:
            part = part + zero
        lead, units, width = part.shape
        if len(grid.xs) > 1 or units % 16:
            rows = share_units(grid, part)
            results.append([r.T if t else r for r, t in zip(rows, turns)])
            continue
        from_x = grid.swap(part, grid.xs[0])
        from_c = grid.swap(jnp.stack([part, from_x]), grid.core)
        results.append(
            pl.pallas_call(
                partial(place_kernel, turns),
                in_specs=[pl.BlockSpec(memory_space=pltpu.SMEM)] + [pl.BlockSpec(memory_space=pltpu.VMEM)] * 3,
                out_specs=[pl.BlockSpec(memory_space=pltpu.VMEM)] * (lead + 1),
                out_shape=[shape_of(*((width, 4 * units) if t else (4 * units, width))) for t in turns] + [shape_of(8, 128)],
                cost_estimate=cost(5),
            )(jnp.stack([grid.bit(grid.core), grid.bit(grid.xs[0])]).astype(jnp.int32), part, from_x, from_c)
        )
    return results


def pack_kernel(
    bits, before, eta0, eta1, one0, one1, two0, two1, omega0, omega1, gain0, gain1, gates_ref, shared_ref, ffn_ref, out_sum_ref,
    v0, v1, r0, r1, i0, i1, packed_ref, rows,
):
    heads = eta0.shape[0]
    n = heads * 8
    for k, (a, b) in enumerate(((eta0, eta1), (one0, one1), (two0, two1))):
        rows[k * n : (k + 1) * n] = (a[...] + b[...]).reshape(n, 128)
    at = 3 * n

    def line(v, at):
        for j in range(v.shape[-1] // 128):
            rows[at + j : at + j + 1] = v[:, j * 128 : (j + 1) * 128]
        return at + v.shape[-1] // 128

    total = lambda v: jnp.sum(v, axis=0, keepdims=True)
    at = line(total(gain0[...] + gain1[...]), at)
    rows[at : at + 8] = omega0[...] + omega1[...]
    at = line(total(gates_ref[...]), at + 8)
    rows[at : at + 1] = shared_ref[3:4]
    rows[at + 1 : at + 4] = shared_ref[0:3]
    at = line(total(ffn_ref[...]), at + 4)
    at = line(total(out_sum_ref[...]), at)
    core, x = bits[0], bits[1]
    tensor = i0.shape[-1] // 256
    for low, high in ((v0, v1), (r0, r1)):
        for k, ref in enumerate((low, high)):
            for t in range(tensor):
                own, other = (ref[:, (q * tensor + t) * 64 : (q * tensor + t + 1) * 64] for q in (0, 1))
                row = jnp.where(
                    x == 0, jnp.concatenate([own, other], axis=1), jnp.concatenate([other, own], axis=1)
                )
                rows[pl.ds(at + 2 * t + (core ^ k), 1), :] = row
        at += 2 * tensor
    for k, ref in enumerate((i0, i1)):
        for q in (0, 1):
            for t in range(tensor):
                row = ref[:, (q * tensor + t) * 128 : (q * tensor + t + 1) * 128]
                rows[pl.ds(at + 4 * t + 2 * (core ^ k) + (x ^ q), 1), :] = row
    at += 4 * tensor
    rows[at:] = jnp.zeros((rows.shape[0] - at, 128), F32)
    packed_ref[...] = rows[...].astype(BF16)


def run_pack(bits, token, sums, count):
    vmem = pl.BlockSpec(memory_space=pltpu.VMEM)
    return pl.pallas_call(
        pack_kernel,
        in_specs=[pl.BlockSpec(memory_space=pltpu.SMEM), pl.BlockSpec(memory_space=pl.ANY)] + [vmem] * len(sums),
        out_specs=vmem,
        out_shape=shape_of(count, 128, dtype=BF16),
        scratch_shapes=[pltpu.VMEM((count, 128), F32)],
        cost_estimate=cost(4),
    )(bits, token, *sums)


def join_kernel(place, left_ref, right_ref, out_ref):
    n = left_ref.shape[1]
    out_ref[:, :n] = left_ref[...].astype(F32)
    part = right_ref.shape[1]
    count = out_ref.shape[0] // part
    for k in range(count):
        v = right_ref[place[pl.program_id(0) * count + k]]
        out_ref[k * part : (k + 1) * part, n:] = v.astype(F32)


def join(place, left, right):
    rows, n = left.shape
    block = 256
    return pl.pallas_call(
        join_kernel,
        grid_spec=pltpu.PrefetchScalarGridSpec(
            num_scalar_prefetch=1,
            grid=(rows // block,),
            in_specs=[pl.BlockSpec((block, n), lambda i, p: (i, 0)), pl.BlockSpec(right.shape, lambda i, p: (0, 0, 0))],
            out_specs=pl.BlockSpec((block, n + right.shape[2]), lambda i, p: (i, 0)),
        ),
        out_shape=shape_of(rows, n + right.shape[2]),
        cost_estimate=cost(5),
    )(place, left, right)


def sum_flat(grid, packed, hold, last_hold):
    held = packed.astype(F32)
    masks = [grid.core, *grid.xs, *grid.tensor]
    for mask in masks:
        if mask == masks[-1]:
            held = held + last_hold
        low = packed if mask == masks[0] else held.astype(BF16)
        held = low.astype(F32) + grid.swap(low, mask).astype(F32)
        if mask == masks[0]:
            held = held + hold
    return held.reshape(-1)


def every_part(grid, part):
    parts = part
    masks = [grid.core, *grid.xs, *grid.tensor]
    for mask in masks:
        parts = jnp.concatenate([parts, grid.swap(parts, mask)])
    devices = jnp.arange(grid.count) ^ grid.index
    place = sum(((devices // mask) % 2) << k for k, mask in enumerate(masks)).astype(jnp.int32)
    return parts.reshape(grid.count, *part.shape), place


def padded(v, size):
    return jnp.concatenate([v, jnp.zeros(-v.size % size, F32)])


def local(
    inputs, resets, cotangent, norm_gain, ema_alpha, ema_damp, ema_beta, ema_eta, ema_omega,
    w_gates, b_gates, qk_gain, q_bias, w_value, b_value, w_reset, b_reset, w_branch, ffn_gain,
    w_in, b_in, w_out, b_out,
):
    grid = Grid()
    micros, rows, width = inputs.shape
    total = micros * rows
    heads = ema_alpha.shape[1]
    rank = lax.axis_index("tensor")
    units_v, units_f = w_value.shape[1], w_in.shape[1]
    n_x = 1 << len(grid.xs)
    split_x = n_x == 2
    core, x_at = grid.bit(grid.core), lax.axis_index("dp") // 2

    half_v, half_f = units_v // 2, units_f // 2

    def chunks(w, half, axis, whole):
        size = half // n_x
        picks = range(n_x) if whole else range(1)
        return jnp.concatenate(
            [lax.dynamic_slice_in_dim(w, core * half + (x_at ^ r) * size, size, axis) for r in picks],
            axis=axis,
        )

    n_tensor = lax.axis_size("tensor")
    part_f, part_v = half_f // n_x, half_v // n_x
    own = lambda w, half, axis: chunks(w, half, axis, False)
    bias = jnp.concatenate([own(b_value, half_v, 0), own(b_reset, half_v, 0), own(b_in, half_f, 0)])
    bias = jnp.zeros((8, width), BF16).at[0, : bias.size].set(bias)
    seed = jnp.concatenate(
        [
            own(w_in, half_f, 1).T, own(w_value, half_v, 1).T, own(w_reset, half_v, 1).T, own(w_branch, half_v, 0),
            bias,
        ]
    )
    gathered = lax.all_gather(seed, AXES, axis=0)
    gathered_out = lax.all_gather(own(w_out, half_f, 0), AXES, axis=0)
    which = [
        jnp.stack([(x_at ^ r) * 2 + c for r in range(n_x)]).astype(jnp.int32) for c in (core, 1 - core)
    ]
    pieces = [Pieces(gathered, gathered_out, w, n_tensor, part_f, part_v) for w in which]
    table = gathered[:, part_f + 3 * part_v].astype(F32).reshape(2 * n_x, n_tensor, width)
    tables = [jnp.stack([lax.dynamic_index_in_dim(table, w[r], 0, False) for r in range(n_x)]) for w in which]
    bias_v = [t[..., :part_v].reshape(1, -1) for t in tables]
    bias_r = [t[..., part_v : 2 * part_v].reshape(1, -1) for t in tables]
    bias_i = [t[..., 2 * part_v : 2 * part_v + part_f].reshape(1, -1) for t in tables]
    dims = [*grid.xs[::-1], *grid.tensor[::-1]]
    still = grid.tensor

    def in_place(low, high):
        d = [grid.core, *dims]
        v = jnp.stack([low, high]).reshape(*[2] * len(d), -1)
        for axis, mask in enumerate(d):
            if mask not in still:
                v = jnp.where(grid.bit(mask) == 1, jnp.flip(v, axis), v)
        want = [*grid.tensor[::-1], grid.core, *grid.xs[::-1]]
        return v.transpose(*[d.index(m) for m in want], len(d)).reshape(-1)

    offsets = rank * rows + jnp.arange(rows)
    flags = jnp.where(offsets[None] == 0, 1, resets).astype(jnp.int32)
    sel = jnp.stack([grid.bit(m) ^ i for m in [*grid.tensor, *grid.xs] for i in (0, 1)]).astype(jnp.int32)
    places = [jnp.stack([2 * x + c for x in range(n_x)]).astype(jnp.int32) for c in (core, 1 - core)]
    flags, grid.sel, places, which = lax.optimization_barrier((flags, sel, places, which))
    for p, w in zip(pieces, which):
        p.which = w
    tile = lambda a: a.T.reshape(heads, 8, 128)
    decay = tile(1.0 - ema_alpha * ema_damp)
    feed = tile(ema_alpha * ema_beta)
    tell = tile(ema_eta)
    whole = jnp.exp(rows * jnp.log(decay))[None]
    clear = (jnp.sum(flags, axis=1) == 0).astype(F32)
    source_low = inputs.reshape(total, width)
    laid = jax.ShapeDtypeStruct((total * 8, 128), F32)
    wide = jax.ShapeDtypeStruct((total, width), F32)
    wide_low = jax.ShapeDtypeStruct((total, width), BF16)
    states = jax.ShapeDtypeStruct((micros, heads, 8, 128), F32)
    sums = jax.ShapeDtypeStruct((heads, 8, 128), F32)
    normed_laid, normed_low, final = call(
        norm_kernel, (laid, wide_low, states), [], 1,
        flags, source_low, norm_gain[None], decay, feed,
    )
    start = scan_carry(grid, final, clear, whole, False)
    blended, mixed_low = call(
        blend_kernel, (wide, wide_low), [pltpu.VMEM((total * 8, 128), F32)], 1,
        flags, normed_laid, start, decay, feed, tell, ema_omega.reshape(8, 128),
    )

    source = source_low.astype(F32)
    gate_pre = dot_plain(mixed_low, w_gates) + b_gates
    update = jax.nn.sigmoid(gate_pre[:, :width])
    direct = gate_pre[:, width : 2 * width]
    shared_pre = gate_pre[:, 2 * width :]
    shared = rounded(jax.nn.silu(shared_pre))
    query = (shared * qk_gain[0] + q_bias).astype(BF16)
    key = (shared * qk_gain[1]).astype(BF16)
    blocks = total // BLOCK
    doc = jnp.cumsum(flags.reshape(blocks, BLOCK), axis=1)
    order = jnp.arange(BLOCK)
    allowed = (doc[:, :, None] == doc[:, None, :]) & (order[:, None] >= order[None, :])[None]
    score_scale = query.shape[-1] ** (-0.5)
    query_b, key_b = query.reshape(blocks, BLOCK, -1), key.reshape(blocks, BLOCK, -1)
    scores = jnp.einsum("cik,cjk->cij", query_b, key_b, preferred_element_type=F32) * score_scale
    scores = jnp.where(allowed, scores, -1000000000.0)
    probs = jax.nn.softmax(scores, axis=-1)
    probs_low = probs.astype(BF16)

    both = Pieces(gathered, gathered_out, jnp.concatenate(which), n_tensor, part_f, part_v)
    bias_v, bias_r = jnp.concatenate(bias_v, axis=1), jnp.concatenate(bias_r, axis=1)
    *kept, branch = run_value(both, bias_v, normed_low, mixed_low, probs_low, bias_v, bias_r)
    mixed_out, ffn_low = run_middle(gate_pre, branch, source_low, ffn_gain)
    grad_low = cotangent.reshape(total, width)

    inner = [None, None]
    inner[1] = run_inner(pieces[1], bias_i[1], ffn_low, grad_low, bias_i[1])
    r_out = Reduce(grid, inner[1][2], dims, still)
    inner[0] = run_inner(pieces[0], inner[1][1], ffn_low, grad_low, bias_i[0])
    r_out.add_low(inner[0][2])
    token, gathered_out = point(grid, [], r_out, behind=gathered_out)
    for p in pieces:
        p.outer = gathered_out
    sum_in = [None, None]
    d_high, sum_in[1], feed_out, grad_ffn = run_outer(
        pieces[1], token, ffn_low, grad_low, inner[1][0], inner[1][1]
    )
    r_in = Reduce(grid, d_high, dims, still)
    token = point(grid, [sum_in[1]], r_out)
    d_low, sum_in[0], feed_out, grad_ffn = run_outer(
        pieces[0], token, ffn_low, grad_low, inner[0][0], inner[0][1], feed_out, grad_ffn
    )
    r_in.add_low(d_low)
    token = point(grid, [], r_out, r_in)
    output, grad_source, grad_gates_low, sum_ffn_gain, sum_out, sum_gates = run_middle_back(
        token, gate_pre, branch, source_low, ffn_gain, b_out, mixed_out, feed_out, grad_low, grad_ffn
    )
    bits = [*grid.xs[::-1], grid.core, *grid.tensor[::-1]]
    dims_g = [m for m in bits if m != grid.core]
    if width // (2 * n_x) % 128 == 0:
        d_gates = [None, None]
        d_gates[1] = run_gates(places[1], sum_gates, mixed_low, grad_gates_low)
        r_gates = Reduce(grid, d_gates[1], dims_g, dims_g)
        d_gates[0] = run_gates(places[0], d_gates[1], mixed_low, grad_gates_low)
        r_gates.add_low(d_gates[0])
        token = d_gates[0]
    else:
        c_axis = bits.index(grid.core)
        d_gates = [
            dot_over_rows(mixed_low, side).astype(BF16).reshape(*[2] * len(bits), -1, width)
            for side in (grad_gates_low[:, :width], grad_gates_low[:, width:])
        ]
        half_of = lambda i: jnp.stack(
            [lax.dynamic_index_in_dim(d, i, c_axis, False).reshape(1, width // 2, width) for d in d_gates]
        )
        r_gates = Reduce(grid, half_of(1 - core), dims_g, dims_g)
        r_gates.add_low(half_of(core))
        token = sum_gates

    def run_vb(k, token):
        return run_value_back(
            pieces[k], k, 200 if k == 0 else 1, token, grad_gates_low, normed_low, mixed_low, probs_low, kept
        )

    back = [None, None]
    back[1] = run_vb(1, token)
    r_v = Reduce(grid, back[1][0], dims, still)
    token = point(grid, [back[1][1], *r_out.raw], r_in, r_gates)
    back[0] = run_vb(0, token)
    r_v.add_low(back[0][0])
    token = point(grid, [back[0][1]], r_v, r_gates, r_in)
    grad_laid, left, grad_shared_low, sums_shared = run_shared(
        token, flags, back[0][5], back[1][5], probs, query, key, shared, shared_pre, qk_gain, grad_gates_low, w_gates,
        back[0][3], back[1][3], blended, decay, tell,
    )
    token = point(grid, [left, *r_in.raw], r_gates)
    left = left + token[0, 0]
    d_shared = dot_over_rows(mixed_low, grad_shared_low + token[0, 0].astype(BF16))
    d_shared = d_shared.reshape(*[2] * len(bits), -1, d_shared.shape[-1])

    def fold(v, mask):
        axis, here = bits.index(mask), grid.bit(mask)
        got = grid.swap(lax.dynamic_slice_in_dim(v, 1 - here, 1, axis).astype(BF16), mask)
        return lax.dynamic_slice_in_dim(v, here, 1, axis) + got.astype(F32)

    right = scan_carry(grid, left, clear, whole, True)
    t_first, *t_rest = grid.tensor
    for mask in [grid.core, *grid.xs, t_first]:
        d_shared = fold(d_shared, mask)
    token = point(grid, [right], r_v, r_gates, r_in, r_out)
    d_shared = fold(d_shared + token[0, 0], t_rest[0])
    column = shape_of(8, 128)
    results = []
    for m in range(micros):
        part = slice(m * rows, (m + 1) * rows)
        laid_part = slice(m * rows * 8, (m + 1) * rows * 8)
        results.append(
            run_back(
                m, token, flags, normed_laid, grad_laid, start, right, decay, feed, tell, ema_omega.reshape(8, 128),
                back[0][4], back[1][4], source_low, grad_source, norm_gain[None],
            )
        )
        if m == 0:
            token, *done = ends(point(grid, [results[0][1]], r_gates, r_in, r_out, r_v))
            d_shared = d_shared + token[0, 0]
            for mask in t_rest[1:]:
                d_shared = fold(d_shared, mask)
    done_gates = finish(grid, [token], r_gates, *done[:1])
    done_in = finish(grid, [token], r_in, *done[1:2])
    done_out = finish(grid, [token], r_out, *done[2:])
    token_v = point(grid, [results[-1][1]], r_v)
    token_w, *done_v = ends(point(grid, [token_v], r_v))
    done_v = finish(grid, [token_w], r_v, *done_v)
    grad_w_out, grad_w_in = share_and_place(grid, [done_out, done_in], [(False,), (True,)], None)
    grad_w_out, grad_w_in = grad_w_out[0], grad_w_in[0]
    grad_w_gates = lax.all_gather(
        done_gates.reshape(width // grid.count, 2 * width), AXES, axis=0, tiled=True
    )

    z = token_v[0, 0]
    part = d_shared.reshape(width // grid.count, -1) + token_w[0, 0]
    sizes_late = [heads * width] * 3 + [width, width]
    sizes_early = [2 * width + 128, 256, 128, width, width, units_v * n_tensor, units_v * n_tensor, units_f * n_tensor]
    count = -(-sum(sizes_late + sizes_early) // 2048) * 16
    if (part_v, part_f, n_x) == (64, 128, 2):
        by_kind = [r[k] for k in range(1, 4) for r in results]
        packed = run_pack(
            jnp.stack([core, x_at]).astype(jnp.int32), token_v,
            [
                *by_kind, *[r[4] for r in results], *[r[5] for r in results], sum_gates, sums_shared, sum_ffn_gain, sum_out,
                back[0][2], back[1][2], back[0][1], back[1][1], *sum_in,
            ],
            count,
        )
    else:
        spread_in = lambda k: in_place(back[0][k] + z, back[1][k] + z)
        both = [sum(r[k] + z for r in results) for k in range(1, 6)]
        small = [
            *[v.reshape(-1) for v in both[:3]], jnp.sum(both[4], axis=0), both[3].reshape(-1), jnp.sum(sum_gates + z, axis=0),
            sums_shared[3] + z, sums_shared[:2].reshape(-1) + z, sums_shared[2] + z, jnp.sum(sum_ffn_gain + z, axis=0),
            jnp.sum(sum_out + z, axis=0), spread_in(2), spread_in(1), in_place(sum_in[0] + z, sum_in[1] + z),
        ]
        packed = padded(jnp.concatenate(small), count * 128).reshape(-1, 128).astype(BF16)

    def cut_like(v, sizes):
        out, first = [], 0
        for n in sizes:
            out.append(v[first : first + n])
            first += n
        return out

    ((grad_w_branch, grad_w_reset, grad_w_value, *placed),) = share_and_place(grid, [done_v], [(False, True, True)], None)
    summed = sum_flat(grid, packed, token_w[0, 0], placed[0][0, 0] if placed else 0.0)
    parts, place = every_part(grid, part.astype(BF16))
    grad_w_gates = join(place, grad_w_gates, parts)
    last, cut = cut_like(summed, sizes_late), cut_like(summed[sum(sizes_late) :], sizes_early)
    untile = lambda v: v.reshape(heads, width).T
    eta, one, two = (untile(v) for v in last[:3])
    mine = lambda v, n: lax.dynamic_slice_in_dim(v, rank * n, n, 0)
    return (
        output.reshape(inputs.shape),
        jnp.stack([r[0] + z for r in results]),
        last[3],
        ema_beta * one - ema_damp * two,
        -ema_alpha * two,
        ema_alpha * one,
        eta,
        last[4],
        grad_w_gates,
        cut[0],
        cut[1].reshape(2, -1),
        cut[2],
        grad_w_value,
        mine(cut[5], units_v),
        grad_w_reset,
        mine(cut[6], units_v),
        grad_w_branch,
        cut[3],
        grad_w_in,
        mine(cut[7], units_f),
        grad_w_out,
        cut[4],
    )


def solution(mesh):
    rows = P(None, AXES, None)
    col, row, vec, rep = P(None, "tensor"), P("tensor", None), P("tensor"), P()
    return jax.shard_map(
        local,
        mesh=mesh,
        in_specs=(
            rows, P(None, AXES), rows, rep, rep, rep, rep, rep, rep, rep, rep, rep, rep,
            col, vec, col, vec, row, rep, col, vec, row, rep,
        ),
        out_specs=(
            rows, rows, rep, rep, rep, rep, rep, rep, rep, rep, rep, rep,
            col, vec, col, vec, row, rep, col, vec, row, rep,
        ),
        check_vma=False,
    )
```

```python
from functools import partial

import jax
import jax.numpy as jnp
from jax import lax
from jax.experimental import pallas as pl
from jax.experimental.pallas import tpu as pltpu
from jax.sharding import PartitionSpec as P

BLOCK = 128
HIGHEST = lax.Precision.HIGHEST
EPSILON = 1e-06
AXES = ("dp", "tensor")
F32 = jnp.float32
BF16 = jnp.bfloat16


def dot_plain(a, b):
    return jnp.dot(a, b, preferred_element_type=F32)


def dot_against(a, b):
    return lax.dot_general(a, b, (((1,), (1,)), ((), ())), preferred_element_type=F32)


def dot_over_rows(a, b):
    return lax.dot_general(a, b, (((0,), (0,)), ((), ())), preferred_element_type=F32)


def rounded(v):
    return lax.reduce_precision(v, exponent_bits=8, mantissa_bits=7)


def silu_slope(v):
    s = jax.nn.sigmoid(v)
    return s * (1.0 + v * (1.0 - s))


class Grid:
    def __init__(self):
        dp, tensor = lax.axis_size("dp"), lax.axis_size("tensor")
        self.count = dp * tensor
        self.index = lax.axis_index("dp") * tensor + lax.axis_index("tensor")
        masks = lambda n, first: [first << k for k in range(n.bit_length() - 1)]
        self.tensor = masks(tensor, 1)
        self.core, *self.xs = masks(dp, tensor)

    def bit(self, mask):
        return (self.index // mask) % 2

    def swap(self, value, mask):
        return lax.ppermute(value, AXES, [(i, i ^ mask) for i in range(self.count)])


def ema_step(state, row, keep, decay, feed):
    return [(s * keep) * q + f * row for s, q, f in zip(state, decay, feed)]


def row_of(ref, base, r):
    return ref[pl.ds(base + r, 8, stride=8), :]


def spread(ref, block, values):
    for j in range(8):
        ref[pl.ds(pl.multiple_of(block * 64, 64) + 8 * j, 8), :] = values[:, j * 128 : (j + 1) * 128]


def collect(ref, block):
    return jnp.concatenate(
        [ref[pl.ds(pl.multiple_of(block * 64, 64) + 8 * j, 8), :] for j in range(8)], axis=1
    )


def norm_kernel(flags, x_ref, gain_ref, decay_ref, feed_ref, normed_ref, low_ref, final_ref):
    micros, rows = flags.shape
    heads = decay_ref.shape[0]

    def norm_block(b, carry):
        at = pl.ds(pl.multiple_of(b * 16, 16), 16)
        x = x_ref[at, :].astype(F32)
        n = x * lax.rsqrt(jnp.mean(x * x, axis=-1, keepdims=True) + EPSILON) * gain_ref[...]
        low_ref[at, :] = n.astype(BF16)
        spread(normed_ref, 2 * b, n[:8])
        spread(normed_ref, 2 * b + 1, n[8:])
        return carry

    lax.fori_loop(0, micros * rows // 16, norm_block, 0)
    for m in range(micros):
        for h0 in range(0, heads, 8):
            decay = [decay_ref[h0 + h] for h in range(8)]
            feed = [feed_ref[h0 + h] for h in range(8)]

            def block(b, state, m=m, decay=decay, feed=feed):
                base = pl.multiple_of((m * (rows // 8) + b) * 64, 64)
                for r in range(8):
                    keep = (1 - flags[m, b * 8 + r]).astype(F32)
                    state = ema_step(state, row_of(normed_ref, base, r), keep, decay, feed)
                return state

            state = lax.fori_loop(0, rows // 8, block, [jnp.zeros((8, 128), F32)] * 8)
            for h in range(8):
                final_ref[m, h0 + h] = state[h]


def blend_kernel(
    flags, normed_ref, start_ref, decay_ref, feed_ref, out_ref, omega_ref, blended_ref, low_ref, acc_ref
):
    micros, rows = flags.shape
    heads = decay_ref.shape[0]
    omega = omega_ref[...]
    for m in range(micros):
        for h0 in range(0, heads, 8):
            decay = [decay_ref[h0 + h] for h in range(8)]
            feed = [feed_ref[h0 + h] for h in range(8)]
            tell = [out_ref[h0 + h] for h in range(8)]

            def block(b, state, m=m, h0=h0, decay=decay, feed=feed, tell=tell):
                base = pl.multiple_of((m * (rows // 8) + b) * 64, 64)
                for r in range(8):
                    keep = (1 - flags[m, b * 8 + r]).astype(F32)
                    row = row_of(normed_ref, base, r)
                    state = ema_step(state, row, keep, decay, feed)
                    told = [s * t for s, t in zip(state, tell)]
                    while len(told) > 1:
                        told = [told[i] + told[i + 1] for i in range(0, len(told), 2)]
                    at = pl.ds(base + r, 8, stride=8)
                    if h0 == 0:
                        acc_ref[at, :] = told[0] + omega * row
                    else:
                        acc_ref[at, :] = acc_ref[at, :] + told[0]
                return state

            lax.fori_loop(0, rows // 8, block, [start_ref[m, h0 + h] for h in range(8)])

    def finish(b, carry):
        at = pl.ds(pl.multiple_of(b * 16, 16), 16)
        v = jnp.concatenate([collect(acc_ref, 2 * b), collect(acc_ref, 2 * b + 1)], axis=0)
        blended_ref[at, :] = v
        low_ref[at, :] = (v / (1.0 + jnp.exp(-v))).astype(BF16)
        return carry

    lax.fori_loop(0, micros * rows // 16, finish, 0)


def shared_kernel(
    before, flags, gp0_ref, gp1_ref, probs_ref, query_ref, key_ref, shared_ref, pre_ref, gain_ref, gates_ref, weight_ref,
    mix0_ref, mix1_ref, blended_ref, decay_ref, tell_ref,
    rows_ref, left_ref, low_ref, sums_ref,
):
    b = pl.program_id(0)
    width = mix0_ref.shape[-1]
    probs = probs_ref[0]
    grad_probs = gp0_ref[0] + gp1_ref[0]
    scale = query_ref.shape[-1] ** (-0.5)
    grad_scores = probs * (grad_probs - jnp.sum(grad_probs * probs, axis=-1, keepdims=True)) * scale
    exact = partial(lax.dot_general, precision=HIGHEST, preferred_element_type=F32)
    grad_query = exact(grad_scores, key_ref[...].astype(F32), (((1,), (0,)), ((), ())))
    grad_key = exact(grad_scores, query_ref[...].astype(F32), (((0,), (0,)), ((), ())))
    shared = shared_ref[...]
    pre = pre_ref[...]
    grad_pre = (grad_query * gain_ref[0:1] + grad_key * gain_ref[1:2]) * slope(pre, sigmoid(pre))
    low = grad_pre.astype(BF16)
    low_ref[...] = low
    total = lambda v: jnp.sum(v, axis=0, keepdims=True)
    part = jnp.concatenate(
        [
            total(grad_query * shared), total(grad_key * shared), total(grad_query), total(low.astype(F32)),
            jnp.zeros((4, low.shape[-1]), F32),
        ]
    )
    add_to(sums_ref, part)
    mixed = (
        mix0_ref[...]
        + mix1_ref[...]
        + dot_nt(gates_ref[...], weight_ref[:, : 2 * width])
        + dot_nt(low, weight_ref[:, 2 * width :])
    )
    v = blended_ref[...]
    grad = mixed * slope(v, sigmoid(v))
    for i in range(BLOCK // 8):
        spread(rows_ref, b * (BLOCK // 8) + i, grad[8 * i : 8 * i + 8])

    @pl.when(b == pl.num_programs(0) - 1)
    def _():
        micros, rows = flags.shape
        heads = decay_ref.shape[0]
        for m in range(micros):
            for h0 in range(0, heads, 8):
                decay = [decay_ref[h0 + h] for h in range(8)]
                tell = [tell_ref[h0 + h] for h in range(8)]

                def block(i, left, m=m, decay=decay, tell=tell):
                    b = rows // 8 - 1 - i
                    base = pl.multiple_of((m * (rows // 8) + b) * 64, 64)
                    for r in reversed(range(8)):
                        keep = (1 - flags[m, b * 8 + r]).astype(F32)
                        row = row_of(rows_ref, base, r)
                        left = [((t * row + k) * keep) * q for k, q, t in zip(left, decay, tell)]
                    return left

                left = lax.fori_loop(0, rows // 8, block, [jnp.zeros((8, 128), F32)] * 8)
                for h in range(8):
                    left_ref[m, h0 + h] = left[h]


def run_shared(token, flags, gp0, gp1, probs, query, key, shared, pre, gain, gates, weight, mix0, mix1, blended, decay, tell):
    total, width = mix0.shape
    z = query.shape[1]
    rows = lambda n: pl.BlockSpec((BLOCK, n), lambda b: (b, 0))
    pair = pl.BlockSpec((1, BLOCK, BLOCK), lambda b: (b, 0, 0))
    whole = lambda a: pl.BlockSpec(a.shape, lambda b: (0,) * a.ndim)
    micros, heads = flags.shape[0], decay.shape[0]
    return pl.pallas_call(
        shared_kernel,
        grid=(total // BLOCK,),
        in_specs=[
            pl.BlockSpec(memory_space=pl.ANY), pl.BlockSpec(memory_space=pltpu.SMEM), pair, pair, pair, rows(z), rows(z), rows(z), rows(z), whole(gain),
            rows(2 * width), whole(weight), rows(width), rows(width), rows(width), whole(decay), whole(tell),
        ],
        out_specs=[
            pl.BlockSpec((total * 8, 128), lambda b: (0, 0)),
            pl.BlockSpec((micros, heads, 8, 128), lambda b: (0, 0, 0, 0)),
            rows(z),
            pl.BlockSpec((8, z), lambda b: (0, 0)),
        ],
        out_shape=[
            shape_of(total * 8, 128), shape_of(micros, heads, 8, 128), shape_of(total, z, dtype=BF16), shape_of(8, z),
        ],
        cost_estimate=cost(200),
    )(token, flags, gp0, gp1, probs, query, key, shared, pre, gain, gates, weight, mix0, mix1, blended, decay, tell)


def back_kernel(
    m, before, flags, normed_ref, rows_ref, start_ref, right_ref, decay_ref, feed_ref, tell_ref, omega_ref,
    add0_ref, add1_ref, source_ref, base_ref, gain_ref,
    grad_ref, eta_ref, one_ref, two_ref, omega_out, gain_out, token_ref, states, acc_ref,
):
    rows = flags.shape[1]
    heads = decay_ref.shape[0]
    group = 4
    omega = omega_ref[...]
    zero = jnp.zeros((8, 128), F32)
    token_ref[...] = zero
    for h0 in range(0, heads, group):
        decay = [decay_ref[h0 + h] for h in range(group)]
        feed = [feed_ref[h0 + h] for h in range(group)]
        tell = [tell_ref[h0 + h] for h in range(group)]

        def ahead(b, state, decay=decay, feed=feed):
            base = pl.multiple_of(b * 64, 64)
            for r in range(8):
                keep = (1 - flags[m, b * 8 + r]).astype(F32)
                for h in range(group):
                    states[b * 8 + r, h] = state[h]
                state = ema_step(state, row_of(normed_ref, base, r), keep, decay, feed)
            return state

        last = lax.fori_loop(0, rows // 8, ahead, [start_ref[0, h0 + h] for h in range(group)])

        def back(i, carry, h0=h0, decay=decay, feed=feed, tell=tell):
            left, after_state, eta, one, two, with_omega = carry
            b = rows // 8 - 1 - i
            base = pl.multiple_of(b * 64, 64)
            for r in reversed(range(8)):
                keep = (1 - flags[m, b * 8 + r]).astype(F32)
                g = row_of(rows_ref, base, r)
                x = row_of(normed_ref, base, r)
                earlier = [states[b * 8 + r, h] for h in range(group)]
                eta = [e + s * g for e, s in zip(eta, after_state)]
                now = [t * g + k for t, k in zip(tell, left)]
                one = [o + n * x for o, n in zip(one, now)]
                kept = [n * keep for n in now]
                two = [w + k * s for w, k, s in zip(two, kept, earlier)]
                left = [k * q for k, q in zip(kept, decay)]
                gn = [n * f for n, f in zip(now, feed)]
                while len(gn) > 1:
                    gn = [gn[i] + gn[i + 1] for i in range(0, len(gn), 2)]
                at = pl.ds(base + r, 8, stride=8)
                if h0 == 0:
                    acc_ref[at, :] = gn[0] + omega * g
                    with_omega = with_omega + g * x
                else:
                    acc_ref[at, :] = acc_ref[at, :] + gn[0]
                after_state = earlier
            return left, after_state, eta, one, two, with_omega

        right = [right_ref[0, h0 + h] for h in range(group)]
        nothing = [zero] * group
        _, _, eta, one, two, with_omega = lax.fori_loop(
            0, rows // 8, back, (right, last, nothing, nothing, nothing, zero)
        )
        if h0 == 0:
            omega_out[...] = with_omega
        for h in range(group):
            eta_ref[h0 + h] = eta[h]
            one_ref[h0 + h] = one[h]
            two_ref[h0 + h] = two[h]

    def finish(b, gained):
        at = pl.ds(pl.multiple_of(b * 16, 16), 16)
        x = source_ref[at, :].astype(F32)
        scale = lax.rsqrt(jnp.mean(x * x, axis=-1, keepdims=True) + EPSILON)
        scaled = x * scale
        grad = jnp.concatenate([collect(acc_ref, 2 * b), collect(acc_ref, 2 * b + 1)], axis=0)
        grad = grad + add0_ref[at, :] + add1_ref[at, :]
        own = grad * scaled
        gained = gained + own[:8] + own[8:]
        inner = grad * gain_ref[...]
        mean = jnp.mean(inner * scaled, axis=-1, keepdims=True)
        grad_ref[at, :] = base_ref[at, :] + scale * (inner - scaled * mean)
        return gained

    width = source_ref.shape[-1]
    gain_out[...] = lax.fori_loop(0, rows // 16, finish, jnp.zeros((8, width), F32))


def run_back(m, token, flags, laid, grads, start, right, decay, feed, tell, omega, add0, add1, source, base, gain):
    rows, heads = flags.shape[1], decay.shape[0]
    width = source.shape[1]
    whole = lambda a: pl.BlockSpec(a.shape, lambda i: (0,) * a.ndim)
    tall = pl.BlockSpec((rows * 8, 128), lambda i: (m, 0))
    carry = pl.BlockSpec((1, heads, 8, 128), lambda i: (m, 0, 0, 0))
    wide = pl.BlockSpec((rows, width), lambda i: (m, 0))
    sums = pl.BlockSpec((heads, 8, 128), lambda i: (0, 0, 0))
    return pl.pallas_call(
        partial(back_kernel, m),
        grid=(1,),
        in_specs=[
            pl.BlockSpec(memory_space=pl.ANY), pl.BlockSpec(memory_space=pltpu.SMEM), tall, tall, carry, carry,
            whole(decay), whole(feed), whole(tell), whole(omega), wide, wide, wide, wide, whole(gain),
        ],
        out_specs=[
            pl.BlockSpec((rows, width), lambda i: (0, 0)), sums, sums, sums,
            pl.BlockSpec((8, 128), lambda i: (0, 0)), pl.BlockSpec((8, width), lambda i: (0, 0)),
            pl.BlockSpec((8, 128), lambda i: (0, 0)),
        ],
        out_shape=[
            jax.ShapeDtypeStruct((rows, width), F32),
            *[jax.ShapeDtypeStruct((heads, 8, 128), F32)] * 3,
            jax.ShapeDtypeStruct((8, 128), F32),
            jax.ShapeDtypeStruct((8, width), F32),
            jax.ShapeDtypeStruct((8, 128), F32),
        ],
        scratch_shapes=[pltpu.VMEM((rows, 4, 8, 128), F32), pltpu.VMEM((rows * 8, 128), F32)],
        cost_estimate=cost(200),
    )(token, flags, laid, grads, start, right, decay, feed, tell, omega, add0, add1, source, base, gain)


def dot_tn(a, b):
    return lax.dot_general(a, b, (((0,), (0,)), ((), ())), preferred_element_type=F32)


def dot_nt(a, b):
    return lax.dot_general(a, b, (((1,), (1,)), ((), ())), preferred_element_type=F32)


def dot_nn(a, b):
    return lax.dot_general(a, b, (((1,), (0,)), ((), ())), preferred_element_type=F32)


def sigmoid(v):
    return 1.0 / (1.0 + jnp.exp(-v))


def slope(v, s):
    return s * (1.0 + v * (1.0 - s))


def add_to(ref, value, first_ref=None):
    first = pl.program_id(0) == 0

    @pl.when(first)
    def _():
        ref[...] = value if first_ref is None else first_ref[...] + value

    @pl.when(jnp.logical_not(first))
    def _():
        ref[...] = ref[...] + value


def put_sides(ref, lead, v):
    half = v.shape[-1] // 2
    v = v.astype(BF16)
    ref[0, lead] = v[:, :half]
    ref[1, lead] = v[:, half:]


def value_kernel(
    piece, normed_ref, mixed_ref, probs_ref, wv_ref, wr_ref, wb_ref, bv_ref, br_ref,
    value_ref, reset_ref, attended_ref, gated_ref, out_ref,
):
    value_pre = dot_nt(normed_ref[...], flat(wv_ref)) + bv_ref[...]
    value_ref[...] = value_pre
    value = (value_pre * sigmoid(value_pre)).astype(BF16)
    blocks = probs_ref.shape[0]
    attended = jnp.concatenate(
        [dot_nn(probs_ref[b], value[b * BLOCK : (b + 1) * BLOCK]) for b in range(blocks)], axis=0
    )
    attended_ref[...] = attended
    reset_pre = dot_nt(mixed_ref[...], flat(wr_ref)) + br_ref[...]
    reset_ref[...] = reset_pre
    gated = (reset_pre * sigmoid(reset_pre) * attended).astype(BF16)
    gated_ref[...] = gated
    add_to(out_ref, dot_nn(gated, flat(wb_ref)))


def value_back_kernel(
    piece, grad_ref, normed_ref, mixed_ref, probs_ref, wv_ref, wr_ref, wb_ref,
    value_ref, reset_ref, attended_ref, gated_ref,
    d_ref, sum_r_ref, sum_v_ref, mixed_out, normed_out, probs_out,
):
    grad = grad_ref[...]
    grad_gated = dot_nt(grad, flat(wb_ref))
    put_sides(d_ref, 0, dot_tn(gated_ref[...], grad))
    reset_pre = reset_ref[...]
    s = sigmoid(reset_pre)
    grad_attended = (grad_gated * (reset_pre * s)).astype(BF16)
    grad_reset = (grad_gated * attended_ref[...] * slope(reset_pre, s)).astype(BF16)
    sum_r_ref[...] = jnp.sum(grad_reset.astype(F32), axis=0, keepdims=True)
    mixed = mixed_ref[...]
    put_sides(d_ref, 1, dot_tn(grad_reset, mixed))
    add_to(mixed_out, dot_nn(grad_reset, flat(wr_ref)))
    value_pre = value_ref[...]
    s = sigmoid(value_pre)
    value = (value_pre * s).astype(BF16)
    blocks = probs_ref.shape[0]
    grad_value, grad_probs = [], []
    for b in range(blocks):
        rows = slice(b * BLOCK, (b + 1) * BLOCK)
        grad_probs.append(dot_nt(grad_attended[rows], value[rows])[None])
        grad_value.append(dot_tn(probs_ref[b], grad_attended[rows]))
    add_to(probs_out, jnp.concatenate(grad_probs, axis=0))
    grad_value = (jnp.concatenate(grad_value, axis=0) * slope(value_pre, s)).astype(BF16)
    sum_v_ref[...] = jnp.sum(grad_value.astype(F32), axis=0, keepdims=True)
    put_sides(d_ref, 2, dot_tn(grad_value, normed_ref[...]))
    add_to(normed_out, dot_nn(grad_value, flat(wv_ref)))


def inner_kernel(piece, ffn_ref, grad_ref, wi_ref, bi_ref, pre_ref, activ_ref, do_ref):
    wi = flat(wi_ref)
    pre = dot_nt(ffn_ref[...], wi) + bi_ref[...]
    pre_ref[...] = pre
    activ = (pre * sigmoid(pre)).astype(BF16)
    activ_ref[...] = activ
    put_sides(do_ref, 0, dot_tn(activ, grad_ref[...]))


def outer_kernel(
    piece, ffn_ref, grad_ref, wi_ref, wo_ref, pre_ref, activ_ref, *rest
):
    *sums, di_ref, sum_i_ref, out_ref, ffn_out = rest
    sum_o_ref, sum_f_ref = sums if sums else (None, None)
    wi = flat(wi_ref)
    wo = flat(wo_ref)
    add_to(out_ref, dot_nn(activ_ref[...], wo), sum_o_ref)
    pre = pre_ref[...]
    grad = (dot_nt(grad_ref[...], wo) * slope(pre, sigmoid(pre))).astype(BF16)
    sum_i_ref[...] = jnp.sum(grad.astype(F32), axis=0, keepdims=True)
    put_sides(di_ref, 0, dot_tn(grad, ffn_ref[...]))
    add_to(ffn_out, dot_nn(grad, wi), sum_f_ref)


UNITS = 1024


def cost(micros):
    return pl.CostEstimate(flops=int(micros * SCALE * 1.15e9), bytes_accessed=int(micros * SCALE * 3.3e6), transcendentals=0)


SCALE = 1.0


def shape_of(*dims, dtype=F32):
    return jax.ShapeDtypeStruct(dims, dtype)


def middle(gate_ref, branch_ref, source_ref):
    width = source_ref.shape[-1]
    update = sigmoid(gate_ref[:, :width])
    pre = gate_ref[:, width : 2 * width] + branch_ref[...]
    s = sigmoid(pre)
    return source_ref[...].astype(F32), update, pre, s


def middle_kernel(gate_ref, branch_ref, source_ref, gain_ref, mixed_ref, ffn_ref):
    source, update, pre, s = middle(gate_ref, branch_ref, source_ref)
    mixed = update * (pre * s) + (1.0 - update) * source
    mixed_ref[...] = mixed
    scale = lax.rsqrt(jnp.mean(mixed * mixed, axis=-1, keepdims=True) + EPSILON)
    ffn_ref[...] = (mixed * scale * gain_ref[...]).astype(BF16)


def column_sums(v):
    return jnp.sum(v.reshape(-1, 8, v.shape[-1]), axis=0)


def middle_back_kernel(
    before, gate_ref, branch_ref, source_ref, gain_ref, bias_ref, mixed_ref, feed_ref, grad_ref, ffn_ref,
    out_ref, base_ref, gates_ref, sum_gain_ref, sum_out_ref, sum_gates_ref,
):
    width = source_ref.shape[-1]
    source, update, pre, s = middle(gate_ref, branch_ref, source_ref)
    mixed = mixed_ref[...]
    out_ref[...] = (mixed + feed_ref[...] + bias_ref[...]).astype(BF16)
    scale = lax.rsqrt(jnp.mean(mixed * mixed, axis=-1, keepdims=True) + EPSILON)
    scaled = mixed * scale
    grad_out = grad_ref[...].astype(F32)
    grad_ffn = ffn_ref[...]
    add_to(sum_out_ref, column_sums(grad_out))
    add_to(sum_gain_ref, column_sums(grad_ffn * scaled))
    gained = grad_ffn * gain_ref[...]
    grad = grad_out + scale * (gained - scaled * jnp.mean(gained * scaled, axis=-1, keepdims=True))
    base_ref[...] = grad * (1.0 - update)
    grad_update = (grad * (pre * s - source) * update * (1.0 - update)).astype(BF16)
    grad_hidden = (grad * update * slope(pre, s)).astype(BF16)
    gates_ref[:, :width] = grad_update
    gates_ref[:, width:] = grad_hidden
    add_to(
        sum_gates_ref,
        jnp.concatenate([column_sums(grad_update.astype(F32)), column_sums(grad_hidden.astype(F32))], axis=1),
    )


def run_middle(gate, branch, source, gain):
    total, width = source.shape
    rows = lambda n: pl.BlockSpec((BLOCK, n), lambda i: (i, 0))
    line = pl.BlockSpec((1, width), lambda i: (0, 0))
    return pl.pallas_call(
        middle_kernel,
        grid=(total // BLOCK,),
        in_specs=[rows(gate.shape[1]), rows(width), rows(width), line],
        out_specs=[rows(width), rows(width)],
        out_shape=[shape_of(total, width), shape_of(total, width, dtype=BF16)],
        cost_estimate=cost(5),
    )(gate, branch, source, gain[None])


def run_middle_back(token, gate, branch, source, gain, bias, mixed, feed, grad, ffn):
    total, width = source.shape
    rows = lambda n: pl.BlockSpec((BLOCK, n), lambda i: (i, 0))
    line = pl.BlockSpec((1, width), lambda i: (0, 0))
    few = lambda n: pl.BlockSpec((8, n), lambda i: (0, 0))
    wide = rows(width)
    return pl.pallas_call(
        middle_back_kernel,
        grid=(total // BLOCK,),
        in_specs=[
            pl.BlockSpec(memory_space=pl.ANY), rows(gate.shape[1]), wide, wide, line, line, wide, wide, wide, wide
        ],
        out_specs=[wide, wide, rows(2 * width), few(width), few(width), few(2 * width)],
        out_shape=[
            shape_of(total, width, dtype=BF16), shape_of(total, width), shape_of(total, 2 * width, dtype=BF16),
            shape_of(8, width), shape_of(8, width), shape_of(8, 2 * width),
        ],
        cost_estimate=cost(1),
    )(token, gate, branch, source, gain[None], bias[None], mixed, feed, grad, ffn)


def gates_kernel(piece, before, mixed_ref, gates_ref, d_ref):
    grad = dot_tn(mixed_ref[...], gates_ref[...]).astype(BF16)
    half = grad.shape[-1] // 2
    d_ref[0] = grad[:, :half].reshape(d_ref.shape[1:])
    d_ref[1] = grad[:, half:].reshape(d_ref.shape[1:])


def run_gates(which, token, mixed, gates):
    total, width = mixed.shape
    n = which.shape[0]
    block = width // (2 * n)
    return pl.pallas_call(
        gates_kernel,
        grid_spec=pltpu.PrefetchScalarGridSpec(
            num_scalar_prefetch=1,
            grid=(n,),
            in_specs=[
                pl.BlockSpec(memory_space=pl.ANY),
                pl.BlockSpec((total, block), lambda i, p: (0, p[i])),
                pl.BlockSpec(gates.shape, lambda i, p: (0, 0)),
            ],
            out_specs=pl.BlockSpec((2, 1, block, width), lambda i, p: (0, 0, i, 0)),
        ),
        out_shape=shape_of(2, 1, n * block, width, dtype=BF16),
        cost_estimate=cost(1),
    )(which, token, mixed, gates)


class Pieces:
    def __init__(self, gathered, outer, which, tensor, part_f, part_v):
        self.gathered, self.outer, self.which, self.tensor = gathered, outer, which, tensor
        self.part_f, self.part_v = part_f, part_v
        self.width = gathered.shape[-1]

    def units(self, part):
        return self.which.shape[0] * self.tensor * part

    def block(self, part):
        return min(UNITS, self.tensor * part)

    def spec(self, part, row):
        step = self.block(part) // part
        per = self.tensor // step
        return pl.BlockSpec(
            (step, part, self.width), lambda i, p: (p[i // per] * per + i % per, row // part, 0)
        )

    @property
    def w_in(self):
        return self.spec(self.part_f, 0)

    @property
    def w_out(self):
        return self.spec(self.part_f, 0)

    def v(self, k):
        return self.spec(self.part_v, self.part_f + k * self.part_v)


def flat(ref):
    return ref[...].reshape(-1, ref.shape[-1])


def blocked(kernel, micros, pieces, steps, token, in_specs, out_specs, out_shape, *arrays):
    def body(piece, before, *refs):
        kernel(piece, *refs)

    return pl.pallas_call(
        body,
        grid_spec=pltpu.PrefetchScalarGridSpec(
            num_scalar_prefetch=1,
            grid=(steps,),
            in_specs=[pl.BlockSpec(memory_space=pl.ANY), *in_specs],
            out_specs=out_specs,
        ),
        out_shape=out_shape,
        cost_estimate=cost(micros),
    )(pieces.which, token, *arrays)


def block_specs(total, width, block, lead):
    full = pl.BlockSpec((total, width), lambda i, p: (0, 0))
    cols = pl.BlockSpec((total, block), lambda i, p: (0, i))
    line = pl.BlockSpec((1, block), lambda i, p: (0, i))
    grads = pl.BlockSpec((2, lead, block, width // 2), lambda i, p: (0, 0, i, 0))
    return full, cols, line, grads


def run_value(pieces, token, normed, mixed, probs, bv, br):
    total, width = normed.shape
    units, block = pieces.units(pieces.part_v), pieces.block(pieces.part_v)
    full, cols, line, grads = block_specs(total, width, block, 3)
    pairs = pl.BlockSpec(probs.shape, lambda i, p: (0, 0, 0))
    g = pieces.gathered
    return blocked(
        value_kernel, 200, pieces, units // block, token,
        [full, full, pairs, pieces.v(0), pieces.v(1), pieces.v(2), line, line],
        [cols, cols, cols, cols, full],
        [shape_of(total, units)] * 3 + [shape_of(total, units, dtype=BF16), shape_of(total, width)],
        normed, mixed, probs, g, g, g, bv, br,
    )


def run_value_back(pieces, k, micros, token, grad, normed, mixed, probs, kept):
    total, width = normed.shape
    units, block = pieces.units(pieces.part_v), pieces.block(pieces.part_v)
    full, cols, line, grads = block_specs(total, width, block, 3)
    pairs = pl.BlockSpec(probs.shape, lambda i, p: (0, 0, 0))
    g = pieces.gathered
    return blocked(
        value_back_kernel, micros, pieces, units // block, token,
        [
            pl.BlockSpec((total, width), lambda i, p: (0, 1)), full, full, pairs,
            pieces.v(0), pieces.v(1), pieces.v(2), *[pl.BlockSpec((total, block), lambda i, p: (0, k * (units // block) + i))] * 4,
        ],
        [grads, line, line, full, full, pairs],
        [shape_of(2, 3, units, width // 2, dtype=BF16)]
        + [shape_of(1, units)] * 2
        + [shape_of(total, width)] * 2
        + [shape_of(*probs.shape)],
        grad, normed, mixed, probs, g, g, g, *kept,
    )


def run_inner(pieces, token, ffn, grad, bias):
    total, width = ffn.shape
    units, block = pieces.units(pieces.part_f), pieces.block(pieces.part_f)
    full, cols, line, grads = block_specs(total, width, block, 1)
    return blocked(
        inner_kernel, 200, pieces, units // block, token,
        [full, full, pieces.w_in, line],
        [cols, cols, grads],
        [shape_of(total, units), shape_of(total, units, dtype=BF16), shape_of(2, 1, units, width // 2, dtype=BF16)],
        ffn, grad, pieces.gathered, bias,
    )


def run_outer(pieces, token, ffn, grad, pre, activ, *before):
    total, width = ffn.shape
    units, block = pieces.units(pieces.part_f), pieces.block(pieces.part_f)
    full, cols, line, grads = block_specs(total, width, block, 1)
    return blocked(
        outer_kernel, 200, pieces, units // block, token,
        [full, full, pieces.w_in, pieces.w_out, cols, cols, *[full] * len(before)],
        [grads, line, full, full],
        [shape_of(2, 1, units, width // 2, dtype=BF16), shape_of(1, units), shape_of(total, width), shape_of(total, width)],
        ffn, grad, pieces.gathered, pieces.outer, pre, activ, *before,
    )


def call(kernel, outs, scratch, smem, *arrays):
    return pl.pallas_call(
        kernel,
        out_shape=outs,
        in_specs=[pl.BlockSpec(memory_space=pltpu.SMEM)] * smem
        + [pl.BlockSpec(memory_space=pltpu.VMEM)] * (len(arrays) - smem),
        out_specs=jax.tree.map(lambda _: pl.BlockSpec(memory_space=pltpu.VMEM), outs),
        scratch_shapes=scratch,
        cost_estimate=cost(12),
    )(*arrays)


def scan_carry(grid, local, clear, whole, reverse):
    micros, heads = local.shape[:2]
    clear = jnp.broadcast_to(clear[:, None, None, None], (micros, 1, 8, 128))
    entering = jnp.zeros_like(local)
    reach = jnp.ones_like(local)
    total = local
    for mask in grid.tensor:
        got = grid.swap(jnp.concatenate([total, clear], axis=1), mask)
        got_total, got_clear = got[:, :heads], got[:, heads:]
        later = grid.bit(mask) == (0 if reverse else 1)
        entering = jnp.where(later, entering + reach * got_total, entering)
        reach = jnp.where(later, reach * got_clear * whole, reach)
        total = jnp.where(
            later, total + clear * whole * got_total, got_total + got_clear * whole * total
        )
        clear = clear * got_clear
        whole = whole * whole
    return entering


def after(values, *others):
    return lax.optimization_barrier((values, others))[0]


class Term:
    def __init__(self, array, labels, fixed):
        self.array, self.labels, self.fixed = array, labels, fixed


class Reduce:
    def __init__(self, grid, high, dims, still=()):
        self.grid, self.dims, self.still = grid, list(dims), still
        self.labels = ["side", "lead", *self.dims, "u", "h"]
        xs, (lo, *hi) = grid.xs[::-1], grid.tensor
        self.orders = [[*xs, lo], [lo, *xs]], hi[::-1]
        self.step, self.pair = -1, None
        self.high = self.view(high)
        self.raw = [grid.swap(self.high, grid.core)]

    def view(self, v):
        n = len(self.dims)
        return v.reshape(*v.shape[:2], *[2] * n, v.shape[2] >> n, v.shape[3])

    @property
    def steps(self):
        return len(self.orders[0][0]) + len(self.orders[1])

    def add_low(self, low):
        self.low = self.view(low)

    def take(self):
        if self.step < 0:
            self.sides = [[Term(a, self.labels, {"side": s}) for a in (self.low, self.raw[0])] for s in (0, 1)]
            self.left = [list(self.dims), list(self.dims)]
        else:
            for s in (0, 1):
                for t in self.sides[s]:
                    if self.masks[s] in t.labels:
                        t.fixed[self.masks[s]] = 0
                self.left[s] = [d for d in self.left[s] if d != self.masks[s]]
                if len(self.raw) == 2:
                    self.sides[s].append(Term(self.raw[s], ["lead", *self.left[s], "u", "h"], {}))
                elif self.pair is None:
                    self.sides[s].append(Term(self.raw[0], ["lead", *self.left[s], "u", "hh"], {"hh": s}))
                else:
                    names = ["pair", "lead", *self.left[s], "u", "hh"]
                    self.sides[s].append(Term(self.raw[0], names, {"pair": self.pair, "hh": s}))
            self.pair = None
        self.step += 1

    def wanted(self):
        (first, second), hi = self.orders
        k = self.step
        if k == self.steps:
            return [(self.sides[s], {}, self.left[s]) for s in (0, 1)], True
        self.masks = [first[k], second[k]] if k < len(first) else [hi[k - len(first)]] * 2
        return [
            (self.sides[s], {self.masks[s]: 1}, [d for d in self.left[s] if d != self.masks[s]]) for s in (0, 1)
        ], k >= len(first)

    def start(self, sends):
        if len(sends) == 2:
            self.raw = [self.grid.swap(v, m) for v, m in zip(sends, self.masks)]
        else:
            self.raw = [self.grid.swap(sends[0], self.masks[0])]


def place_of(grid, still, fixed, name, sel):
    if name in still:
        masks = [*grid.tensor, *grid.xs]
        return sel[2 * masks.index(name) + fixed[name]]
    return fixed[name]


def picked(grid, still, term, extra, sel):
    v = term.array
    fixed = {**term.fixed, **extra}
    for axis in reversed(range(len(term.labels))):
        name = term.labels[axis]
        if name == "hh":
            half = v.shape[-1] // 2
            v = v[..., fixed[name] * half : (fixed[name] + 1) * half]
        elif name in fixed:
            v = lax.dynamic_index_in_dim(v, place_of(grid, still, fixed, name, sel), axis, False)
    return v.astype(F32)


def point(grid, gates, *sums, behind=None):
    for r in sums:
        r.take()
    outs, tasks = [], []
    for r in sums:
        sides, joined = r.wanted()
        for terms, fixed, left in sides:
            tasks.append((r, terms, fixed, left))
        shapes = []
        for terms, fixed, left in sides:
            low = r.low.shape
            shapes.append((low[1], *[2] * len(left), *low[-2:]))
        if joined:
            outs.append((*shapes[0][:-1], 2 * shapes[0][-1]))
        else:
            outs.extend(shapes)
    pair = [
        k for k in range(len(sums) - 1)
        if 0 < len(sums[k].orders[0][0]) <= sums[k].step < sums[k].steps
        and sums[k].step == sums[k + 1].step and sums[k].low.shape == sums[k + 1].low.shape
    ]
    joined_outs, ranks, k = [], [], 0
    for n, r in enumerate(sums):
        if n - 1 in pair:
            continue
        if n in pair:
            joined_outs.append((2, *outs[k]))
            ranks.append(True)
            k += 2
        else:
            m = 1 if r.step >= len(r.orders[0][0]) else 2
            joined_outs.extend(outs[k : k + m])
            ranks.extend([False] * m)
            k += m
    sel = grid.sel
    fits = all(len(r.dims) <= 4 and r.low.shape[-2] % 32 == 0 for r in sums)
    if fits:
        *values, token = run_point(grid, gates, tasks, joined_outs, ranks, sel)
    else:
        values = []
        sides = [
            sum(picked(grid, r.still, t, {k: v for k, v in fixed.items() if k in t.labels}, sel) for t in terms).astype(BF16)
            for r, terms, fixed, left in tasks
        ]
        for shape in outs:
            v = sides.pop(0)
            values.append(v if v.shape == shape else jnp.concatenate([v, sides.pop(0)], axis=-1))
        for n in pair:
            first = sum(1 if r.step >= len(r.orders[0][0]) else 2 for r in sums[:n]) - sum(m < n for m in pair)
            values[first : first + 2] = [jnp.stack(values[first : first + 2])]
        token = after(jnp.zeros((8, 128), F32), [g[(0,) * g.ndim] for g in gates])
    if behind is not None:
        values, behind = lax.optimization_barrier((values, behind))
    done, skip = [], False
    for k, r in enumerate(sums):
        if skip:
            skip = False
            continue
        if r.step == r.steps:
            done.append(values.pop(0))
        elif k in pair:
            both = grid.swap(values[0], r.masks[0])
            r.raw, r.pair = [both], 0
            sums[k + 1].raw, sums[k + 1].pair = [both], 1
            values, skip = values[1:], True
        else:
            n = 2 if r.step < len(r.orders[0][0]) else 1
            r.start(values[:n])
            values = values[n:]
    if behind is not None:
        return token, behind
    return (token, *done) if done else token


def run_point(grid, gates, tasks, outs, ranks, sel):
    parts = 2
    arrays, specs, layout = [], [], []
    for r, terms, extra, left in tasks:
        mine = []
        for t in terms:
            fixed = {**t.fixed, **{k: v for k, v in extra.items() if k in t.labels}}
            block = []
            for name, size in zip(t.labels, t.array.shape):
                if name == "hh":
                    block.append(size // 2)
                elif name == "u":
                    block.append(size // parts)
                else:
                    block.append(None if name in fixed else size)

            def index(i, p, t=t, fixed=fixed, r=r):
                return tuple(
                    i if name == "u" else place_of(grid, r.still, fixed, name, p) if name in fixed else 0
                    for name in t.labels
                )

            mine.append(len(arrays))
            arrays.append(t.array)
            specs.append(pl.BlockSpec(tuple(block), index))
        layout.append(mine)
    out_specs = []
    for shape in outs:
        block = (*shape[:-2], shape[-2] // parts, shape[-1])
        out_specs.append(pl.BlockSpec(block, lambda i, p, n=len(shape): (*[0] * (n - 2), i, 0)))
    out_specs.append(pl.BlockSpec((8, 128), lambda i, p: (0, 0)))

    def body(p, *refs):
        refs = refs[len(gates) :]
        ins, results = refs[: len(arrays)], refs[len(arrays) :]
        queue = list(layout)
        for ref, rank in zip(results[:-1], ranks):
            for ref in [ref.at[k] for k in (0, 1)] if rank else [ref]:
                first = 0
                while first < ref.shape[-1]:
                    mine = queue.pop(0)
                    total = ins[mine[0]][...].astype(F32)
                    for k in mine[1:]:
                        total = total + ins[k][...].astype(F32)
                    ref[..., first : first + total.shape[-1]] = total.astype(BF16)
                    first += total.shape[-1]
        results[-1][...] = jnp.zeros((8, 128), F32)

    return pl.pallas_call(
        body,
        grid_spec=pltpu.PrefetchScalarGridSpec(
            num_scalar_prefetch=1,
            grid=(parts,),
            in_specs=[pl.BlockSpec(memory_space=pl.ANY)] * len(gates) + specs,
            out_specs=out_specs,
        ),
        out_shape=[shape_of(*shape, dtype=BF16) for shape in outs] + [shape_of(8, 128)],
        cost_estimate=cost(1),
    )(sel, *gates, *arrays)


def ends(result):
    return result if isinstance(result, tuple) else (result,)


def finish(grid, gates, r, value=None):
    while value is None:
        out = point(grid, gates, r)
        value = out[1] if isinstance(out, tuple) else None
    return value


def share_units(grid, part):
    held = part[None]
    masks = [*grid.xs, grid.core]
    for mask in masks:
        held = jnp.concatenate([held, grid.swap(held, mask)], axis=0)
    n = held.shape[0]
    held = held.astype(F32)
    for k, mask in enumerate(masks):
        held = held.reshape(n >> (k + 1), 2, -1, *part.shape)
        held = jnp.where(grid.bit(mask) == 1, held[:, ::-1], held)
    held = held.reshape(n, *part.shape).transpose(1, 0, 2, 3)
    return held.reshape(part.shape[0], -1, part.shape[-1])


def place_kernel(turned, bits, own_ref, x_ref, c_ref, *outs):
    swap_c, swap_x = bits[0] == 1, bits[1] == 1
    outs[-1][...] = jnp.zeros((8, 128), F32)
    for k, turn in enumerate(turned):
        rows = []
        for own, other in ((own_ref[k], x_ref[k]), (c_ref[0, k], c_ref[1, k])):
            own, other = own.astype(F32), other.astype(F32)
            rows.append(jnp.concatenate([jnp.where(swap_x, other, own), jnp.where(swap_x, own, other)], axis=0))
        v = jnp.concatenate(
            [jnp.where(swap_c, rows[1], rows[0]), jnp.where(swap_c, rows[0], rows[1])], axis=0
        )
        outs[k][...] = v.T if turn else v


def share_and_place(grid, parts, turned, zero):
    results = []
    for part, turns in zip(parts, turned):
        if zero is not None:
            part = part + zero
        lead, units, width = part.shape
        if len(grid.xs) > 1 or units % 16:
            rows = share_units(grid, part)
            results.append([r.T if t else r for r, t in zip(rows, turns)])
            continue
        from_x = grid.swap(part, grid.xs[0])
        from_c = grid.swap(jnp.stack([part, from_x]), grid.core)
        results.append(
            pl.pallas_call(
                partial(place_kernel, turns),
                in_specs=[pl.BlockSpec(memory_space=pltpu.SMEM)] + [pl.BlockSpec(memory_space=pltpu.VMEM)] * 3,
                out_specs=[pl.BlockSpec(memory_space=pltpu.VMEM)] * (lead + 1),
                out_shape=[shape_of(*((width, 4 * units) if t else (4 * units, width))) for t in turns] + [shape_of(8, 128)],
                cost_estimate=cost(5),
            )(jnp.stack([grid.bit(grid.core), grid.bit(grid.xs[0])]).astype(jnp.int32), part, from_x, from_c)
        )
    return results


def pack_kernel(
    bits, before, eta0, eta1, one0, one1, two0, two1, omega0, omega1, gain0, gain1, gates_ref, shared_ref, ffn_ref, out_sum_ref,
    v0, v1, r0, r1, i0, i1, packed_ref, rows,
):
    heads = eta0.shape[0]
    n = heads * 8
    for k, (a, b) in enumerate(((eta0, eta1), (one0, one1), (two0, two1))):
        rows[k * n : (k + 1) * n] = (a[...] + b[...]).reshape(n, 128)
    at = 3 * n

    def line(v, at):
        for j in range(v.shape[-1] // 128):
            rows[at + j : at + j + 1] = v[:, j * 128 : (j + 1) * 128]
        return at + v.shape[-1] // 128

    total = lambda v: jnp.sum(v, axis=0, keepdims=True)
    at = line(total(gain0[...] + gain1[...]), at)
    rows[at : at + 8] = omega0[...] + omega1[...]
    at = line(total(gates_ref[...]), at + 8)
    rows[at : at + 1] = shared_ref[3:4]
    rows[at + 1 : at + 4] = shared_ref[0:3]
    at = line(total(ffn_ref[...]), at + 4)
    at = line(total(out_sum_ref[...]), at)
    core, x = bits[0], bits[1]
    tensor = i0.shape[-1] // 256
    for low, high in ((v0, v1), (r0, r1)):
        for k, ref in enumerate((low, high)):
            for t in range(tensor):
                own, other = (ref[:, (q * tensor + t) * 64 : (q * tensor + t + 1) * 64] for q in (0, 1))
                row = jnp.where(
                    x == 0, jnp.concatenate([own, other], axis=1), jnp.concatenate([other, own], axis=1)
                )
                rows[pl.ds(at + 2 * t + (core ^ k), 1), :] = row
        at += 2 * tensor
    for k, ref in enumerate((i0, i1)):
        for q in (0, 1):
            for t in range(tensor):
                row = ref[:, (q * tensor + t) * 128 : (q * tensor + t + 1) * 128]
                rows[pl.ds(at + 4 * t + 2 * (core ^ k) + (x ^ q), 1), :] = row
    at += 4 * tensor
    rows[at:] = jnp.zeros((rows.shape[0] - at, 128), F32)
    packed_ref[...] = rows[...].astype(BF16)


def run_pack(bits, token, sums, count):
    vmem = pl.BlockSpec(memory_space=pltpu.VMEM)
    return pl.pallas_call(
        pack_kernel,
        in_specs=[pl.BlockSpec(memory_space=pltpu.SMEM), pl.BlockSpec(memory_space=pl.ANY)] + [vmem] * len(sums),
        out_specs=vmem,
        out_shape=shape_of(count, 128, dtype=BF16),
        scratch_shapes=[pltpu.VMEM((count, 128), F32)],
        cost_estimate=cost(4),
    )(bits, token, *sums)


def join_kernel(place, left_ref, right_ref, out_ref, token_ref):
    token_ref[...] = jnp.zeros((8, 128), F32)
    n = left_ref.shape[1]
    out_ref[:, :n] = left_ref[...].astype(F32)
    part = right_ref.shape[1]
    count = out_ref.shape[0] // part
    for k in range(count):
        v = right_ref[place[pl.program_id(0) * count + k]]
        out_ref[k * part : (k + 1) * part, n:] = v.astype(F32)


def join(place, left, right):
    rows, n = left.shape
    block = 256
    return pl.pallas_call(
        join_kernel,
        grid_spec=pltpu.PrefetchScalarGridSpec(
            num_scalar_prefetch=1,
            grid=(rows // block,),
            in_specs=[pl.BlockSpec((block, n), lambda i, p: (i, 0)), pl.BlockSpec(right.shape, lambda i, p: (0, 0, 0))],
            out_specs=[
                pl.BlockSpec((block, n + right.shape[2]), lambda i, p: (i, 0)), pl.BlockSpec((8, 128), lambda i, p: (0, 0))
            ],
        ),
        out_shape=[shape_of(rows, n + right.shape[2]), shape_of(8, 128)],
        cost_estimate=cost(50),
    )(place, left, right)


def sum_flat(grid, packed, hold, last_hold, end_hold):
    held = packed.astype(F32)
    masks = [grid.core, *grid.tensor, *grid.xs]
    for mask in masks:
        if mask == masks[-1]:
            held = tied(held, last_hold)
        low = packed if mask == masks[0] else held.astype(BF16)
        held = low.astype(F32) + grid.swap(low, mask).astype(F32)
        if mask == masks[0]:
            held = tied(held, hold)
    return tied(held, end_hold).reshape(-1)


def every_part(grid, part):
    parts = part
    masks = [grid.core, *grid.tensor, *grid.xs]
    for mask in masks:
        parts = jnp.concatenate([parts, grid.swap(parts, mask)])
    devices = jnp.arange(grid.count) ^ grid.index
    place = sum(((devices // mask) % 2) << k for k, mask in enumerate(masks)).astype(jnp.int32)
    return parts.reshape(grid.count, *part.shape), place


def tied(v, token):
    return (v.reshape(-1, 8, 128) + token.astype(v.dtype)).reshape(v.shape)


def padded(v, size):
    return jnp.concatenate([v, jnp.zeros(-v.size % size, F32)])


def local(
    inputs, resets, cotangent, norm_gain, ema_alpha, ema_damp, ema_beta, ema_eta, ema_omega,
    w_gates, b_gates, qk_gain, q_bias, w_value, b_value, w_reset, b_reset, w_branch, ffn_gain,
    w_in, b_in, w_out, b_out,
):
    grid = Grid()
    micros, rows, width = inputs.shape
    total = micros * rows
    heads = ema_alpha.shape[1]
    rank = lax.axis_index("tensor")
    units_v, units_f = w_value.shape[1], w_in.shape[1]
    n_x = 1 << len(grid.xs)
    split_x = n_x == 2
    core, x_at = grid.bit(grid.core), lax.axis_index("dp") // 2

    half_v, half_f = units_v // 2, units_f // 2

    def chunks(w, half, axis, whole):
        size = half // n_x
        picks = range(n_x) if whole else range(1)
        return jnp.concatenate(
            [lax.dynamic_slice_in_dim(w, core * half + (x_at ^ r) * size, size, axis) for r in picks],
            axis=axis,
        )

    n_tensor = lax.axis_size("tensor")
    part_f, part_v = half_f // n_x, half_v // n_x
    own = lambda w, half, axis: chunks(w, half, axis, False)
    bias = jnp.concatenate([own(b_value, half_v, 0), own(b_reset, half_v, 0), own(b_in, half_f, 0)])
    bias = jnp.zeros((8, width), BF16).at[0, : bias.size].set(bias)
    seed = jnp.concatenate(
        [
            own(w_in, half_f, 1).T, own(w_value, half_v, 1).T, own(w_reset, half_v, 1).T, own(w_branch, half_v, 0),
            bias,
        ]
    )
    gathered = lax.all_gather(seed, AXES, axis=0)
    gathered_out = lax.all_gather(own(w_out, half_f, 0), AXES, axis=0)
    which = [
        jnp.stack([(x_at ^ r) * 2 + c for r in range(n_x)]).astype(jnp.int32) for c in (core, 1 - core)
    ]
    pieces = [Pieces(gathered, gathered_out, w, n_tensor, part_f, part_v) for w in which]
    table = gathered[:, part_f + 3 * part_v].astype(F32).reshape(2 * n_x, n_tensor, width)
    tables = [jnp.stack([lax.dynamic_index_in_dim(table, w[r], 0, False) for r in range(n_x)]) for w in which]
    bias_v = [t[..., :part_v].reshape(1, -1) for t in tables]
    bias_r = [t[..., part_v : 2 * part_v].reshape(1, -1) for t in tables]
    bias_i = [t[..., 2 * part_v : 2 * part_v + part_f].reshape(1, -1) for t in tables]
    dims = [*grid.xs[::-1], *grid.tensor[::-1]]
    still = grid.tensor

    def in_place(low, high):
        d = [grid.core, *dims]
        v = jnp.stack([low, high]).reshape(*[2] * len(d), -1)
        for axis, mask in enumerate(d):
            if mask not in still:
                v = jnp.where(grid.bit(mask) == 1, jnp.flip(v, axis), v)
        want = [*grid.tensor[::-1], grid.core, *grid.xs[::-1]]
        return v.transpose(*[d.index(m) for m in want], len(d)).reshape(-1)

    offsets = rank * rows + jnp.arange(rows)
    flags = jnp.where(offsets[None] == 0, 1, resets).astype(jnp.int32)
    sel = jnp.stack([grid.bit(m) ^ i for m in [*grid.tensor, *grid.xs] for i in (0, 1)]).astype(jnp.int32)
    places = [jnp.stack([2 * x + c for x in range(n_x)]).astype(jnp.int32) for c in (core, 1 - core)]
    flags, grid.sel, places, which = lax.optimization_barrier((flags, sel, places, which))
    for p, w in zip(pieces, which):
        p.which = w
    tile = lambda a: a.T.reshape(heads, 8, 128)
    decay = tile(1.0 - ema_alpha * ema_damp)
    feed = tile(ema_alpha * ema_beta)
    tell = tile(ema_eta)
    whole = jnp.exp(rows * jnp.log(decay))[None]
    clear = (jnp.sum(flags, axis=1) == 0).astype(F32)
    source_low = inputs.reshape(total, width)
    laid = jax.ShapeDtypeStruct((total * 8, 128), F32)
    wide = jax.ShapeDtypeStruct((total, width), F32)
    wide_low = jax.ShapeDtypeStruct((total, width), BF16)
    states = jax.ShapeDtypeStruct((micros, heads, 8, 128), F32)
    sums = jax.ShapeDtypeStruct((heads, 8, 128), F32)
    normed_laid, normed_low, final = call(
        norm_kernel, (laid, wide_low, states), [], 1,
        flags, source_low, norm_gain[None], decay, feed,
    )
    start = scan_carry(grid, final, clear, whole, False)
    blended, mixed_low = call(
        blend_kernel, (wide, wide_low), [pltpu.VMEM((total * 8, 128), F32)], 1,
        flags, normed_laid, start, decay, feed, tell, ema_omega.reshape(8, 128),
    )

    source = source_low.astype(F32)
    gate_pre = dot_plain(mixed_low, w_gates) + b_gates
    update = jax.nn.sigmoid(gate_pre[:, :width])
    direct = gate_pre[:, width : 2 * width]
    shared_pre = gate_pre[:, 2 * width :]
    shared = rounded(jax.nn.silu(shared_pre))
    query = (shared * qk_gain[0] + q_bias).astype(BF16)
    key = (shared * qk_gain[1]).astype(BF16)
    blocks = total // BLOCK
    doc = jnp.cumsum(flags.reshape(blocks, BLOCK), axis=1)
    order = jnp.arange(BLOCK)
    allowed = (doc[:, :, None] == doc[:, None, :]) & (order[:, None] >= order[None, :])[None]
    score_scale = query.shape[-1] ** (-0.5)
    query_b, key_b = query.reshape(blocks, BLOCK, -1), key.reshape(blocks, BLOCK, -1)
    scores = jnp.einsum("cik,cjk->cij", query_b, key_b, preferred_element_type=F32) * score_scale
    scores = jnp.where(allowed, scores, -1000000000.0)
    probs = jax.nn.softmax(scores, axis=-1)
    probs_low = probs.astype(BF16)

    both = Pieces(gathered, gathered_out, jnp.concatenate(which), n_tensor, part_f, part_v)
    bias_v, bias_r = jnp.concatenate(bias_v, axis=1), jnp.concatenate(bias_r, axis=1)
    *kept, branch = run_value(both, bias_v, normed_low, mixed_low, probs_low, bias_v, bias_r)
    mixed_out, ffn_low = run_middle(gate_pre, branch, source_low, ffn_gain)
    grad_low = cotangent.reshape(total, width)

    inner = [None, None]
    inner[1] = run_inner(pieces[1], bias_i[1], ffn_low, grad_low, bias_i[1])
    r_out = Reduce(grid, inner[1][2], dims, still)
    inner[0] = run_inner(pieces[0], inner[1][1], ffn_low, grad_low, bias_i[0])
    r_out.add_low(inner[0][2])
    token, gathered_out = point(grid, [], r_out, behind=gathered_out)
    for p in pieces:
        p.outer = gathered_out
    sum_in = [None, None]
    d_high, sum_in[1], feed_out, grad_ffn = run_outer(
        pieces[1], token, ffn_low, grad_low, inner[1][0], inner[1][1]
    )
    r_in = Reduce(grid, d_high, dims, still)
    token = point(grid, [sum_in[1]], r_out)
    d_low, sum_in[0], feed_out, grad_ffn = run_outer(
        pieces[0], token, ffn_low, grad_low, inner[0][0], inner[0][1], feed_out, grad_ffn
    )
    r_in.add_low(d_low)
    token = point(grid, [], r_out, r_in)
    output, grad_source, grad_gates_low, sum_ffn_gain, sum_out, sum_gates = run_middle_back(
        token, gate_pre, branch, source_low, ffn_gain, b_out, mixed_out, feed_out, grad_low, grad_ffn
    )
    bits = [*grid.xs[::-1], grid.core, *grid.tensor[::-1]]
    dims_g = [m for m in bits if m != grid.core]
    if width // (2 * n_x) % 128 == 0:
        d_gates = [None, None]
        d_gates[1] = run_gates(places[1], sum_gates, mixed_low, grad_gates_low)
        r_gates = Reduce(grid, d_gates[1], dims_g, dims_g)
        d_gates[0] = run_gates(places[0], d_gates[1], mixed_low, grad_gates_low)
        r_gates.add_low(d_gates[0])
        token = d_gates[0]
    else:
        c_axis = bits.index(grid.core)
        d_gates = [
            dot_over_rows(mixed_low, side).astype(BF16).reshape(*[2] * len(bits), -1, width)
            for side in (grad_gates_low[:, :width], grad_gates_low[:, width:])
        ]
        half_of = lambda i: jnp.stack(
            [lax.dynamic_index_in_dim(d, i, c_axis, False).reshape(1, width // 2, width) for d in d_gates]
        )
        r_gates = Reduce(grid, half_of(1 - core), dims_g, dims_g)
        r_gates.add_low(half_of(core))
        token = sum_gates

    def run_vb(k, token):
        return run_value_back(
            pieces[k], k, 200 if k == 0 else 1, token, grad_gates_low, normed_low, mixed_low, probs_low, kept
        )

    back = [None, None]
    back[1] = run_vb(1, token)
    r_v = Reduce(grid, back[1][0], dims, still)
    token = point(grid, [back[1][1], *r_out.raw], r_in, r_gates)
    back[0] = run_vb(0, token)
    r_v.add_low(back[0][0])
    token = point(grid, [back[0][1]], r_v, r_gates, r_in)
    grad_laid, left, grad_shared_low, sums_shared = run_shared(
        token, flags, back[0][5], back[1][5], probs, query, key, shared, shared_pre, qk_gain, grad_gates_low, w_gates,
        back[0][3], back[1][3], blended, decay, tell,
    )
    token = point(grid, [left, *r_in.raw], r_gates)
    left = left + token
    d_shared = dot_over_rows(mixed_low, tied(grad_shared_low, token))
    d_shared = d_shared.reshape(*[2] * len(bits), -1, d_shared.shape[-1])

    def fold(v, mask):
        axis, here = bits.index(mask), grid.bit(mask)
        got = grid.swap(lax.dynamic_slice_in_dim(v, 1 - here, 1, axis).astype(BF16), mask)
        return lax.dynamic_slice_in_dim(v, here, 1, axis) + got.astype(F32)

    right = scan_carry(grid, left, clear, whole, True)
    t_first, *t_rest = grid.tensor
    for mask in [grid.core, *grid.xs, t_first]:
        d_shared = fold(d_shared, mask)
    token = point(grid, [right], r_v, r_gates, r_in, r_out)
    d_shared = fold(tied(d_shared, token) if d_shared.shape[-2] % 8 == 0 else d_shared, t_rest[0])
    column = shape_of(8, 128)
    results = []
    for m in range(micros):
        part = slice(m * rows, (m + 1) * rows)
        laid_part = slice(m * rows * 8, (m + 1) * rows * 8)
        results.append(
            run_back(
                m, token, flags, normed_laid, grad_laid, start, right, decay, feed, tell, ema_omega.reshape(8, 128),
                back[0][4], back[1][4], source_low, grad_source, norm_gain[None],
            )
        )
        if m == 0:
            token, *done = ends(point(grid, [results[0][1]], r_gates, r_in, r_out, r_v))
            d_shared = tied(d_shared, token) if d_shared.shape[-2] % 8 == 0 else d_shared
            for mask in t_rest[1:]:
                d_shared = fold(d_shared, mask)
    done_gates = finish(grid, [token], r_gates, *done[:1])
    done_in = finish(grid, [token], r_in, *done[1:2])
    done_out = finish(grid, [token], r_out, *done[2:])
    token_v = point(grid, [results[-1][1]], r_v)
    token_w, *done_v = ends(point(grid, [token_v], r_v))
    done_v = finish(grid, [token_w], r_v, *done_v)
    grad_w_out, grad_w_in = share_and_place(grid, [done_out, done_in], [(False,), (True,)], None)
    grad_w_out, grad_w_in = grad_w_out[0], grad_w_in[0]
    grad_w_gates = lax.all_gather(
        done_gates.reshape(width // grid.count, 2 * width), AXES, axis=0, tiled=True
    )

    z = token_v[0, 0]
    part = d_shared.reshape(width // grid.count, -1)
    part = tied(part, token_w) if part.shape[0] % 8 == 0 else part
    sizes_late = [heads * width] * 3 + [width, width]
    sizes_early = [2 * width + 128, 256, 128, width, width, units_v * n_tensor, units_v * n_tensor, units_f * n_tensor]
    count = -(-sum(sizes_late + sizes_early) // 2048) * 16
    if (part_v, part_f, n_x) == (64, 128, 2):
        by_kind = [r[k] for k in range(1, 4) for r in results]
        packed = run_pack(
            jnp.stack([core, x_at]).astype(jnp.int32), token_v,
            [
                *by_kind, *[r[4] for r in results], *[r[5] for r in results], sum_gates, sums_shared, sum_ffn_gain, sum_out,
                back[0][2], back[1][2], back[0][1], back[1][1], *sum_in,
            ],
            count,
        )
    else:
        spread_in = lambda k: in_place(back[0][k] + z, back[1][k] + z)
        both = [sum(r[k] + z for r in results) for k in range(1, 6)]
        small = [
            *[v.reshape(-1) for v in both[:3]], jnp.sum(both[4], axis=0), both[3].reshape(-1), jnp.sum(sum_gates + z, axis=0),
            sums_shared[3] + z, sums_shared[:2].reshape(-1) + z, sums_shared[2] + z, jnp.sum(sum_ffn_gain + z, axis=0),
            jnp.sum(sum_out + z, axis=0), spread_in(2), spread_in(1), in_place(sum_in[0] + z, sum_in[1] + z),
        ]
        packed = padded(jnp.concatenate(small), count * 128).reshape(-1, 128).astype(BF16)

    def cut_like(v, sizes):
        out, first = [], 0
        for n in sizes:
            out.append(v[first : first + n])
            first += n
        return out

    ((grad_w_branch, grad_w_reset, grad_w_value, *placed),) = share_and_place(grid, [done_v], [(False, True, True)], None)
    parts, place = every_part(grid, part.astype(BF16))
    grad_w_gates, token_j = join(place, grad_w_gates, parts)
    summed = sum_flat(grid, packed, token_w, placed[0] if placed else token_w, token_j)
    last, cut = cut_like(summed, sizes_late), cut_like(summed[sum(sizes_late) :], sizes_early)
    untile = lambda v: v.reshape(heads, width).T
    eta, one, two = (untile(v) for v in last[:3])
    mine = lambda v, n: lax.dynamic_slice_in_dim(v, rank * n, n, 0)
    return (
        output.reshape(inputs.shape),
        jnp.stack([r[0] + z for r in results]),
        last[3],
        ema_beta * one - ema_damp * two,
        -ema_alpha * two,
        ema_alpha * one,
        eta,
        last[4],
        grad_w_gates,
        cut[0],
        cut[1].reshape(2, -1),
        cut[2],
        grad_w_value,
        mine(cut[5], units_v),
        grad_w_reset,
        mine(cut[6], units_v),
        grad_w_branch,
        cut[3],
        grad_w_in,
        mine(cut[7], units_f),
        grad_w_out,
        cut[4],
    )


def solution(mesh):
    rows = P(None, AXES, None)
    col, row, vec, rep = P(None, "tensor"), P("tensor", None), P("tensor"), P()
    return jax.shard_map(
        local,
        mesh=mesh,
        in_specs=(
            rows, P(None, AXES), rows, rep, rep, rep, rep, rep, rep, rep, rep, rep, rep,
            col, vec, col, vec, row, rep, col, vec, row, rep,
        ),
        out_specs=(
            rows, rows, rep, rep, rep, rep, rep, rep, rep, rep, rep, rep,
            col, vec, col, vec, row, rep, col, vec, row, rep,
        ),
        check_vma=False,
    )
```

```python
from functools import partial

import jax
import jax.numpy as jnp
from jax import lax
from jax.experimental import pallas as pl
from jax.experimental.pallas import tpu as pltpu
from jax.sharding import PartitionSpec as P

BLOCK = 128
HIGHEST = lax.Precision.HIGHEST
EPSILON = 1e-06
AXES = ("dp", "tensor")
F32 = jnp.float32
BF16 = jnp.bfloat16


def dot_plain(a, b):
    return jnp.dot(a, b, preferred_element_type=F32)


def dot_against(a, b):
    return lax.dot_general(a, b, (((1,), (1,)), ((), ())), preferred_element_type=F32)


def dot_over_rows(a, b):
    return lax.dot_general(a, b, (((0,), (0,)), ((), ())), preferred_element_type=F32)


def rounded(v):
    return lax.reduce_precision(v, exponent_bits=8, mantissa_bits=7)


def silu_slope(v):
    s = jax.nn.sigmoid(v)
    return s * (1.0 + v * (1.0 - s))


class Grid:
    def __init__(self):
        dp, tensor = lax.axis_size("dp"), lax.axis_size("tensor")
        self.count = dp * tensor
        self.index = lax.axis_index("dp") * tensor + lax.axis_index("tensor")
        masks = lambda n, first: [first << k for k in range(n.bit_length() - 1)]
        self.tensor = masks(tensor, 1)
        self.core, *self.xs = masks(dp, tensor)

    def bit(self, mask):
        return (self.index // mask) % 2

    def swap(self, value, mask):
        return lax.ppermute(value, AXES, [(i, i ^ mask) for i in range(self.count)])


def ema_step(state, row, keep, decay, feed):
    return [(s * keep) * q + f * row for s, q, f in zip(state, decay, feed)]


def row_of(ref, base, r):
    return ref[pl.ds(base + r, 8, stride=8), :]


def spread(ref, block, values):
    for j in range(8):
        ref[pl.ds(pl.multiple_of(block * 64, 64) + 8 * j, 8), :] = values[:, j * 128 : (j + 1) * 128]


def collect(ref, block):
    return jnp.concatenate(
        [ref[pl.ds(pl.multiple_of(block * 64, 64) + 8 * j, 8), :] for j in range(8)], axis=1
    )


def norm_kernel(flags, x_ref, gain_ref, decay_ref, feed_ref, normed_ref, low_ref, final_ref):
    micros, rows = flags.shape
    heads = decay_ref.shape[0]

    def norm_block(b, carry):
        at = pl.ds(pl.multiple_of(b * 16, 16), 16)
        x = x_ref[at, :].astype(F32)
        n = x * lax.rsqrt(jnp.mean(x * x, axis=-1, keepdims=True) + EPSILON) * gain_ref[...]
        low_ref[at, :] = n.astype(BF16)
        spread(normed_ref, 2 * b, n[:8])
        spread(normed_ref, 2 * b + 1, n[8:])
        return carry

    lax.fori_loop(0, micros * rows // 16, norm_block, 0)
    for m in range(micros):
        for h0 in range(0, heads, 8):
            decay = [decay_ref[h0 + h] for h in range(8)]
            feed = [feed_ref[h0 + h] for h in range(8)]

            def block(b, state, m=m, decay=decay, feed=feed):
                base = pl.multiple_of((m * (rows // 8) + b) * 64, 64)
                for r in range(8):
                    keep = (1 - flags[m, b * 8 + r]).astype(F32)
                    state = ema_step(state, row_of(normed_ref, base, r), keep, decay, feed)
                return state

            state = lax.fori_loop(0, rows // 8, block, [jnp.zeros((8, 128), F32)] * 8)
            for h in range(8):
                final_ref[m, h0 + h] = state[h]


def blend_kernel(
    flags, normed_ref, start_ref, decay_ref, feed_ref, out_ref, omega_ref, blended_ref, low_ref, acc_ref
):
    micros, rows = flags.shape
    heads = decay_ref.shape[0]
    omega = omega_ref[...]
    for m in range(micros):
        for h0 in range(0, heads, 8):
            decay = [decay_ref[h0 + h] for h in range(8)]
            feed = [feed_ref[h0 + h] for h in range(8)]
            tell = [out_ref[h0 + h] for h in range(8)]

            def block(b, state, m=m, h0=h0, decay=decay, feed=feed, tell=tell):
                base = pl.multiple_of((m * (rows // 8) + b) * 64, 64)
                for r in range(8):
                    keep = (1 - flags[m, b * 8 + r]).astype(F32)
                    row = row_of(normed_ref, base, r)
                    state = ema_step(state, row, keep, decay, feed)
                    told = [s * t for s, t in zip(state, tell)]
                    while len(told) > 1:
                        told = [told[i] + told[i + 1] for i in range(0, len(told), 2)]
                    at = pl.ds(base + r, 8, stride=8)
                    if h0 == 0:
                        acc_ref[at, :] = told[0] + omega * row
                    else:
                        acc_ref[at, :] = acc_ref[at, :] + told[0]
                return state

            lax.fori_loop(0, rows // 8, block, [start_ref[m, h0 + h] for h in range(8)])

    def finish(b, carry):
        at = pl.ds(pl.multiple_of(b * 16, 16), 16)
        v = jnp.concatenate([collect(acc_ref, 2 * b), collect(acc_ref, 2 * b + 1)], axis=0)
        blended_ref[at, :] = v
        low_ref[at, :] = (v / (1.0 + jnp.exp(-v))).astype(BF16)
        return carry

    lax.fori_loop(0, micros * rows // 16, finish, 0)


def shared_kernel(
    before, flags, gp0_ref, gp1_ref, probs_ref, query_ref, key_ref, shared_ref, pre_ref, gain_ref, gates_ref, weight_ref,
    mix0_ref, mix1_ref, blended_ref, decay_ref, tell_ref,
    rows_ref, left_ref, low_ref, sums_ref,
):
    b = pl.program_id(0)
    width = mix0_ref.shape[-1]
    probs = probs_ref[0]
    grad_probs = gp0_ref[0] + gp1_ref[0]
    scale = query_ref.shape[-1] ** (-0.5)
    grad_scores = probs * (grad_probs - jnp.sum(grad_probs * probs, axis=-1, keepdims=True)) * scale
    exact = partial(lax.dot_general, precision=HIGHEST, preferred_element_type=F32)
    grad_query = exact(grad_scores, key_ref[...].astype(F32), (((1,), (0,)), ((), ())))
    grad_key = exact(grad_scores, query_ref[...].astype(F32), (((0,), (0,)), ((), ())))
    shared = shared_ref[...]
    pre = pre_ref[...]
    grad_pre = (grad_query * gain_ref[0:1] + grad_key * gain_ref[1:2]) * slope(pre, sigmoid(pre))
    low = grad_pre.astype(BF16)
    low_ref[...] = low
    total = lambda v: jnp.sum(v, axis=0, keepdims=True)
    part = jnp.concatenate(
        [
            total(grad_query * shared), total(grad_key * shared), total(grad_query), total(low.astype(F32)),
            jnp.zeros((4, low.shape[-1]), F32),
        ]
    )
    add_to(sums_ref, part)
    mixed = (
        mix0_ref[...]
        + mix1_ref[...]
        + dot_nt(gates_ref[...], weight_ref[:, : 2 * width])
        + dot_nt(low, weight_ref[:, 2 * width :])
    )
    v = blended_ref[...]
    grad = mixed * slope(v, sigmoid(v))
    for i in range(BLOCK // 8):
        spread(rows_ref, b * (BLOCK // 8) + i, grad[8 * i : 8 * i + 8])

    @pl.when(b == pl.num_programs(0) - 1)
    def _():
        micros, rows = flags.shape
        heads = decay_ref.shape[0]
        for m in range(micros):
            for h0 in range(0, heads, 8):
                decay = [decay_ref[h0 + h] for h in range(8)]
                tell = [tell_ref[h0 + h] for h in range(8)]

                def block(i, left, m=m, decay=decay, tell=tell):
                    b = rows // 8 - 1 - i
                    base = pl.multiple_of((m * (rows // 8) + b) * 64, 64)
                    for r in reversed(range(8)):
                        keep = (1 - flags[m, b * 8 + r]).astype(F32)
                        row = row_of(rows_ref, base, r)
                        left = [((t * row + k) * keep) * q for k, q, t in zip(left, decay, tell)]
                    return left

                left = lax.fori_loop(0, rows // 8, block, [jnp.zeros((8, 128), F32)] * 8)
                for h in range(8):
                    left_ref[m, h0 + h] = left[h]


def run_shared(token, flags, gp0, gp1, probs, query, key, shared, pre, gain, gates, weight, mix0, mix1, blended, decay, tell):
    total, width = mix0.shape
    z = query.shape[1]
    rows = lambda n: pl.BlockSpec((BLOCK, n), lambda b: (b, 0))
    pair = pl.BlockSpec((1, BLOCK, BLOCK), lambda b: (b, 0, 0))
    whole = lambda a: pl.BlockSpec(a.shape, lambda b: (0,) * a.ndim)
    micros, heads = flags.shape[0], decay.shape[0]
    return pl.pallas_call(
        shared_kernel,
        grid=(total // BLOCK,),
        in_specs=[
            pl.BlockSpec(memory_space=pl.ANY), pl.BlockSpec(memory_space=pltpu.SMEM), pair, pair, pair, rows(z), rows(z), rows(z), rows(z), whole(gain),
            rows(2 * width), whole(weight), rows(width), rows(width), rows(width), whole(decay), whole(tell),
        ],
        out_specs=[
            pl.BlockSpec((total * 8, 128), lambda b: (0, 0)),
            pl.BlockSpec((micros, heads, 8, 128), lambda b: (0, 0, 0, 0)),
            rows(z),
            pl.BlockSpec((8, z), lambda b: (0, 0)),
        ],
        out_shape=[
            shape_of(total * 8, 128), shape_of(micros, heads, 8, 128), shape_of(total, z, dtype=BF16), shape_of(8, z),
        ],
        cost_estimate=cost(200),
    )(token, flags, gp0, gp1, probs, query, key, shared, pre, gain, gates, weight, mix0, mix1, blended, decay, tell)


def back_kernel(
    m, before, flags, normed_ref, rows_ref, start_ref, right_ref, decay_ref, feed_ref, tell_ref, omega_ref,
    add0_ref, add1_ref, source_ref, base_ref, gain_ref,
    grad_ref, eta_ref, one_ref, two_ref, omega_out, gain_out, token_ref, states, acc_ref,
):
    rows = flags.shape[1]
    heads = decay_ref.shape[0]
    group = 4
    omega = omega_ref[...]
    zero = jnp.zeros((8, 128), F32)
    token_ref[...] = zero
    for h0 in range(0, heads, group):
        decay = [decay_ref[h0 + h] for h in range(group)]
        feed = [feed_ref[h0 + h] for h in range(group)]
        tell = [tell_ref[h0 + h] for h in range(group)]

        def ahead(b, state, decay=decay, feed=feed):
            base = pl.multiple_of(b * 64, 64)
            for r in range(8):
                keep = (1 - flags[m, b * 8 + r]).astype(F32)
                for h in range(group):
                    states[b * 8 + r, h] = state[h]
                state = ema_step(state, row_of(normed_ref, base, r), keep, decay, feed)
            return state

        last = lax.fori_loop(0, rows // 8, ahead, [start_ref[0, h0 + h] for h in range(group)])

        def back(i, carry, h0=h0, decay=decay, feed=feed, tell=tell):
            left, after_state, eta, one, two, with_omega = carry
            b = rows // 8 - 1 - i
            base = pl.multiple_of(b * 64, 64)
            for r in reversed(range(8)):
                keep = (1 - flags[m, b * 8 + r]).astype(F32)
                g = row_of(rows_ref, base, r)
                x = row_of(normed_ref, base, r)
                earlier = [states[b * 8 + r, h] for h in range(group)]
                eta = [e + s * g for e, s in zip(eta, after_state)]
                now = [t * g + k for t, k in zip(tell, left)]
                one = [o + n * x for o, n in zip(one, now)]
                kept = [n * keep for n in now]
                two = [w + k * s for w, k, s in zip(two, kept, earlier)]
                left = [k * q for k, q in zip(kept, decay)]
                gn = [n * f for n, f in zip(now, feed)]
                while len(gn) > 1:
                    gn = [gn[i] + gn[i + 1] for i in range(0, len(gn), 2)]
                at = pl.ds(base + r, 8, stride=8)
                if h0 == 0:
                    acc_ref[at, :] = gn[0] + omega * g
                    with_omega = with_omega + g * x
                else:
                    acc_ref[at, :] = acc_ref[at, :] + gn[0]
                after_state = earlier
            return left, after_state, eta, one, two, with_omega

        right = [right_ref[0, h0 + h] for h in range(group)]
        nothing = [zero] * group
        _, _, eta, one, two, with_omega = lax.fori_loop(
            0, rows // 8, back, (right, last, nothing, nothing, nothing, zero)
        )
        if h0 == 0:
            omega_out[...] = with_omega
        for h in range(group):
            eta_ref[h0 + h] = eta[h]
            one_ref[h0 + h] = one[h]
            two_ref[h0 + h] = two[h]

    def finish(b, gained):
        at = pl.ds(pl.multiple_of(b * 16, 16), 16)
        x = source_ref[at, :].astype(F32)
        scale = lax.rsqrt(jnp.mean(x * x, axis=-1, keepdims=True) + EPSILON)
        scaled = x * scale
        grad = jnp.concatenate([collect(acc_ref, 2 * b), collect(acc_ref, 2 * b + 1)], axis=0)
        grad = grad + add0_ref[at, :] + add1_ref[at, :]
        own = grad * scaled
        gained = gained + own[:8] + own[8:]
        inner = grad * gain_ref[...]
        mean = jnp.mean(inner * scaled, axis=-1, keepdims=True)
        grad_ref[at, :] = base_ref[at, :] + scale * (inner - scaled * mean)
        return gained

    width = source_ref.shape[-1]
    gain_out[...] = lax.fori_loop(0, rows // 16, finish, jnp.zeros((8, width), F32))


def run_back(m, token, flags, laid, grads, start, right, decay, feed, tell, omega, add0, add1, source, base, gain):
    rows, heads = flags.shape[1], decay.shape[0]
    width = source.shape[1]
    whole = lambda a: pl.BlockSpec(a.shape, lambda i: (0,) * a.ndim)
    tall = pl.BlockSpec((rows * 8, 128), lambda i: (m, 0))
    carry = pl.BlockSpec((1, heads, 8, 128), lambda i: (m, 0, 0, 0))
    wide = pl.BlockSpec((rows, width), lambda i: (m, 0))
    sums = pl.BlockSpec((heads, 8, 128), lambda i: (0, 0, 0))
    return pl.pallas_call(
        partial(back_kernel, m),
        grid=(1,),
        in_specs=[
            pl.BlockSpec(memory_space=pl.ANY), pl.BlockSpec(memory_space=pltpu.SMEM), tall, tall, carry, carry,
            whole(decay), whole(feed), whole(tell), whole(omega), wide, wide, wide, wide, whole(gain),
        ],
        out_specs=[
            pl.BlockSpec((rows, width), lambda i: (0, 0)), sums, sums, sums,
            pl.BlockSpec((8, 128), lambda i: (0, 0)), pl.BlockSpec((8, width), lambda i: (0, 0)),
            pl.BlockSpec((8, 128), lambda i: (0, 0)),
        ],
        out_shape=[
            jax.ShapeDtypeStruct((rows, width), F32),
            *[jax.ShapeDtypeStruct((heads, 8, 128), F32)] * 3,
            jax.ShapeDtypeStruct((8, 128), F32),
            jax.ShapeDtypeStruct((8, width), F32),
            jax.ShapeDtypeStruct((8, 128), F32),
        ],
        scratch_shapes=[pltpu.VMEM((rows, 4, 8, 128), F32), pltpu.VMEM((rows * 8, 128), F32)],
        cost_estimate=cost(200),
    )(token, flags, laid, grads, start, right, decay, feed, tell, omega, add0, add1, source, base, gain)


def dot_tn(a, b):
    return lax.dot_general(a, b, (((0,), (0,)), ((), ())), preferred_element_type=F32)


def dot_nt(a, b):
    return lax.dot_general(a, b, (((1,), (1,)), ((), ())), preferred_element_type=F32)


def dot_nn(a, b):
    return lax.dot_general(a, b, (((1,), (0,)), ((), ())), preferred_element_type=F32)


def sigmoid(v):
    return 1.0 / (1.0 + jnp.exp(-v))


def slope(v, s):
    return s * (1.0 + v * (1.0 - s))


def add_to(ref, value, first_ref=None):
    first = pl.program_id(0) == 0

    @pl.when(first)
    def _():
        ref[...] = value if first_ref is None else first_ref[...] + value

    @pl.when(jnp.logical_not(first))
    def _():
        ref[...] = ref[...] + value


def put_sides(ref, lead, v):
    half = v.shape[-1] // 2
    v = v.astype(BF16)
    ref[0, lead] = v[:, :half]
    ref[1, lead] = v[:, half:]


def value_kernel(
    piece, normed_ref, mixed_ref, probs_ref, wv_ref, wr_ref, wb_ref, bv_ref, br_ref,
    value_ref, reset_ref, attended_ref, gated_ref, out_ref,
):
    value_pre = dot_nt(normed_ref[...], flat(wv_ref)) + bv_ref[...]
    value_ref[...] = value_pre
    value = (value_pre * sigmoid(value_pre)).astype(BF16)
    blocks = probs_ref.shape[0]
    attended = jnp.concatenate(
        [dot_nn(probs_ref[b], value[b * BLOCK : (b + 1) * BLOCK]) for b in range(blocks)], axis=0
    )
    attended_ref[...] = attended
    reset_pre = dot_nt(mixed_ref[...], flat(wr_ref)) + br_ref[...]
    reset_ref[...] = reset_pre
    gated = (reset_pre * sigmoid(reset_pre) * attended).astype(BF16)
    gated_ref[...] = gated
    add_to(out_ref, dot_nn(gated, flat(wb_ref)))


def value_back_kernel(
    piece, grad_ref, normed_ref, mixed_ref, probs_ref, wv_ref, wr_ref, wb_ref,
    value_ref, reset_ref, attended_ref, gated_ref,
    d_ref, sum_r_ref, sum_v_ref, mixed_out, normed_out, probs_out,
):
    grad = grad_ref[...]
    grad_gated = dot_nt(grad, flat(wb_ref))
    put_sides(d_ref, 0, dot_tn(gated_ref[...], grad))
    reset_pre = reset_ref[...]
    s = sigmoid(reset_pre)
    grad_attended = (grad_gated * (reset_pre * s)).astype(BF16)
    grad_reset = (grad_gated * attended_ref[...] * slope(reset_pre, s)).astype(BF16)
    sum_r_ref[...] = jnp.sum(grad_reset.astype(F32), axis=0, keepdims=True)
    mixed = mixed_ref[...]
    put_sides(d_ref, 1, dot_tn(grad_reset, mixed))
    add_to(mixed_out, dot_nn(grad_reset, flat(wr_ref)))
    value_pre = value_ref[...]
    s = sigmoid(value_pre)
    value = (value_pre * s).astype(BF16)
    blocks = probs_ref.shape[0]
    grad_value, grad_probs = [], []
    for b in range(blocks):
        rows = slice(b * BLOCK, (b + 1) * BLOCK)
        grad_probs.append(dot_nt(grad_attended[rows], value[rows])[None])
        grad_value.append(dot_tn(probs_ref[b], grad_attended[rows]))
    add_to(probs_out, jnp.concatenate(grad_probs, axis=0))
    grad_value = (jnp.concatenate(grad_value, axis=0) * slope(value_pre, s)).astype(BF16)
    sum_v_ref[...] = jnp.sum(grad_value.astype(F32), axis=0, keepdims=True)
    put_sides(d_ref, 2, dot_tn(grad_value, normed_ref[...]))
    add_to(normed_out, dot_nn(grad_value, flat(wv_ref)))


def inner_kernel(piece, ffn_ref, grad_ref, wi_ref, bi_ref, pre_ref, activ_ref, do_ref):
    wi = flat(wi_ref)
    pre = dot_nt(ffn_ref[...], wi) + bi_ref[...]
    pre_ref[...] = pre
    activ = (pre * sigmoid(pre)).astype(BF16)
    activ_ref[...] = activ
    put_sides(do_ref, 0, dot_tn(activ, grad_ref[...]))


def outer_kernel(
    piece, ffn_ref, grad_ref, wi_ref, wo_ref, pre_ref, activ_ref, *rest
):
    *sums, di_ref, sum_i_ref, out_ref, ffn_out = rest
    sum_o_ref, sum_f_ref = sums if sums else (None, None)
    wi = flat(wi_ref)
    wo = flat(wo_ref)
    add_to(out_ref, dot_nn(activ_ref[...], wo), sum_o_ref)
    pre = pre_ref[...]
    grad = (dot_nt(grad_ref[...], wo) * slope(pre, sigmoid(pre))).astype(BF16)
    sum_i_ref[...] = jnp.sum(grad.astype(F32), axis=0, keepdims=True)
    put_sides(di_ref, 0, dot_tn(grad, ffn_ref[...]))
    add_to(ffn_out, dot_nn(grad, wi), sum_f_ref)


UNITS = 512


def cost(micros):
    return pl.CostEstimate(flops=int(micros * SCALE * 1.15e9), bytes_accessed=int(micros * SCALE * 3.3e6), transcendentals=0)


SCALE = 1.0


def shape_of(*dims, dtype=F32):
    return jax.ShapeDtypeStruct(dims, dtype)


def middle(gate_ref, branch_ref, source_ref):
    width = source_ref.shape[-1]
    update = sigmoid(gate_ref[:, :width])
    pre = gate_ref[:, width : 2 * width] + branch_ref[...]
    s = sigmoid(pre)
    return source_ref[...].astype(F32), update, pre, s


def middle_kernel(gate_ref, branch_ref, source_ref, gain_ref, mixed_ref, ffn_ref):
    source, update, pre, s = middle(gate_ref, branch_ref, source_ref)
    mixed = update * (pre * s) + (1.0 - update) * source
    mixed_ref[...] = mixed
    scale = lax.rsqrt(jnp.mean(mixed * mixed, axis=-1, keepdims=True) + EPSILON)
    ffn_ref[...] = (mixed * scale * gain_ref[...]).astype(BF16)


def column_sums(v):
    return jnp.sum(v.reshape(-1, 8, v.shape[-1]), axis=0)


def middle_back_kernel(
    before, gate_ref, branch_ref, source_ref, gain_ref, bias_ref, mixed_ref, feed_ref, grad_ref, ffn_ref,
    out_ref, base_ref, gates_ref, sum_gain_ref, sum_out_ref, sum_gates_ref,
):
    width = source_ref.shape[-1]
    source, update, pre, s = middle(gate_ref, branch_ref, source_ref)
    mixed = mixed_ref[...]
    out_ref[...] = (mixed + feed_ref[...] + bias_ref[...]).astype(BF16)
    scale = lax.rsqrt(jnp.mean(mixed * mixed, axis=-1, keepdims=True) + EPSILON)
    scaled = mixed * scale
    grad_out = grad_ref[...].astype(F32)
    grad_ffn = ffn_ref[...]
    add_to(sum_out_ref, column_sums(grad_out))
    add_to(sum_gain_ref, column_sums(grad_ffn * scaled))
    gained = grad_ffn * gain_ref[...]
    grad = grad_out + scale * (gained - scaled * jnp.mean(gained * scaled, axis=-1, keepdims=True))
    base_ref[...] = grad * (1.0 - update)
    grad_update = (grad * (pre * s - source) * update * (1.0 - update)).astype(BF16)
    grad_hidden = (grad * update * slope(pre, s)).astype(BF16)
    gates_ref[:, :width] = grad_update
    gates_ref[:, width:] = grad_hidden
    add_to(
        sum_gates_ref,
        jnp.concatenate([column_sums(grad_update.astype(F32)), column_sums(grad_hidden.astype(F32))], axis=1),
    )


def run_middle(gate, branch, source, gain):
    total, width = source.shape
    rows = lambda n: pl.BlockSpec((BLOCK, n), lambda i: (i, 0))
    line = pl.BlockSpec((1, width), lambda i: (0, 0))
    return pl.pallas_call(
        middle_kernel,
        grid=(total // BLOCK,),
        in_specs=[rows(gate.shape[1]), rows(width), rows(width), line],
        out_specs=[rows(width), rows(width)],
        out_shape=[shape_of(total, width), shape_of(total, width, dtype=BF16)],
        cost_estimate=cost(5),
    )(gate, branch, source, gain[None])


def run_middle_back(token, gate, branch, source, gain, bias, mixed, feed, grad, ffn):
    total, width = source.shape
    rows = lambda n: pl.BlockSpec((BLOCK, n), lambda i: (i, 0))
    line = pl.BlockSpec((1, width), lambda i: (0, 0))
    few = lambda n: pl.BlockSpec((8, n), lambda i: (0, 0))
    wide = rows(width)
    return pl.pallas_call(
        middle_back_kernel,
        grid=(total // BLOCK,),
        in_specs=[
            pl.BlockSpec(memory_space=pl.ANY), rows(gate.shape[1]), wide, wide, line, line, wide, wide, wide, wide
        ],
        out_specs=[wide, wide, rows(2 * width), few(width), few(width), few(2 * width)],
        out_shape=[
            shape_of(total, width, dtype=BF16), shape_of(total, width), shape_of(total, 2 * width, dtype=BF16),
            shape_of(8, width), shape_of(8, width), shape_of(8, 2 * width),
        ],
        cost_estimate=cost(1),
    )(token, gate, branch, source, gain[None], bias[None], mixed, feed, grad, ffn)


def gates_kernel(piece, before, mixed_ref, gates_ref, d_ref):
    grad = dot_tn(mixed_ref[...], gates_ref[...]).astype(BF16)
    half = grad.shape[-1] // 2
    d_ref[0] = grad[:, :half].reshape(d_ref.shape[1:])
    d_ref[1] = grad[:, half:].reshape(d_ref.shape[1:])


def run_gates(which, token, mixed, gates):
    total, width = mixed.shape
    n = which.shape[0]
    block = width // (2 * n)
    return pl.pallas_call(
        gates_kernel,
        grid_spec=pltpu.PrefetchScalarGridSpec(
            num_scalar_prefetch=1,
            grid=(n,),
            in_specs=[
                pl.BlockSpec(memory_space=pl.ANY),
                pl.BlockSpec((total, block), lambda i, p: (0, p[i])),
                pl.BlockSpec(gates.shape, lambda i, p: (0, 0)),
            ],
            out_specs=pl.BlockSpec((2, 1, block, width), lambda i, p: (0, 0, i, 0)),
        ),
        out_shape=shape_of(2, 1, n * block, width, dtype=BF16),
        cost_estimate=cost(1),
    )(which, token, mixed, gates)


class Pieces:
    def __init__(self, gathered, outer, which, tensor, part_f, part_v):
        self.gathered, self.outer, self.which, self.tensor = gathered, outer, which, tensor
        self.part_f, self.part_v = part_f, part_v
        self.width = gathered.shape[-1]

    def units(self, part):
        return self.which.shape[0] * self.tensor * part

    def block(self, part):
        return min(UNITS, self.tensor * part)

    def spec(self, part, row):
        step = self.block(part) // part
        per = self.tensor // step
        return pl.BlockSpec(
            (step, part, self.width), lambda i, p: (p[i // per] * per + i % per, row // part, 0)
        )

    @property
    def w_in(self):
        return self.spec(self.part_f, 0)

    @property
    def w_out(self):
        return self.spec(self.part_f, 0)

    def v(self, k):
        return self.spec(self.part_v, self.part_f + k * self.part_v)


def flat(ref):
    return ref[...].reshape(-1, ref.shape[-1])


def blocked(kernel, micros, pieces, steps, token, in_specs, out_specs, out_shape, *arrays):
    def body(piece, before, *refs):
        kernel(piece, *refs)

    return pl.pallas_call(
        body,
        grid_spec=pltpu.PrefetchScalarGridSpec(
            num_scalar_prefetch=1,
            grid=(steps,),
            in_specs=[pl.BlockSpec(memory_space=pl.ANY), *in_specs],
            out_specs=out_specs,
        ),
        out_shape=out_shape,
        cost_estimate=cost(micros),
    )(pieces.which, token, *arrays)


def block_specs(total, width, block, lead):
    full = pl.BlockSpec((total, width), lambda i, p: (0, 0))
    cols = pl.BlockSpec((total, block), lambda i, p: (0, i))
    line = pl.BlockSpec((1, block), lambda i, p: (0, i))
    grads = pl.BlockSpec((2, lead, block, width // 2), lambda i, p: (0, 0, i, 0))
    return full, cols, line, grads


def run_value(pieces, token, normed, mixed, probs, bv, br):
    total, width = normed.shape
    units, block = pieces.units(pieces.part_v), pieces.block(pieces.part_v)
    full, cols, line, grads = block_specs(total, width, block, 3)
    pairs = pl.BlockSpec(probs.shape, lambda i, p: (0, 0, 0))
    g = pieces.gathered
    return blocked(
        value_kernel, 200, pieces, units // block, token,
        [full, full, pairs, pieces.v(0), pieces.v(1), pieces.v(2), line, line],
        [cols, cols, cols, cols, full],
        [shape_of(total, units)] * 3 + [shape_of(total, units, dtype=BF16), shape_of(total, width)],
        normed, mixed, probs, g, g, g, bv, br,
    )


def run_value_back(pieces, k, micros, token, grad, normed, mixed, probs, kept):
    total, width = normed.shape
    units, block = pieces.units(pieces.part_v), pieces.block(pieces.part_v)
    full, cols, line, grads = block_specs(total, width, block, 3)
    pairs = pl.BlockSpec(probs.shape, lambda i, p: (0, 0, 0))
    g = pieces.gathered
    return blocked(
        value_back_kernel, micros, pieces, units // block, token,
        [
            pl.BlockSpec((total, width), lambda i, p: (0, 1)), full, full, pairs,
            pieces.v(0), pieces.v(1), pieces.v(2), *[pl.BlockSpec((total, block), lambda i, p: (0, k * (units // block) + i))] * 4,
        ],
        [grads, line, line, full, full, pairs],
        [shape_of(2, 3, units, width // 2, dtype=BF16)]
        + [shape_of(1, units)] * 2
        + [shape_of(total, width)] * 2
        + [shape_of(*probs.shape)],
        grad, normed, mixed, probs, g, g, g, *kept,
    )


def run_inner(pieces, token, ffn, grad, bias):
    total, width = ffn.shape
    units, block = pieces.units(pieces.part_f), pieces.block(pieces.part_f)
    full, cols, line, grads = block_specs(total, width, block, 1)
    return blocked(
        inner_kernel, 200, pieces, units // block, token,
        [full, full, pieces.w_in, line],
        [cols, cols, grads],
        [shape_of(total, units), shape_of(total, units, dtype=BF16), shape_of(2, 1, units, width // 2, dtype=BF16)],
        ffn, grad, pieces.gathered, bias,
    )


def run_outer(pieces, token, ffn, grad, pre, activ, *before):
    total, width = ffn.shape
    units, block = pieces.units(pieces.part_f), pieces.block(pieces.part_f)
    full, cols, line, grads = block_specs(total, width, block, 1)
    return blocked(
        outer_kernel, 200, pieces, units // block, token,
        [full, full, pieces.w_in, pieces.w_out, cols, cols, *[full] * len(before)],
        [grads, line, full, full],
        [shape_of(2, 1, units, width // 2, dtype=BF16), shape_of(1, units), shape_of(total, width), shape_of(total, width)],
        ffn, grad, pieces.gathered, pieces.outer, pre, activ, *before,
    )


def call(kernel, outs, scratch, smem, *arrays):
    return pl.pallas_call(
        kernel,
        out_shape=outs,
        in_specs=[pl.BlockSpec(memory_space=pltpu.SMEM)] * smem
        + [pl.BlockSpec(memory_space=pltpu.VMEM)] * (len(arrays) - smem),
        out_specs=jax.tree.map(lambda _: pl.BlockSpec(memory_space=pltpu.VMEM), outs),
        scratch_shapes=scratch,
        cost_estimate=cost(12),
    )(*arrays)


def scan_carry(grid, local, clear, whole, reverse):
    micros, heads = local.shape[:2]
    clear = jnp.broadcast_to(clear[:, None, None, None], (micros, 1, 8, 128))
    entering = jnp.zeros_like(local)
    reach = jnp.ones_like(local)
    total = local
    for mask in grid.tensor:
        got = grid.swap(jnp.concatenate([total, clear], axis=1), mask)
        got_total, got_clear = got[:, :heads], got[:, heads:]
        later = grid.bit(mask) == (0 if reverse else 1)
        entering = jnp.where(later, entering + reach * got_total, entering)
        reach = jnp.where(later, reach * got_clear * whole, reach)
        total = jnp.where(
            later, total + clear * whole * got_total, got_total + got_clear * whole * total
        )
        clear = clear * got_clear
        whole = whole * whole
    return entering


def after(values, *others):
    return lax.optimization_barrier((values, others))[0]


class Term:
    def __init__(self, array, labels, fixed):
        self.array, self.labels, self.fixed = array, labels, fixed


class Reduce:
    def __init__(self, grid, high, dims, still=()):
        self.grid, self.dims, self.still = grid, list(dims), still
        self.labels = ["side", "lead", *self.dims, "u", "h"]
        xs, (lo, *hi) = grid.xs[::-1], grid.tensor
        self.orders = [[*xs, lo], [lo, *xs]], hi[::-1]
        self.step, self.pair = -1, None
        self.high = self.view(high)
        self.raw = [grid.swap(self.high, grid.core)]

    def view(self, v):
        n = len(self.dims)
        return v.reshape(*v.shape[:2], *[2] * n, v.shape[2] >> n, v.shape[3])

    @property
    def steps(self):
        return len(self.orders[0][0]) + len(self.orders[1])

    def add_low(self, low):
        self.low = self.view(low)

    def take(self):
        if self.step < 0:
            self.sides = [[Term(a, self.labels, {"side": s}) for a in (self.low, self.raw[0])] for s in (0, 1)]
            self.left = [list(self.dims), list(self.dims)]
        else:
            for s in (0, 1):
                for t in self.sides[s]:
                    if self.masks[s] in t.labels:
                        t.fixed[self.masks[s]] = 0
                self.left[s] = [d for d in self.left[s] if d != self.masks[s]]
                if len(self.raw) == 2:
                    self.sides[s].append(Term(self.raw[s], ["lead", *self.left[s], "u", "h"], {}))
                elif self.pair is None:
                    self.sides[s].append(Term(self.raw[0], ["lead", *self.left[s], "u", "hh"], {"hh": s}))
                else:
                    names = ["pair", "lead", *self.left[s], "u", "hh"]
                    self.sides[s].append(Term(self.raw[0], names, {"pair": self.pair, "hh": s}))
            self.pair = None
        self.step += 1

    def wanted(self):
        (first, second), hi = self.orders
        k = self.step
        if k == self.steps:
            return [(self.sides[s], {}, self.left[s]) for s in (0, 1)], True
        self.masks = [first[k], second[k]] if k < len(first) else [hi[k - len(first)]] * 2
        return [
            (self.sides[s], {self.masks[s]: 1}, [d for d in self.left[s] if d != self.masks[s]]) for s in (0, 1)
        ], k >= len(first)

    def start(self, sends):
        if len(sends) == 2:
            self.raw = [self.grid.swap(v, m) for v, m in zip(sends, self.masks)]
        else:
            self.raw = [self.grid.swap(sends[0], self.masks[0])]


def place_of(grid, still, fixed, name, sel):
    if name in still:
        masks = [*grid.tensor, *grid.xs]
        return sel[2 * masks.index(name) + fixed[name]]
    return fixed[name]


def picked(grid, still, term, extra, sel):
    v = term.array
    fixed = {**term.fixed, **extra}
    for axis in reversed(range(len(term.labels))):
        name = term.labels[axis]
        if name == "hh":
            half = v.shape[-1] // 2
            v = v[..., fixed[name] * half : (fixed[name] + 1) * half]
        elif name in fixed:
            v = lax.dynamic_index_in_dim(v, place_of(grid, still, fixed, name, sel), axis, False)
    return v.astype(F32)


def point(grid, gates, *sums, behind=None):
    for r in sums:
        r.take()
    outs, tasks = [], []
    for r in sums:
        sides, joined = r.wanted()
        for terms, fixed, left in sides:
            tasks.append((r, terms, fixed, left))
        shapes = []
        for terms, fixed, left in sides:
            low = r.low.shape
            shapes.append((low[1], *[2] * len(left), *low[-2:]))
        if joined:
            outs.append((*shapes[0][:-1], 2 * shapes[0][-1]))
        else:
            outs.extend(shapes)
    pair = [
        k for k in range(len(sums) - 1)
        if 0 < len(sums[k].orders[0][0]) <= sums[k].step < sums[k].steps
        and sums[k].step == sums[k + 1].step and sums[k].low.shape == sums[k + 1].low.shape
    ]
    joined_outs, ranks, k = [], [], 0
    for n, r in enumerate(sums):
        if n - 1 in pair:
            continue
        if n in pair:
            joined_outs.append((2, *outs[k]))
            ranks.append(True)
            k += 2
        else:
            m = 1 if r.step >= len(r.orders[0][0]) else 2
            joined_outs.extend(outs[k : k + m])
            ranks.extend([False] * m)
            k += m
    sel = grid.sel
    fits = all(len(r.dims) <= 4 and r.low.shape[-2] % 32 == 0 for r in sums)
    if fits:
        *values, token = run_point(grid, gates, tasks, joined_outs, ranks, sel)
    else:
        values = []
        sides = [
            sum(picked(grid, r.still, t, {k: v for k, v in fixed.items() if k in t.labels}, sel) for t in terms).astype(BF16)
            for r, terms, fixed, left in tasks
        ]
        for shape in outs:
            v = sides.pop(0)
            values.append(v if v.shape == shape else jnp.concatenate([v, sides.pop(0)], axis=-1))
        for n in pair:
            first = sum(1 if r.step >= len(r.orders[0][0]) else 2 for r in sums[:n]) - sum(m < n for m in pair)
            values[first : first + 2] = [jnp.stack(values[first : first + 2])]
        token = after(jnp.zeros((8, 128), F32), [g[(0,) * g.ndim] for g in gates])
    if behind is not None:
        values, behind = lax.optimization_barrier((values, behind))
    done, skip = [], False
    for k, r in enumerate(sums):
        if skip:
            skip = False
            continue
        if r.step == r.steps:
            done.append(values.pop(0))
        elif k in pair:
            both = grid.swap(values[0], r.masks[0])
            r.raw, r.pair = [both], 0
            sums[k + 1].raw, sums[k + 1].pair = [both], 1
            values, skip = values[1:], True
        else:
            n = 2 if r.step < len(r.orders[0][0]) else 1
            r.start(values[:n])
            values = values[n:]
    if behind is not None:
        return token, behind
    return (token, *done) if done else token


def run_point(grid, gates, tasks, outs, ranks, sel):
    parts = 2
    arrays, specs, layout = [], [], []
    for r, terms, extra, left in tasks:
        mine = []
        for t in terms:
            fixed = {**t.fixed, **{k: v for k, v in extra.items() if k in t.labels}}
            block = []
            for name, size in zip(t.labels, t.array.shape):
                if name == "hh":
                    block.append(size // 2)
                elif name == "u":
                    block.append(size // parts)
                else:
                    block.append(None if name in fixed else size)

            def index(i, p, t=t, fixed=fixed, r=r):
                return tuple(
                    i if name == "u" else place_of(grid, r.still, fixed, name, p) if name in fixed else 0
                    for name in t.labels
                )

            mine.append(len(arrays))
            arrays.append(t.array)
            specs.append(pl.BlockSpec(tuple(block), index))
        layout.append(mine)
    out_specs = []
    for shape in outs:
        block = (*shape[:-2], shape[-2] // parts, shape[-1])
        out_specs.append(pl.BlockSpec(block, lambda i, p, n=len(shape): (*[0] * (n - 2), i, 0)))
    out_specs.append(pl.BlockSpec((8, 128), lambda i, p: (0, 0)))

    def body(p, *refs):
        refs = refs[len(gates) :]
        ins, results = refs[: len(arrays)], refs[len(arrays) :]
        queue = list(layout)
        for ref, rank in zip(results[:-1], ranks):
            for ref in [ref.at[k] for k in (0, 1)] if rank else [ref]:
                first = 0
                while first < ref.shape[-1]:
                    mine = queue.pop(0)
                    total = ins[mine[0]][...].astype(F32)
                    for k in mine[1:]:
                        total = total + ins[k][...].astype(F32)
                    ref[..., first : first + total.shape[-1]] = total.astype(BF16)
                    first += total.shape[-1]
        results[-1][...] = jnp.zeros((8, 128), F32)

    return pl.pallas_call(
        body,
        grid_spec=pltpu.PrefetchScalarGridSpec(
            num_scalar_prefetch=1,
            grid=(parts,),
            in_specs=[pl.BlockSpec(memory_space=pl.ANY)] * len(gates) + specs,
            out_specs=out_specs,
        ),
        out_shape=[shape_of(*shape, dtype=BF16) for shape in outs] + [shape_of(8, 128)],
        cost_estimate=cost(1),
    )(sel, *gates, *arrays)


def ends(result):
    return result if isinstance(result, tuple) else (result,)


def finish(grid, gates, r, value=None):
    while value is None:
        out = point(grid, gates, r)
        value = out[1] if isinstance(out, tuple) else None
    return value


def share_units(grid, part):
    held = part[None]
    masks = [*grid.xs, grid.core]
    for mask in masks:
        held = jnp.concatenate([held, grid.swap(held, mask)], axis=0)
    n = held.shape[0]
    held = held.astype(F32)
    for k, mask in enumerate(masks):
        held = held.reshape(n >> (k + 1), 2, -1, *part.shape)
        held = jnp.where(grid.bit(mask) == 1, held[:, ::-1], held)
    held = held.reshape(n, *part.shape).transpose(1, 0, 2, 3)
    return held.reshape(part.shape[0], -1, part.shape[-1])


def place_kernel(turned, bits, own_ref, x_ref, c_ref, *outs):
    swap_c, swap_x = bits[0] == 1, bits[1] == 1
    outs[-1][...] = jnp.zeros((8, 128), F32)
    for k, turn in enumerate(turned):
        rows = []
        for own, other in ((own_ref[k], x_ref[k]), (c_ref[0, k], c_ref[1, k])):
            own, other = own.astype(F32), other.astype(F32)
            rows.append(jnp.concatenate([jnp.where(swap_x, other, own), jnp.where(swap_x, own, other)], axis=0))
        v = jnp.concatenate(
            [jnp.where(swap_c, rows[1], rows[0]), jnp.where(swap_c, rows[0], rows[1])], axis=0
        )
        outs[k][...] = v.T if turn else v


def share_and_place(grid, parts, turned, zero):
    results = []
    for part, turns in zip(parts, turned):
        if zero is not None:
            part = part + zero
        lead, units, width = part.shape
        if len(grid.xs) > 1 or units % 16:
            rows = share_units(grid, part)
            results.append([r.T if t else r for r, t in zip(rows, turns)])
            continue
        from_x = grid.swap(part, grid.xs[0])
        from_c = grid.swap(jnp.stack([part, from_x]), grid.core)
        results.append(
            pl.pallas_call(
                partial(place_kernel, turns),
                in_specs=[pl.BlockSpec(memory_space=pltpu.SMEM)] + [pl.BlockSpec(memory_space=pltpu.VMEM)] * 3,
                out_specs=[pl.BlockSpec(memory_space=pltpu.VMEM)] * (lead + 1),
                out_shape=[shape_of(*((width, 4 * units) if t else (4 * units, width))) for t in turns] + [shape_of(8, 128)],
                cost_estimate=cost(5),
            )(jnp.stack([grid.bit(grid.core), grid.bit(grid.xs[0])]).astype(jnp.int32), part, from_x, from_c)
        )
    return results


def pack_kernel(
    bits, before, eta0, eta1, one0, one1, two0, two1, omega0, omega1, gain0, gain1, gates_ref, shared_ref, ffn_ref, out_sum_ref,
    v0, v1, r0, r1, i0, i1, packed_ref, rows,
):
    heads = eta0.shape[0]
    n = heads * 8
    for k, (a, b) in enumerate(((eta0, eta1), (one0, one1), (two0, two1))):
        rows[k * n : (k + 1) * n] = (a[...] + b[...]).reshape(n, 128)
    at = 3 * n

    def line(v, at):
        for j in range(v.shape[-1] // 128):
            rows[at + j : at + j + 1] = v[:, j * 128 : (j + 1) * 128]
        return at + v.shape[-1] // 128

    total = lambda v: jnp.sum(v, axis=0, keepdims=True)
    at = line(total(gain0[...] + gain1[...]), at)
    rows[at : at + 8] = omega0[...] + omega1[...]
    at = line(total(gates_ref[...]), at + 8)
    rows[at : at + 1] = shared_ref[3:4]
    rows[at + 1 : at + 4] = shared_ref[0:3]
    at = line(total(ffn_ref[...]), at + 4)
    at = line(total(out_sum_ref[...]), at)
    core, x = bits[0], bits[1]
    tensor = i0.shape[-1] // 256
    for low, high in ((v0, v1), (r0, r1)):
        for k, ref in enumerate((low, high)):
            for t in range(tensor):
                own, other = (ref[:, (q * tensor + t) * 64 : (q * tensor + t + 1) * 64] for q in (0, 1))
                row = jnp.where(
                    x == 0, jnp.concatenate([own, other], axis=1), jnp.concatenate([other, own], axis=1)
                )
                rows[pl.ds(at + 2 * t + (core ^ k), 1), :] = row
        at += 2 * tensor
    for k, ref in enumerate((i0, i1)):
        for q in (0, 1):
            for t in range(tensor):
                row = ref[:, (q * tensor + t) * 128 : (q * tensor + t + 1) * 128]
                rows[pl.ds(at + 4 * t + 2 * (core ^ k) + (x ^ q), 1), :] = row
    at += 4 * tensor
    rows[at:] = jnp.zeros((rows.shape[0] - at, 128), F32)
    packed_ref[...] = rows[...].astype(BF16)


def run_pack(bits, token, sums, count):
    vmem = pl.BlockSpec(memory_space=pltpu.VMEM)
    return pl.pallas_call(
        pack_kernel,
        in_specs=[pl.BlockSpec(memory_space=pltpu.SMEM), pl.BlockSpec(memory_space=pl.ANY)] + [vmem] * len(sums),
        out_specs=vmem,
        out_shape=shape_of(count, 128, dtype=BF16),
        scratch_shapes=[pltpu.VMEM((count, 128), F32)],
        cost_estimate=cost(4),
    )(bits, token, *sums)


def join_kernel(place, left_ref, right_ref, out_ref, token_ref):
    token_ref[...] = jnp.zeros((8, 128), F32)
    n = left_ref.shape[1]
    out_ref[:, :n] = left_ref[...].astype(F32)
    part = right_ref.shape[1]
    count = out_ref.shape[0] // part
    for k in range(count):
        v = right_ref[place[pl.program_id(0) * count + k]]
        out_ref[k * part : (k + 1) * part, n:] = v.astype(F32)


def join(place, left, right):
    rows, n = left.shape
    block = 256
    return pl.pallas_call(
        join_kernel,
        grid_spec=pltpu.PrefetchScalarGridSpec(
            num_scalar_prefetch=1,
            grid=(rows // block,),
            in_specs=[pl.BlockSpec((block, n), lambda i, p: (i, 0)), pl.BlockSpec(right.shape, lambda i, p: (0, 0, 0))],
            out_specs=[
                pl.BlockSpec((block, n + right.shape[2]), lambda i, p: (i, 0)), pl.BlockSpec((8, 128), lambda i, p: (0, 0))
            ],
        ),
        out_shape=[shape_of(rows, n + right.shape[2]), shape_of(8, 128)],
        cost_estimate=cost(50),
    )(place, left, right)


def sum_flat(grid, packed, hold, last_hold, end_hold):
    held = packed.astype(F32)
    masks = [grid.core, *grid.tensor, *grid.xs]
    for mask in masks:
        if mask == masks[-1]:
            held = tied(held, last_hold)
        low = packed if mask == masks[0] else held.astype(BF16)
        held = low.astype(F32) + grid.swap(low, mask).astype(F32)
        if mask == masks[0]:
            held = tied(held, hold)
    return tied(held, end_hold).reshape(-1)


def every_part(grid, part):
    parts = part
    masks = [grid.core, *grid.tensor, *grid.xs]
    for mask in masks:
        parts = jnp.concatenate([parts, grid.swap(parts, mask)])
    devices = jnp.arange(grid.count) ^ grid.index
    place = sum(((devices // mask) % 2) << k for k, mask in enumerate(masks)).astype(jnp.int32)
    return parts.reshape(grid.count, *part.shape), place


def tied(v, token):
    return (v.reshape(-1, 8, 128) + token.astype(v.dtype)).reshape(v.shape)


def padded(v, size):
    return jnp.concatenate([v, jnp.zeros(-v.size % size, F32)])


def local(
    inputs, resets, cotangent, norm_gain, ema_alpha, ema_damp, ema_beta, ema_eta, ema_omega,
    w_gates, b_gates, qk_gain, q_bias, w_value, b_value, w_reset, b_reset, w_branch, ffn_gain,
    w_in, b_in, w_out, b_out,
):
    grid = Grid()
    micros, rows, width = inputs.shape
    total = micros * rows
    heads = ema_alpha.shape[1]
    rank = lax.axis_index("tensor")
    units_v, units_f = w_value.shape[1], w_in.shape[1]
    n_x = 1 << len(grid.xs)
    split_x = n_x == 2
    core, x_at = grid.bit(grid.core), lax.axis_index("dp") // 2

    half_v, half_f = units_v // 2, units_f // 2

    def chunks(w, half, axis, whole):
        size = half // n_x
        picks = range(n_x) if whole else range(1)
        return jnp.concatenate(
            [lax.dynamic_slice_in_dim(w, core * half + (x_at ^ r) * size, size, axis) for r in picks],
            axis=axis,
        )

    n_tensor = lax.axis_size("tensor")
    part_f, part_v = half_f // n_x, half_v // n_x
    own = lambda w, half, axis: chunks(w, half, axis, False)
    bias = jnp.concatenate([own(b_value, half_v, 0), own(b_reset, half_v, 0), own(b_in, half_f, 0)])
    bias = jnp.zeros((8, width), BF16).at[0, : bias.size].set(bias)
    seed = jnp.concatenate(
        [
            own(w_in, half_f, 1).T, own(w_value, half_v, 1).T, own(w_reset, half_v, 1).T, own(w_branch, half_v, 0),
            bias,
        ]
    )
    gathered = lax.all_gather(seed, AXES, axis=0)
    gathered_out = lax.all_gather(own(w_out, half_f, 0), AXES, axis=0)
    which = [
        jnp.stack([(x_at ^ r) * 2 + c for r in range(n_x)]).astype(jnp.int32) for c in (core, 1 - core)
    ]
    pieces = [Pieces(gathered, gathered_out, w, n_tensor, part_f, part_v) for w in which]
    table = gathered[:, part_f + 3 * part_v].astype(F32).reshape(2 * n_x, n_tensor, width)
    tables = [jnp.stack([lax.dynamic_index_in_dim(table, w[r], 0, False) for r in range(n_x)]) for w in which]
    bias_v = [t[..., :part_v].reshape(1, -1) for t in tables]
    bias_r = [t[..., part_v : 2 * part_v].reshape(1, -1) for t in tables]
    bias_i = [t[..., 2 * part_v : 2 * part_v + part_f].reshape(1, -1) for t in tables]
    dims = [*grid.xs[::-1], *grid.tensor[::-1]]
    still = grid.tensor

    def in_place(low, high):
        d = [grid.core, *dims]
        v = jnp.stack([low, high]).reshape(*[2] * len(d), -1)
        for axis, mask in enumerate(d):
            if mask not in still:
                v = jnp.where(grid.bit(mask) == 1, jnp.flip(v, axis), v)
        want = [*grid.tensor[::-1], grid.core, *grid.xs[::-1]]
        return v.transpose(*[d.index(m) for m in want], len(d)).reshape(-1)

    offsets = rank * rows + jnp.arange(rows)
    flags = jnp.where(offsets[None] == 0, 1, resets).astype(jnp.int32)
    sel = jnp.stack([grid.bit(m) ^ i for m in [*grid.tensor, *grid.xs] for i in (0, 1)]).astype(jnp.int32)
    places = [jnp.stack([2 * x + c for x in range(n_x)]).astype(jnp.int32) for c in (core, 1 - core)]
    flags, grid.sel, places, which = lax.optimization_barrier((flags, sel, places, which))
    for p, w in zip(pieces, which):
        p.which = w
    tile = lambda a: a.T.reshape(heads, 8, 128)
    decay = tile(1.0 - ema_alpha * ema_damp)
    feed = tile(ema_alpha * ema_beta)
    tell = tile(ema_eta)
    whole = jnp.exp(rows * jnp.log(decay))[None]
    clear = (jnp.sum(flags, axis=1) == 0).astype(F32)
    source_low = inputs.reshape(total, width)
    laid = jax.ShapeDtypeStruct((total * 8, 128), F32)
    wide = jax.ShapeDtypeStruct((total, width), F32)
    wide_low = jax.ShapeDtypeStruct((total, width), BF16)
    states = jax.ShapeDtypeStruct((micros, heads, 8, 128), F32)
    sums = jax.ShapeDtypeStruct((heads, 8, 128), F32)
    normed_laid, normed_low, final = call(
        norm_kernel, (laid, wide_low, states), [], 1,
        flags, source_low, norm_gain[None], decay, feed,
    )
    start = scan_carry(grid, final, clear, whole, False)
    blended, mixed_low = call(
        blend_kernel, (wide, wide_low), [pltpu.VMEM((total * 8, 128), F32)], 1,
        flags, normed_laid, start, decay, feed, tell, ema_omega.reshape(8, 128),
    )

    source = source_low.astype(F32)
    gate_pre = dot_plain(mixed_low, w_gates) + b_gates
    update = jax.nn.sigmoid(gate_pre[:, :width])
    direct = gate_pre[:, width : 2 * width]
    shared_pre = gate_pre[:, 2 * width :]
    shared = rounded(jax.nn.silu(shared_pre))
    query = (shared * qk_gain[0] + q_bias).astype(BF16)
    key = (shared * qk_gain[1]).astype(BF16)
    blocks = total // BLOCK
    doc = jnp.cumsum(flags.reshape(blocks, BLOCK), axis=1)
    order = jnp.arange(BLOCK)
    allowed = (doc[:, :, None] == doc[:, None, :]) & (order[:, None] >= order[None, :])[None]
    score_scale = query.shape[-1] ** (-0.5)
    query_b, key_b = query.reshape(blocks, BLOCK, -1), key.reshape(blocks, BLOCK, -1)
    scores = jnp.einsum("cik,cjk->cij", query_b, key_b, preferred_element_type=F32) * score_scale
    scores = jnp.where(allowed, scores, -1000000000.0)
    probs = jax.nn.softmax(scores, axis=-1)
    probs_low = probs.astype(BF16)

    both = Pieces(gathered, gathered_out, jnp.concatenate(which), n_tensor, part_f, part_v)
    bias_v, bias_r = jnp.concatenate(bias_v, axis=1), jnp.concatenate(bias_r, axis=1)
    *kept, branch = run_value(both, bias_v, normed_low, mixed_low, probs_low, bias_v, bias_r)
    mixed_out, ffn_low = run_middle(gate_pre, branch, source_low, ffn_gain)
    grad_low = cotangent.reshape(total, width)

    inner = [None, None]
    inner[1] = run_inner(pieces[1], bias_i[1], ffn_low, grad_low, bias_i[1])
    r_out = Reduce(grid, inner[1][2], dims, still)
    inner[0] = run_inner(pieces[0], inner[1][1], ffn_low, grad_low, bias_i[0])
    r_out.add_low(inner[0][2])
    token, gathered_out = point(grid, [], r_out, behind=gathered_out)
    for p in pieces:
        p.outer = gathered_out
    sum_in = [None, None]
    d_high, sum_in[1], feed_out, grad_ffn = run_outer(
        pieces[1], token, ffn_low, grad_low, inner[1][0], inner[1][1]
    )
    r_in = Reduce(grid, d_high, dims, still)
    token = point(grid, [sum_in[1]], r_out)
    d_low, sum_in[0], feed_out, grad_ffn = run_outer(
        pieces[0], token, ffn_low, grad_low, inner[0][0], inner[0][1], feed_out, grad_ffn
    )
    r_in.add_low(d_low)
    token = point(grid, [], r_out, r_in)
    output, grad_source, grad_gates_low, sum_ffn_gain, sum_out, sum_gates = run_middle_back(
        token, gate_pre, branch, source_low, ffn_gain, b_out, mixed_out, feed_out, grad_low, grad_ffn
    )
    bits = [*grid.xs[::-1], grid.core, *grid.tensor[::-1]]
    dims_g = [m for m in bits if m != grid.core]
    if width // (2 * n_x) % 128 == 0:
        d_gates = [None, None]
        d_gates[1] = run_gates(places[1], sum_gates, mixed_low, grad_gates_low)
        r_gates = Reduce(grid, d_gates[1], dims_g, dims_g)
        d_gates[0] = run_gates(places[0], d_gates[1], mixed_low, grad_gates_low)
        r_gates.add_low(d_gates[0])
        token = d_gates[0]
    else:
        c_axis = bits.index(grid.core)
        d_gates = [
            dot_over_rows(mixed_low, side).astype(BF16).reshape(*[2] * len(bits), -1, width)
            for side in (grad_gates_low[:, :width], grad_gates_low[:, width:])
        ]
        half_of = lambda i: jnp.stack(
            [lax.dynamic_index_in_dim(d, i, c_axis, False).reshape(1, width // 2, width) for d in d_gates]
        )
        r_gates = Reduce(grid, half_of(1 - core), dims_g, dims_g)
        r_gates.add_low(half_of(core))
        token = sum_gates

    def run_vb(k, token):
        return run_value_back(
            pieces[k], k, 200 if k == 0 else 1, token, grad_gates_low, normed_low, mixed_low, probs_low, kept
        )

    back = [None, None]
    back[1] = run_vb(1, token)
    r_v = Reduce(grid, back[1][0], dims, still)
    token = point(grid, [back[1][1], *r_out.raw], r_in, r_gates)
    back[0] = run_vb(0, token)
    r_v.add_low(back[0][0])
    token = point(grid, [back[0][1]], r_v, r_gates, r_in)
    grad_laid, left, grad_shared_low, sums_shared = run_shared(
        token, flags, back[0][5], back[1][5], probs, query, key, shared, shared_pre, qk_gain, grad_gates_low, w_gates,
        back[0][3], back[1][3], blended, decay, tell,
    )
    token = point(grid, [left, *r_in.raw], r_gates)
    left = left + token
    d_shared = dot_over_rows(mixed_low, tied(grad_shared_low, token))
    d_shared = d_shared.reshape(*[2] * len(bits), -1, d_shared.shape[-1])

    def fold(v, mask):
        axis, here = bits.index(mask), grid.bit(mask)
        got = grid.swap(lax.dynamic_slice_in_dim(v, 1 - here, 1, axis).astype(BF16), mask)
        return lax.dynamic_slice_in_dim(v, here, 1, axis) + got.astype(F32)

    right = scan_carry(grid, left, clear, whole, True)
    t_first, *t_rest = grid.tensor
    for mask in [grid.core, *grid.xs, t_first]:
        d_shared = fold(d_shared, mask)
    token = point(grid, [right], r_v, r_gates, r_in, r_out)
    d_shared = fold(tied(d_shared, token) if d_shared.shape[-2] % 8 == 0 else d_shared, t_rest[0])
    column = shape_of(8, 128)
    results = []
    for m in range(micros):
        part = slice(m * rows, (m + 1) * rows)
        laid_part = slice(m * rows * 8, (m + 1) * rows * 8)
        results.append(
            run_back(
                m, token, flags, normed_laid, grad_laid, start, right, decay, feed, tell, ema_omega.reshape(8, 128),
                back[0][4], back[1][4], source_low, grad_source, norm_gain[None],
            )
        )
        if m == 0:
            token, *done = ends(point(grid, [results[0][1]], r_gates, r_in, r_out, r_v))
            d_shared = tied(d_shared, token) if d_shared.shape[-2] % 8 == 0 else d_shared
            for mask in t_rest[1:]:
                d_shared = fold(d_shared, mask)
    done_gates = finish(grid, [token], r_gates, *done[:1])
    done_in = finish(grid, [token], r_in, *done[1:2])
    done_out = finish(grid, [token], r_out, *done[2:])
    token_v = point(grid, [results[-1][1]], r_v)
    token_w, *done_v = ends(point(grid, [token_v], r_v))
    done_v = finish(grid, [token_w], r_v, *done_v)
    grad_w_out, grad_w_in = share_and_place(grid, [done_out, done_in], [(False,), (True,)], None)
    grad_w_out, grad_w_in = grad_w_out[0], grad_w_in[0]
    grad_w_gates = lax.all_gather(
        done_gates.reshape(width // grid.count, 2 * width), AXES, axis=0, tiled=True
    )

    z = token_v[0, 0]
    part = d_shared.reshape(width // grid.count, -1)
    part = tied(part, token_w) if part.shape[0] % 8 == 0 else part
    sizes_late = [heads * width] * 3 + [width, width]
    sizes_early = [2 * width + 128, 256, 128, width, width, units_v * n_tensor, units_v * n_tensor, units_f * n_tensor]
    count = -(-sum(sizes_late + sizes_early) // 2048) * 16
    if (part_v, part_f, n_x) == (64, 128, 2):
        by_kind = [r[k] for k in range(1, 4) for r in results]
        packed = run_pack(
            jnp.stack([core, x_at]).astype(jnp.int32), token_v,
            [
                *by_kind, *[r[4] for r in results], *[r[5] for r in results], sum_gates, sums_shared, sum_ffn_gain, sum_out,
                back[0][2], back[1][2], back[0][1], back[1][1], *sum_in,
            ],
            count,
        )
    else:
        spread_in = lambda k: in_place(back[0][k] + z, back[1][k] + z)
        both = [sum(r[k] + z for r in results) for k in range(1, 6)]
        small = [
            *[v.reshape(-1) for v in both[:3]], jnp.sum(both[4], axis=0), both[3].reshape(-1), jnp.sum(sum_gates + z, axis=0),
            sums_shared[3] + z, sums_shared[:2].reshape(-1) + z, sums_shared[2] + z, jnp.sum(sum_ffn_gain + z, axis=0),
            jnp.sum(sum_out + z, axis=0), spread_in(2), spread_in(1), in_place(sum_in[0] + z, sum_in[1] + z),
        ]
        packed = padded(jnp.concatenate(small), count * 128).reshape(-1, 128).astype(BF16)

    def cut_like(v, sizes):
        out, first = [], 0
        for n in sizes:
            out.append(v[first : first + n])
            first += n
        return out

    ((grad_w_branch, grad_w_reset, grad_w_value, *placed),) = share_and_place(grid, [done_v], [(False, True, True)], None)
    parts, place = every_part(grid, part.astype(BF16))
    grad_w_gates, token_j = join(place, grad_w_gates, parts)
    summed = sum_flat(grid, packed, token_w, placed[0] if placed else token_w, token_j)
    last, cut = cut_like(summed, sizes_late), cut_like(summed[sum(sizes_late) :], sizes_early)
    untile = lambda v: v.reshape(heads, width).T
    eta, one, two = (untile(v) for v in last[:3])
    mine = lambda v, n: lax.dynamic_slice_in_dim(v, rank * n, n, 0)
    return (
        output.reshape(inputs.shape),
        jnp.stack([r[0] + z for r in results]),
        last[3],
        ema_beta * one - ema_damp * two,
        -ema_alpha * two,
        ema_alpha * one,
        eta,
        last[4],
        grad_w_gates,
        cut[0],
        cut[1].reshape(2, -1),
        cut[2],
        grad_w_value,
        mine(cut[5], units_v),
        grad_w_reset,
        mine(cut[6], units_v),
        grad_w_branch,
        cut[3],
        grad_w_in,
        mine(cut[7], units_f),
        grad_w_out,
        cut[4],
    )


def solution(mesh):
    rows = P(None, AXES, None)
    col, row, vec, rep = P(None, "tensor"), P("tensor", None), P("tensor"), P()
    return jax.shard_map(
        local,
        mesh=mesh,
        in_specs=(
            rows, P(None, AXES), rows, rep, rep, rep, rep, rep, rep, rep, rep, rep, rep,
            col, vec, col, vec, row, rep, col, vec, row, rep,
        ),
        out_specs=(
            rows, rows, rep, rep, rep, rep, rep, rep, rep, rep, rep, rep,
            col, vec, col, vec, row, rep, col, vec, row, rep,
        ),
        check_vma=False,
    )
```

```python
from functools import partial

import jax
import jax.numpy as jnp
from jax import lax
from jax.experimental import pallas as pl
from jax.experimental.pallas import tpu as pltpu
from jax.sharding import PartitionSpec as P

BLOCK = 128
HIGHEST = lax.Precision.HIGHEST
EPSILON = 1e-06
AXES = ("dp", "tensor")
F32 = jnp.float32
BF16 = jnp.bfloat16


def dot_plain(a, b):
    return jnp.dot(a, b, preferred_element_type=F32)


def dot_against(a, b):
    return lax.dot_general(a, b, (((1,), (1,)), ((), ())), preferred_element_type=F32)


def dot_over_rows(a, b):
    return lax.dot_general(a, b, (((0,), (0,)), ((), ())), preferred_element_type=F32)


def rounded(v):
    return lax.reduce_precision(v, exponent_bits=8, mantissa_bits=7)


def silu_slope(v):
    s = jax.nn.sigmoid(v)
    return s * (1.0 + v * (1.0 - s))


class Grid:
    def __init__(self):
        dp, tensor = lax.axis_size("dp"), lax.axis_size("tensor")
        self.count = dp * tensor
        self.index = lax.axis_index("dp") * tensor + lax.axis_index("tensor")
        masks = lambda n, first: [first << k for k in range(n.bit_length() - 1)]
        self.tensor = masks(tensor, 1)
        self.core, *self.xs = masks(dp, tensor)

    def bit(self, mask):
        return (self.index // mask) % 2

    def swap(self, value, mask):
        return lax.ppermute(value, AXES, [(i, i ^ mask) for i in range(self.count)])


def ema_step(state, row, keep, decay, feed):
    return [(s * keep) * q + f * row for s, q, f in zip(state, decay, feed)]


def row_of(ref, base, r):
    return ref[pl.ds(base + r, 8, stride=8), :]


def spread(ref, block, values):
    for j in range(8):
        ref[pl.ds(pl.multiple_of(block * 64, 64) + 8 * j, 8), :] = values[:, j * 128 : (j + 1) * 128]


def collect(ref, block):
    return jnp.concatenate(
        [ref[pl.ds(pl.multiple_of(block * 64, 64) + 8 * j, 8), :] for j in range(8)], axis=1
    )


def norm_kernel(flags, x_ref, gain_ref, decay_ref, feed_ref, normed_ref, low_ref, final_ref):
    micros, rows = flags.shape
    heads = decay_ref.shape[0]

    def norm_block(b, carry):
        at = pl.ds(pl.multiple_of(b * 16, 16), 16)
        x = x_ref[at, :].astype(F32)
        n = x * lax.rsqrt(jnp.mean(x * x, axis=-1, keepdims=True) + EPSILON) * gain_ref[...]
        low_ref[at, :] = n.astype(BF16)
        spread(normed_ref, 2 * b, n[:8])
        spread(normed_ref, 2 * b + 1, n[8:])
        return carry

    lax.fori_loop(0, micros * rows // 16, norm_block, 0)
    for m in range(micros):
        for h0 in range(0, heads, 8):
            decay = [decay_ref[h0 + h] for h in range(8)]
            feed = [feed_ref[h0 + h] for h in range(8)]

            def block(b, state, m=m, decay=decay, feed=feed):
                base = pl.multiple_of((m * (rows // 8) + b) * 64, 64)
                for r in range(8):
                    keep = (1 - flags[m, b * 8 + r]).astype(F32)
                    state = ema_step(state, row_of(normed_ref, base, r), keep, decay, feed)
                return state

            state = lax.fori_loop(0, rows // 8, block, [jnp.zeros((8, 128), F32)] * 8)
            for h in range(8):
                final_ref[m, h0 + h] = state[h]


def blend_kernel(
    flags, normed_ref, start_ref, decay_ref, feed_ref, out_ref, omega_ref, blended_ref, low_ref, acc_ref
):
    micros, rows = flags.shape
    heads = decay_ref.shape[0]
    omega = omega_ref[...]
    for m in range(micros):
        for h0 in range(0, heads, 8):
            decay = [decay_ref[h0 + h] for h in range(8)]
            feed = [feed_ref[h0 + h] for h in range(8)]
            tell = [out_ref[h0 + h] for h in range(8)]

            def block(b, state, m=m, h0=h0, decay=decay, feed=feed, tell=tell):
                base = pl.multiple_of((m * (rows // 8) + b) * 64, 64)
                for r in range(8):
                    keep = (1 - flags[m, b * 8 + r]).astype(F32)
                    row = row_of(normed_ref, base, r)
                    state = ema_step(state, row, keep, decay, feed)
                    told = [s * t for s, t in zip(state, tell)]
                    while len(told) > 1:
                        told = [told[i] + told[i + 1] for i in range(0, len(told), 2)]
                    at = pl.ds(base + r, 8, stride=8)
                    if h0 == 0:
                        acc_ref[at, :] = told[0] + omega * row
                    else:
                        acc_ref[at, :] = acc_ref[at, :] + told[0]
                return state

            lax.fori_loop(0, rows // 8, block, [start_ref[m, h0 + h] for h in range(8)])

    def finish(b, carry):
        at = pl.ds(pl.multiple_of(b * 16, 16), 16)
        v = jnp.concatenate([collect(acc_ref, 2 * b), collect(acc_ref, 2 * b + 1)], axis=0)
        blended_ref[at, :] = v
        low_ref[at, :] = (v / (1.0 + jnp.exp(-v))).astype(BF16)
        return carry

    lax.fori_loop(0, micros * rows // 16, finish, 0)


def shared_kernel(
    before, flags, gp0_ref, gp1_ref, probs_ref, query_ref, key_ref, shared_ref, pre_ref, gain_ref, gates_ref, weight_ref,
    mix0_ref, mix1_ref, blended_ref, decay_ref, tell_ref,
    rows_ref, left_ref, low_ref, sums_ref,
):
    b = pl.program_id(0)
    width = mix0_ref.shape[-1]
    probs = probs_ref[0]
    grad_probs = gp0_ref[0] + gp1_ref[0]
    scale = query_ref.shape[-1] ** (-0.5)
    grad_scores = probs * (grad_probs - jnp.sum(grad_probs * probs, axis=-1, keepdims=True)) * scale
    exact = partial(lax.dot_general, precision=HIGHEST, preferred_element_type=F32)
    grad_query = exact(grad_scores, key_ref[...].astype(F32), (((1,), (0,)), ((), ())))
    grad_key = exact(grad_scores, query_ref[...].astype(F32), (((0,), (0,)), ((), ())))
    shared = shared_ref[...]
    pre = pre_ref[...]
    grad_pre = (grad_query * gain_ref[0:1] + grad_key * gain_ref[1:2]) * slope(pre, sigmoid(pre))
    low = grad_pre.astype(BF16)
    low_ref[...] = low
    total = lambda v: jnp.sum(v, axis=0, keepdims=True)
    part = jnp.concatenate(
        [
            total(grad_query * shared), total(grad_key * shared), total(grad_query), total(low.astype(F32)),
            jnp.zeros((4, low.shape[-1]), F32),
        ]
    )
    add_to(sums_ref, part)
    mixed = (
        mix0_ref[...]
        + mix1_ref[...]
        + dot_nt(gates_ref[...], weight_ref[:, : 2 * width])
        + dot_nt(low, weight_ref[:, 2 * width :])
    )
    v = blended_ref[...]
    grad = mixed * slope(v, sigmoid(v))
    for i in range(BLOCK // 8):
        spread(rows_ref, b * (BLOCK // 8) + i, grad[8 * i : 8 * i + 8])

    @pl.when(b == pl.num_programs(0) - 1)
    def _():
        micros, rows = flags.shape
        heads = decay_ref.shape[0]
        for m in range(micros):
            for h0 in range(0, heads, 8):
                decay = [decay_ref[h0 + h] for h in range(8)]
                tell = [tell_ref[h0 + h] for h in range(8)]

                def block(i, left, m=m, decay=decay, tell=tell):
                    b = rows // 8 - 1 - i
                    base = pl.multiple_of((m * (rows // 8) + b) * 64, 64)
                    for r in reversed(range(8)):
                        keep = (1 - flags[m, b * 8 + r]).astype(F32)
                        row = row_of(rows_ref, base, r)
                        left = [((t * row + k) * keep) * q for k, q, t in zip(left, decay, tell)]
                    return left

                left = lax.fori_loop(0, rows // 8, block, [jnp.zeros((8, 128), F32)] * 8)
                for h in range(8):
                    left_ref[m, h0 + h] = left[h]


def run_shared(token, flags, gp0, gp1, probs, query, key, shared, pre, gain, gates, weight, mix0, mix1, blended, decay, tell):
    total, width = mix0.shape
    z = query.shape[1]
    rows = lambda n: pl.BlockSpec((BLOCK, n), lambda b: (b, 0))
    pair = pl.BlockSpec((1, BLOCK, BLOCK), lambda b: (b, 0, 0))
    whole = lambda a: pl.BlockSpec(a.shape, lambda b: (0,) * a.ndim)
    micros, heads = flags.shape[0], decay.shape[0]
    return pl.pallas_call(
        shared_kernel,
        grid=(total // BLOCK,),
        in_specs=[
            pl.BlockSpec(memory_space=pl.ANY), pl.BlockSpec(memory_space=pltpu.SMEM), pair, pair, pair, rows(z), rows(z), rows(z), rows(z), whole(gain),
            rows(2 * width), whole(weight), rows(width), rows(width), rows(width), whole(decay), whole(tell),
        ],
        out_specs=[
            pl.BlockSpec((total * 8, 128), lambda b: (0, 0)),
            pl.BlockSpec((micros, heads, 8, 128), lambda b: (0, 0, 0, 0)),
            rows(z),
            pl.BlockSpec((8, z), lambda b: (0, 0)),
        ],
        out_shape=[
            shape_of(total * 8, 128), shape_of(micros, heads, 8, 128), shape_of(total, z, dtype=BF16), shape_of(8, z),
        ],
        cost_estimate=cost(200),
    )(token, flags, gp0, gp1, probs, query, key, shared, pre, gain, gates, weight, mix0, mix1, blended, decay, tell)


def back_kernel(
    m, before, flags, normed_ref, rows_ref, start_ref, right_ref, decay_ref, feed_ref, tell_ref, omega_ref,
    add0_ref, add1_ref, source_ref, base_ref, gain_ref,
    grad_ref, eta_ref, one_ref, two_ref, omega_out, gain_out, token_ref, states, acc_ref,
):
    rows = flags.shape[1]
    heads = decay_ref.shape[0]
    group = 4
    omega = omega_ref[...]
    zero = jnp.zeros((8, 128), F32)
    token_ref[...] = zero
    for h0 in range(0, heads, group):
        decay = [decay_ref[h0 + h] for h in range(group)]
        feed = [feed_ref[h0 + h] for h in range(group)]
        tell = [tell_ref[h0 + h] for h in range(group)]

        def ahead(b, state, decay=decay, feed=feed):
            base = pl.multiple_of(b * 64, 64)
            for r in range(8):
                keep = (1 - flags[m, b * 8 + r]).astype(F32)
                for h in range(group):
                    states[b * 8 + r, h] = state[h]
                state = ema_step(state, row_of(normed_ref, base, r), keep, decay, feed)
            return state

        last = lax.fori_loop(0, rows // 8, ahead, [start_ref[0, h0 + h] for h in range(group)])

        def back(i, carry, h0=h0, decay=decay, feed=feed, tell=tell):
            left, after_state, eta, one, two, with_omega = carry
            b = rows // 8 - 1 - i
            base = pl.multiple_of(b * 64, 64)
            for r in reversed(range(8)):
                keep = (1 - flags[m, b * 8 + r]).astype(F32)
                g = row_of(rows_ref, base, r)
                x = row_of(normed_ref, base, r)
                earlier = [states[b * 8 + r, h] for h in range(group)]
                eta = [e + s * g for e, s in zip(eta, after_state)]
                now = [t * g + k for t, k in zip(tell, left)]
                one = [o + n * x for o, n in zip(one, now)]
                kept = [n * keep for n in now]
                two = [w + k * s for w, k, s in zip(two, kept, earlier)]
                left = [k * q for k, q in zip(kept, decay)]
                gn = [n * f for n, f in zip(now, feed)]
                while len(gn) > 1:
                    gn = [gn[i] + gn[i + 1] for i in range(0, len(gn), 2)]
                at = pl.ds(base + r, 8, stride=8)
                if h0 == 0:
                    acc_ref[at, :] = gn[0] + omega * g
                    with_omega = with_omega + g * x
                else:
                    acc_ref[at, :] = acc_ref[at, :] + gn[0]
                after_state = earlier
            return left, after_state, eta, one, two, with_omega

        right = [right_ref[0, h0 + h] for h in range(group)]
        nothing = [zero] * group
        _, _, eta, one, two, with_omega = lax.fori_loop(
            0, rows // 8, back, (right, last, nothing, nothing, nothing, zero)
        )
        if h0 == 0:
            omega_out[...] = with_omega
        for h in range(group):
            eta_ref[h0 + h] = eta[h]
            one_ref[h0 + h] = one[h]
            two_ref[h0 + h] = two[h]

    def finish(b, gained):
        at = pl.ds(pl.multiple_of(b * 16, 16), 16)
        x = source_ref[at, :].astype(F32)
        scale = lax.rsqrt(jnp.mean(x * x, axis=-1, keepdims=True) + EPSILON)
        scaled = x * scale
        grad = jnp.concatenate([collect(acc_ref, 2 * b), collect(acc_ref, 2 * b + 1)], axis=0)
        grad = grad + add0_ref[at, :] + add1_ref[at, :]
        own = grad * scaled
        gained = gained + own[:8] + own[8:]
        inner = grad * gain_ref[...]
        mean = jnp.mean(inner * scaled, axis=-1, keepdims=True)
        grad_ref[at, :] = base_ref[at, :] + scale * (inner - scaled * mean)
        return gained

    width = source_ref.shape[-1]
    gain_out[...] = lax.fori_loop(0, rows // 16, finish, jnp.zeros((8, width), F32))


def run_back(m, token, flags, laid, grads, start, right, decay, feed, tell, omega, add0, add1, source, base, gain):
    rows, heads = flags.shape[1], decay.shape[0]
    width = source.shape[1]
    whole = lambda a: pl.BlockSpec(a.shape, lambda i: (0,) * a.ndim)
    tall = pl.BlockSpec((rows * 8, 128), lambda i: (m, 0))
    carry = pl.BlockSpec((1, heads, 8, 128), lambda i: (m, 0, 0, 0))
    wide = pl.BlockSpec((rows, width), lambda i: (m, 0))
    sums = pl.BlockSpec((heads, 8, 128), lambda i: (0, 0, 0))
    return pl.pallas_call(
        partial(back_kernel, m),
        grid=(1,),
        in_specs=[
            pl.BlockSpec(memory_space=pl.ANY), pl.BlockSpec(memory_space=pltpu.SMEM), tall, tall, carry, carry,
            whole(decay), whole(feed), whole(tell), whole(omega), wide, wide, wide, wide, whole(gain),
        ],
        out_specs=[
            pl.BlockSpec((rows, width), lambda i: (0, 0)), sums, sums, sums,
            pl.BlockSpec((8, 128), lambda i: (0, 0)), pl.BlockSpec((8, width), lambda i: (0, 0)),
            pl.BlockSpec((8, 128), lambda i: (0, 0)),
        ],
        out_shape=[
            jax.ShapeDtypeStruct((rows, width), F32),
            *[jax.ShapeDtypeStruct((heads, 8, 128), F32)] * 3,
            jax.ShapeDtypeStruct((8, 128), F32),
            jax.ShapeDtypeStruct((8, width), F32),
            jax.ShapeDtypeStruct((8, 128), F32),
        ],
        scratch_shapes=[pltpu.VMEM((rows, 4, 8, 128), F32), pltpu.VMEM((rows * 8, 128), F32)],
        cost_estimate=cost(200),
    )(token, flags, laid, grads, start, right, decay, feed, tell, omega, add0, add1, source, base, gain)


def dot_tn(a, b):
    return lax.dot_general(a, b, (((0,), (0,)), ((), ())), preferred_element_type=F32)


def dot_nt(a, b):
    return lax.dot_general(a, b, (((1,), (1,)), ((), ())), preferred_element_type=F32)


def dot_nn(a, b):
    return lax.dot_general(a, b, (((1,), (0,)), ((), ())), preferred_element_type=F32)


def sigmoid(v):
    return 1.0 / (1.0 + jnp.exp(-v))


def slope(v, s):
    return s * (1.0 + v * (1.0 - s))


def add_to(ref, value, first_ref=None):
    first = pl.program_id(0) == 0

    @pl.when(first)
    def _():
        ref[...] = value if first_ref is None else first_ref[...] + value

    @pl.when(jnp.logical_not(first))
    def _():
        ref[...] = ref[...] + value


def put_sides(ref, lead, v):
    half = v.shape[-1] // 2
    v = v.astype(BF16)
    ref[0, lead] = v[:, :half]
    ref[1, lead] = v[:, half:]


def value_kernel(
    piece, normed_ref, mixed_ref, probs_ref, wv_ref, wr_ref, wb_ref, bv_ref, br_ref,
    value_ref, reset_ref, attended_ref, gated_ref, out_ref,
):
    value_pre = dot_nt(normed_ref[...], flat(wv_ref)) + bv_ref[...]
    value_ref[...] = value_pre
    value = (value_pre * sigmoid(value_pre)).astype(BF16)
    blocks = probs_ref.shape[0]
    attended = jnp.concatenate(
        [dot_nn(probs_ref[b], value[b * BLOCK : (b + 1) * BLOCK]) for b in range(blocks)], axis=0
    )
    attended_ref[...] = attended
    reset_pre = dot_nt(mixed_ref[...], flat(wr_ref)) + br_ref[...]
    reset_ref[...] = reset_pre
    gated = (reset_pre * sigmoid(reset_pre) * attended).astype(BF16)
    gated_ref[...] = gated
    add_to(out_ref, dot_nn(gated, flat(wb_ref)))


def value_back_kernel(
    piece, grad_ref, normed_ref, mixed_ref, probs_ref, wv_ref, wr_ref, wb_ref,
    value_ref, reset_ref, attended_ref, gated_ref,
    d_ref, sum_r_ref, sum_v_ref, mixed_out, normed_out, probs_out,
):
    grad = grad_ref[...]
    grad_gated = dot_nt(grad, flat(wb_ref))
    put_sides(d_ref, 0, dot_tn(gated_ref[...], grad))
    reset_pre = reset_ref[...]
    s = sigmoid(reset_pre)
    grad_attended = (grad_gated * (reset_pre * s)).astype(BF16)
    grad_reset = (grad_gated * attended_ref[...] * slope(reset_pre, s)).astype(BF16)
    sum_r_ref[...] = jnp.sum(grad_reset.astype(F32), axis=0, keepdims=True)
    mixed = mixed_ref[...]
    put_sides(d_ref, 1, dot_tn(grad_reset, mixed))
    add_to(mixed_out, dot_nn(grad_reset, flat(wr_ref)))
    value_pre = value_ref[...]
    s = sigmoid(value_pre)
    value = (value_pre * s).astype(BF16)
    blocks = probs_ref.shape[0]
    grad_value, grad_probs = [], []
    for b in range(blocks):
        rows = slice(b * BLOCK, (b + 1) * BLOCK)
        grad_probs.append(dot_nt(grad_attended[rows], value[rows])[None])
        grad_value.append(dot_tn(probs_ref[b], grad_attended[rows]))
    add_to(probs_out, jnp.concatenate(grad_probs, axis=0))
    grad_value = (jnp.concatenate(grad_value, axis=0) * slope(value_pre, s)).astype(BF16)
    sum_v_ref[...] = jnp.sum(grad_value.astype(F32), axis=0, keepdims=True)
    put_sides(d_ref, 2, dot_tn(grad_value, normed_ref[...]))
    add_to(normed_out, dot_nn(grad_value, flat(wv_ref)))


def inner_kernel(piece, ffn_ref, grad_ref, wi_ref, bi_ref, pre_ref, activ_ref, do_ref):
    wi = flat(wi_ref)
    pre = dot_nt(ffn_ref[...], wi) + bi_ref[...]
    pre_ref[...] = pre
    activ = (pre * sigmoid(pre)).astype(BF16)
    activ_ref[...] = activ
    put_sides(do_ref, 0, dot_tn(activ, grad_ref[...]))


def outer_kernel(
    piece, ffn_ref, grad_ref, wi_ref, wo_ref, pre_ref, activ_ref, *rest
):
    *sums, di_ref, sum_i_ref, out_ref, ffn_out = rest
    sum_o_ref, sum_f_ref = sums if sums else (None, None)
    wi = flat(wi_ref)
    wo = flat(wo_ref)
    add_to(out_ref, dot_nn(activ_ref[...], wo), sum_o_ref)
    pre = pre_ref[...]
    grad = (dot_nt(grad_ref[...], wo) * slope(pre, sigmoid(pre))).astype(BF16)
    sum_i_ref[...] = jnp.sum(grad.astype(F32), axis=0, keepdims=True)
    put_sides(di_ref, 0, dot_tn(grad, ffn_ref[...]))
    add_to(ffn_out, dot_nn(grad, wi), sum_f_ref)


UNITS = 512


def cost(micros):
    return pl.CostEstimate(flops=int(micros * SCALE * 1.15e9), bytes_accessed=int(micros * SCALE * 3.3e6), transcendentals=0)


SCALE = 1.0


def shape_of(*dims, dtype=F32):
    return jax.ShapeDtypeStruct(dims, dtype)


def middle(gate_ref, branch_ref, source_ref):
    width = source_ref.shape[-1]
    update = sigmoid(gate_ref[:, :width])
    pre = gate_ref[:, width : 2 * width] + branch_ref[...]
    s = sigmoid(pre)
    return source_ref[...].astype(F32), update, pre, s


def middle_kernel(gate_ref, branch_ref, source_ref, gain_ref, mixed_ref, ffn_ref):
    source, update, pre, s = middle(gate_ref, branch_ref, source_ref)
    mixed = update * (pre * s) + (1.0 - update) * source
    mixed_ref[...] = mixed
    scale = lax.rsqrt(jnp.mean(mixed * mixed, axis=-1, keepdims=True) + EPSILON)
    ffn_ref[...] = (mixed * scale * gain_ref[...]).astype(BF16)


def column_sums(v):
    return jnp.sum(v.reshape(-1, 8, v.shape[-1]), axis=0)


def middle_back_kernel(
    before, gate_ref, branch_ref, source_ref, gain_ref, bias_ref, mixed_ref, feed_ref, grad_ref, ffn_ref,
    out_ref, base_ref, gates_ref, sum_gain_ref, sum_out_ref, sum_gates_ref,
):
    width = source_ref.shape[-1]
    source, update, pre, s = middle(gate_ref, branch_ref, source_ref)
    mixed = mixed_ref[...]
    out_ref[...] = (mixed + feed_ref[...] + bias_ref[...]).astype(BF16)
    scale = lax.rsqrt(jnp.mean(mixed * mixed, axis=-1, keepdims=True) + EPSILON)
    scaled = mixed * scale
    grad_out = grad_ref[...].astype(F32)
    grad_ffn = ffn_ref[...]
    add_to(sum_out_ref, column_sums(grad_out))
    add_to(sum_gain_ref, column_sums(grad_ffn * scaled))
    gained = grad_ffn * gain_ref[...]
    grad = grad_out + scale * (gained - scaled * jnp.mean(gained * scaled, axis=-1, keepdims=True))
    base_ref[...] = grad * (1.0 - update)
    grad_update = (grad * (pre * s - source) * update * (1.0 - update)).astype(BF16)
    grad_hidden = (grad * update * slope(pre, s)).astype(BF16)
    gates_ref[:, :width] = grad_update
    gates_ref[:, width:] = grad_hidden
    add_to(
        sum_gates_ref,
        jnp.concatenate([column_sums(grad_update.astype(F32)), column_sums(grad_hidden.astype(F32))], axis=1),
    )


def run_middle(gate, branch, source, gain):
    total, width = source.shape
    rows = lambda n: pl.BlockSpec((BLOCK, n), lambda i: (i, 0))
    line = pl.BlockSpec((1, width), lambda i: (0, 0))
    return pl.pallas_call(
        middle_kernel,
        grid=(total // BLOCK,),
        in_specs=[rows(gate.shape[1]), rows(width), rows(width), line],
        out_specs=[rows(width), rows(width)],
        out_shape=[shape_of(total, width), shape_of(total, width, dtype=BF16)],
        cost_estimate=cost(5),
    )(gate, branch, source, gain[None])


def run_middle_back(token, gate, branch, source, gain, bias, mixed, feed, grad, ffn):
    total, width = source.shape
    rows = lambda n: pl.BlockSpec((BLOCK, n), lambda i: (i, 0))
    line = pl.BlockSpec((1, width), lambda i: (0, 0))
    few = lambda n: pl.BlockSpec((8, n), lambda i: (0, 0))
    wide = rows(width)
    return pl.pallas_call(
        middle_back_kernel,
        grid=(total // BLOCK,),
        in_specs=[
            pl.BlockSpec(memory_space=pl.ANY), rows(gate.shape[1]), wide, wide, line, line, wide, wide, wide, wide
        ],
        out_specs=[wide, wide, rows(2 * width), few(width), few(width), few(2 * width)],
        out_shape=[
            shape_of(total, width, dtype=BF16), shape_of(total, width), shape_of(total, 2 * width, dtype=BF16),
            shape_of(8, width), shape_of(8, width), shape_of(8, 2 * width),
        ],
        cost_estimate=cost(1),
    )(token, gate, branch, source, gain[None], bias[None], mixed, feed, grad, ffn)


def gates_kernel(piece, before, mixed_ref, gates_ref, d_ref):
    grad = dot_tn(mixed_ref[...], gates_ref[...]).astype(BF16)
    half = grad.shape[-1] // 2
    d_ref[0] = grad[:, :half].reshape(d_ref.shape[1:])
    d_ref[1] = grad[:, half:].reshape(d_ref.shape[1:])


def run_gates(which, token, mixed, gates):
    total, width = mixed.shape
    n = which.shape[0]
    block = width // (2 * n)
    return pl.pallas_call(
        gates_kernel,
        grid_spec=pltpu.PrefetchScalarGridSpec(
            num_scalar_prefetch=1,
            grid=(n,),
            in_specs=[
                pl.BlockSpec(memory_space=pl.ANY),
                pl.BlockSpec((total, block), lambda i, p: (0, p[i])),
                pl.BlockSpec(gates.shape, lambda i, p: (0, 0)),
            ],
            out_specs=pl.BlockSpec((2, 1, block, width), lambda i, p: (0, 0, i, 0)),
        ),
        out_shape=shape_of(2, 1, n * block, width, dtype=BF16),
        cost_estimate=cost(1),
    )(which, token, mixed, gates)


class Pieces:
    def __init__(self, gathered, outer, which, tensor, part_f, part_v):
        self.gathered, self.outer, self.which, self.tensor = gathered, outer, which, tensor
        self.part_f, self.part_v = part_f, part_v
        self.width = gathered.shape[-1]

    def units(self, part):
        return self.which.shape[0] * self.tensor * part

    def block(self, part):
        return min(UNITS, self.tensor * part)

    def spec(self, part, row):
        step = self.block(part) // part
        per = self.tensor // step
        return pl.BlockSpec(
            (step, part, self.width), lambda i, p: (p[i // per] * per + i % per, row // part, 0)
        )

    @property
    def w_in(self):
        return self.spec(self.part_f, 0)

    @property
    def w_out(self):
        return self.spec(self.part_f, 0)

    def v(self, k):
        return self.spec(self.part_v, self.part_f + k * self.part_v)


def flat(ref):
    return ref[...].reshape(-1, ref.shape[-1])


def blocked(kernel, micros, pieces, steps, token, in_specs, out_specs, out_shape, *arrays):
    def body(piece, before, *refs):
        kernel(piece, *refs)

    return pl.pallas_call(
        body,
        grid_spec=pltpu.PrefetchScalarGridSpec(
            num_scalar_prefetch=1,
            grid=(steps,),
            in_specs=[pl.BlockSpec(memory_space=pl.ANY), *in_specs],
            out_specs=out_specs,
        ),
        out_shape=out_shape,
        cost_estimate=cost(micros),
    )(pieces.which, token, *arrays)


def block_specs(total, width, block, lead):
    full = pl.BlockSpec((total, width), lambda i, p: (0, 0))
    cols = pl.BlockSpec((total, block), lambda i, p: (0, i))
    line = pl.BlockSpec((1, block), lambda i, p: (0, i))
    grads = pl.BlockSpec((2, lead, block, width // 2), lambda i, p: (0, 0, i, 0))
    return full, cols, line, grads


def run_value(pieces, token, normed, mixed, probs, bv, br):
    total, width = normed.shape
    units, block = pieces.units(pieces.part_v), pieces.block(pieces.part_v)
    full, cols, line, grads = block_specs(total, width, block, 3)
    pairs = pl.BlockSpec(probs.shape, lambda i, p: (0, 0, 0))
    g = pieces.gathered
    return blocked(
        value_kernel, 200, pieces, units // block, token,
        [full, full, pairs, pieces.v(0), pieces.v(1), pieces.v(2), line, line],
        [cols, cols, cols, cols, full],
        [shape_of(total, units)] * 3 + [shape_of(total, units, dtype=BF16), shape_of(total, width)],
        normed, mixed, probs, g, g, g, bv, br,
    )


def run_value_back(pieces, k, micros, token, grad, normed, mixed, probs, kept):
    total, width = normed.shape
    units, block = pieces.units(pieces.part_v), pieces.block(pieces.part_v)
    full, cols, line, grads = block_specs(total, width, block, 3)
    pairs = pl.BlockSpec(probs.shape, lambda i, p: (0, 0, 0))
    g = pieces.gathered
    return blocked(
        value_back_kernel, micros, pieces, units // block, token,
        [
            pl.BlockSpec((total, width), lambda i, p: (0, 1)), full, full, pairs,
            pieces.v(0), pieces.v(1), pieces.v(2), *[pl.BlockSpec((total, block), lambda i, p: (0, k * (units // block) + i))] * 4,
        ],
        [grads, line, line, full, full, pairs],
        [shape_of(2, 3, units, width // 2, dtype=BF16)]
        + [shape_of(1, units)] * 2
        + [shape_of(total, width)] * 2
        + [shape_of(*probs.shape)],
        grad, normed, mixed, probs, g, g, g, *kept,
    )


def run_inner(pieces, token, ffn, grad, bias):
    total, width = ffn.shape
    units, block = pieces.units(pieces.part_f), pieces.block(pieces.part_f)
    full, cols, line, grads = block_specs(total, width, block, 1)
    return blocked(
        inner_kernel, 200, pieces, units // block, token,
        [full, full, pieces.w_in, line],
        [cols, cols, grads],
        [shape_of(total, units), shape_of(total, units, dtype=BF16), shape_of(2, 1, units, width // 2, dtype=BF16)],
        ffn, grad, pieces.gathered, bias,
    )


def run_outer(pieces, token, ffn, grad, pre, activ, *before):
    total, width = ffn.shape
    units, block = pieces.units(pieces.part_f), pieces.block(pieces.part_f)
    full, cols, line, grads = block_specs(total, width, block, 1)
    return blocked(
        outer_kernel, 200, pieces, units // block, token,
        [full, full, pieces.w_in, pieces.w_out, cols, cols, *[full] * len(before)],
        [grads, line, full, full],
        [shape_of(2, 1, units, width // 2, dtype=BF16), shape_of(1, units), shape_of(total, width), shape_of(total, width)],
        ffn, grad, pieces.gathered, pieces.outer, pre, activ, *before,
    )


def call(kernel, outs, scratch, smem, *arrays):
    return pl.pallas_call(
        kernel,
        out_shape=outs,
        in_specs=[pl.BlockSpec(memory_space=pltpu.SMEM)] * smem
        + [pl.BlockSpec(memory_space=pltpu.VMEM)] * (len(arrays) - smem),
        out_specs=jax.tree.map(lambda _: pl.BlockSpec(memory_space=pltpu.VMEM), outs),
        scratch_shapes=scratch,
        cost_estimate=cost(12),
    )(*arrays)


def scan_carry(grid, local, clear, whole, reverse):
    micros, heads = local.shape[:2]
    clear = jnp.broadcast_to(clear[:, None, None, None], (micros, 1, 8, 128))
    entering = jnp.zeros_like(local)
    reach = jnp.ones_like(local)
    total = local
    for mask in grid.tensor:
        got = grid.swap(jnp.concatenate([total, clear], axis=1), mask)
        got_total, got_clear = got[:, :heads], got[:, heads:]
        later = grid.bit(mask) == (0 if reverse else 1)
        entering = jnp.where(later, entering + reach * got_total, entering)
        reach = jnp.where(later, reach * got_clear * whole, reach)
        total = jnp.where(
            later, total + clear * whole * got_total, got_total + got_clear * whole * total
        )
        clear = clear * got_clear
        whole = whole * whole
    return entering


def after(values, *others):
    return lax.optimization_barrier((values, others))[0]


class Term:
    def __init__(self, array, labels, fixed):
        self.array, self.labels, self.fixed = array, labels, fixed


class Reduce:
    def __init__(self, grid, high, dims, still=()):
        self.grid, self.dims, self.still = grid, list(dims), still
        self.labels = ["side", "lead", *self.dims, "u", "h"]
        xs, (lo, *hi) = grid.xs[::-1], grid.tensor
        self.orders = [[*xs, lo], [lo, *xs]], hi[::-1]
        self.step, self.pair = -1, None
        self.high = self.view(high)
        self.raw = [grid.swap(self.high, grid.core)]

    def view(self, v):
        n = len(self.dims)
        return v.reshape(*v.shape[:2], *[2] * n, v.shape[2] >> n, v.shape[3])

    @property
    def steps(self):
        return len(self.orders[0][0]) + len(self.orders[1])

    def add_low(self, low):
        self.low = self.view(low)

    def take(self):
        if self.step < 0:
            self.sides = [[Term(a, self.labels, {"side": s}) for a in (self.low, self.raw[0])] for s in (0, 1)]
            self.left = [list(self.dims), list(self.dims)]
        else:
            for s in (0, 1):
                for t in self.sides[s]:
                    if self.masks[s] in t.labels:
                        t.fixed[self.masks[s]] = 0
                self.left[s] = [d for d in self.left[s] if d != self.masks[s]]
                if len(self.raw) == 2:
                    self.sides[s].append(Term(self.raw[s], ["lead", *self.left[s], "u", "h"], {}))
                elif self.pair is None:
                    self.sides[s].append(Term(self.raw[0], ["lead", *self.left[s], "u", "hh"], {"hh": s}))
                else:
                    names = ["pair", "lead", *self.left[s], "u", "hh"]
                    self.sides[s].append(Term(self.raw[0], names, {"pair": self.pair, "hh": s}))
            self.pair = None
        self.step += 1

    def wanted(self):
        (first, second), hi = self.orders
        k = self.step
        if k == self.steps:
            return [(self.sides[s], {}, self.left[s]) for s in (0, 1)], True
        self.masks = [first[k], second[k]] if k < len(first) else [hi[k - len(first)]] * 2
        return [
            (self.sides[s], {self.masks[s]: 1}, [d for d in self.left[s] if d != self.masks[s]]) for s in (0, 1)
        ], k >= len(first)

    def start(self, sends):
        if len(sends) == 2:
            self.raw = [self.grid.swap(v, m) for v, m in zip(sends, self.masks)]
        else:
            self.raw = [self.grid.swap(sends[0], self.masks[0])]


def place_of(grid, still, fixed, name, sel):
    if name in still:
        masks = [*grid.tensor, *grid.xs]
        return sel[2 * masks.index(name) + fixed[name]]
    return fixed[name]


def picked(grid, still, term, extra, sel):
    v = term.array
    fixed = {**term.fixed, **extra}
    for axis in reversed(range(len(term.labels))):
        name = term.labels[axis]
        if name == "hh":
            half = v.shape[-1] // 2
            v = v[..., fixed[name] * half : (fixed[name] + 1) * half]
        elif name in fixed:
            v = lax.dynamic_index_in_dim(v, place_of(grid, still, fixed, name, sel), axis, False)
    return v.astype(F32)


def point(grid, gates, *sums, behind=None):
    for r in sums:
        r.take()
    outs, tasks = [], []
    for r in sums:
        sides, joined = r.wanted()
        for terms, fixed, left in sides:
            tasks.append((r, terms, fixed, left))
        shapes = []
        for terms, fixed, left in sides:
            low = r.low.shape
            shapes.append((low[1], *[2] * len(left), *low[-2:]))
        if joined:
            outs.append((*shapes[0][:-1], 2 * shapes[0][-1]))
        else:
            outs.extend(shapes)
    pair = [
        k for k in range(len(sums) - 1)
        if 0 < len(sums[k].orders[0][0]) <= sums[k].step < sums[k].steps
        and sums[k].step == sums[k + 1].step and sums[k].low.shape == sums[k + 1].low.shape
    ]
    joined_outs, ranks, k = [], [], 0
    for n, r in enumerate(sums):
        if n - 1 in pair:
            continue
        if n in pair:
            joined_outs.append((2, *outs[k]))
            ranks.append(True)
            k += 2
        else:
            m = 1 if r.step >= len(r.orders[0][0]) else 2
            joined_outs.extend(outs[k : k + m])
            ranks.extend([False] * m)
            k += m
    sel = grid.sel
    fits = all(len(r.dims) <= 4 and r.low.shape[-2] % 32 == 0 for r in sums)
    if fits:
        *values, token = run_point(grid, gates, tasks, joined_outs, ranks, sel)
    else:
        values = []
        sides = [
            sum(picked(grid, r.still, t, {k: v for k, v in fixed.items() if k in t.labels}, sel) for t in terms).astype(BF16)
            for r, terms, fixed, left in tasks
        ]
        for shape in outs:
            v = sides.pop(0)
            values.append(v if v.shape == shape else jnp.concatenate([v, sides.pop(0)], axis=-1))
        for n in pair:
            first = sum(1 if r.step >= len(r.orders[0][0]) else 2 for r in sums[:n]) - sum(m < n for m in pair)
            values[first : first + 2] = [jnp.stack(values[first : first + 2])]
        token = after(jnp.zeros((8, 128), F32), [g[(0,) * g.ndim] for g in gates])
    if behind is not None:
        values, behind = lax.optimization_barrier((values, behind))
    done, skip = [], False
    for k, r in enumerate(sums):
        if skip:
            skip = False
            continue
        if r.step == r.steps:
            done.append(values.pop(0))
        elif k in pair:
            both = grid.swap(values[0], r.masks[0])
            r.raw, r.pair = [both], 0
            sums[k + 1].raw, sums[k + 1].pair = [both], 1
            values, skip = values[1:], True
        else:
            n = 2 if r.step < len(r.orders[0][0]) else 1
            r.start(values[:n])
            values = values[n:]
    if behind is not None:
        return token, behind
    return (token, *done) if done else token


def run_point(grid, gates, tasks, outs, ranks, sel):
    parts = 2
    arrays, specs, layout = [], [], []
    for r, terms, extra, left in tasks:
        mine = []
        for t in terms:
            fixed = {**t.fixed, **{k: v for k, v in extra.items() if k in t.labels}}
            block = []
            for name, size in zip(t.labels, t.array.shape):
                if name == "hh":
                    block.append(size // 2)
                elif name == "u":
                    block.append(size // parts)
                else:
                    block.append(None if name in fixed else size)

            def index(i, p, t=t, fixed=fixed, r=r):
                return tuple(
                    i if name == "u" else place_of(grid, r.still, fixed, name, p) if name in fixed else 0
                    for name in t.labels
                )

            mine.append(len(arrays))
            arrays.append(t.array)
            specs.append(pl.BlockSpec(tuple(block), index))
        layout.append(mine)
    out_specs = []
    for shape in outs:
        block = (*shape[:-2], shape[-2] // parts, shape[-1])
        out_specs.append(pl.BlockSpec(block, lambda i, p, n=len(shape): (*[0] * (n - 2), i, 0)))
    out_specs.append(pl.BlockSpec((8, 128), lambda i, p: (0, 0)))

    def body(p, *refs):
        refs = refs[len(gates) :]
        ins, results = refs[: len(arrays)], refs[len(arrays) :]
        queue = list(layout)
        for ref, rank in zip(results[:-1], ranks):
            for ref in [ref.at[k] for k in (0, 1)] if rank else [ref]:
                first = 0
                while first < ref.shape[-1]:
                    mine = queue.pop(0)
                    total = ins[mine[0]][...].astype(F32)
                    for k in mine[1:]:
                        total = total + ins[k][...].astype(F32)
                    ref[..., first : first + total.shape[-1]] = total.astype(BF16)
                    first += total.shape[-1]
        results[-1][...] = jnp.zeros((8, 128), F32)

    return pl.pallas_call(
        body,
        grid_spec=pltpu.PrefetchScalarGridSpec(
            num_scalar_prefetch=1,
            grid=(parts,),
            in_specs=[pl.BlockSpec(memory_space=pl.ANY)] * len(gates) + specs,
            out_specs=out_specs,
        ),
        out_shape=[shape_of(*shape, dtype=BF16) for shape in outs] + [shape_of(8, 128)],
        cost_estimate=cost(1),
    )(sel, *gates, *arrays)


def ends(result):
    return result if isinstance(result, tuple) else (result,)


def finish(grid, gates, r, value=None):
    while value is None:
        out = point(grid, gates, r)
        value = out[1] if isinstance(out, tuple) else None
    return value


def share_units(grid, part):
    held = part[None]
    masks = [*grid.xs, grid.core]
    for mask in masks:
        held = jnp.concatenate([held, grid.swap(held, mask)], axis=0)
    n = held.shape[0]
    held = held.astype(F32)
    for k, mask in enumerate(masks):
        held = held.reshape(n >> (k + 1), 2, -1, *part.shape)
        held = jnp.where(grid.bit(mask) == 1, held[:, ::-1], held)
    held = held.reshape(n, *part.shape).transpose(1, 0, 2, 3)
    return held.reshape(part.shape[0], -1, part.shape[-1])


def place_kernel(turned, bits, own_ref, x_ref, c_ref, *outs):
    swap_c, swap_x = bits[0] == 1, bits[1] == 1
    outs[-1][...] = jnp.zeros((8, 128), F32)
    for k, turn in enumerate(turned):
        rows = []
        for own, other in ((own_ref[k], x_ref[k]), (c_ref[0, k], c_ref[1, k])):
            own, other = own.astype(F32), other.astype(F32)
            rows.append(jnp.concatenate([jnp.where(swap_x, other, own), jnp.where(swap_x, own, other)], axis=0))
        v = jnp.concatenate(
            [jnp.where(swap_c, rows[1], rows[0]), jnp.where(swap_c, rows[0], rows[1])], axis=0
        )
        outs[k][...] = v.T if turn else v


def share_and_place(grid, parts, turned, zero):
    results = []
    for part, turns in zip(parts, turned):
        if zero is not None:
            part = part + zero
        lead, units, width = part.shape
        if len(grid.xs) > 1 or units % 16:
            rows = share_units(grid, part)
            results.append([r.T if t else r for r, t in zip(rows, turns)])
            continue
        from_x = grid.swap(part, grid.xs[0])
        from_c = grid.swap(jnp.stack([part, from_x]), grid.core)
        results.append(
            pl.pallas_call(
                partial(place_kernel, turns),
                in_specs=[pl.BlockSpec(memory_space=pltpu.SMEM)] + [pl.BlockSpec(memory_space=pltpu.VMEM)] * 3,
                out_specs=[pl.BlockSpec(memory_space=pltpu.VMEM)] * (lead + 1),
                out_shape=[shape_of(*((width, 4 * units) if t else (4 * units, width))) for t in turns] + [shape_of(8, 128)],
                cost_estimate=cost(5),
            )(grid.turns, part, from_x, from_c)
        )
    return results


def pack_kernel(
    bits, before, eta0, eta1, one0, one1, two0, two1, omega0, omega1, gain0, gain1, gates_ref, shared_ref, ffn_ref, out_sum_ref,
    v0, v1, r0, r1, i0, i1, packed_ref, rows,
):
    heads = eta0.shape[0]
    n = heads * 8
    for k, (a, b) in enumerate(((eta0, eta1), (one0, one1), (two0, two1))):
        rows[k * n : (k + 1) * n] = (a[...] + b[...]).reshape(n, 128)
    at = 3 * n

    def line(v, at):
        for j in range(v.shape[-1] // 128):
            rows[at + j : at + j + 1] = v[:, j * 128 : (j + 1) * 128]
        return at + v.shape[-1] // 128

    total = lambda v: jnp.sum(v, axis=0, keepdims=True)
    at = line(total(gain0[...] + gain1[...]), at)
    rows[at : at + 8] = omega0[...] + omega1[...]
    at = line(total(gates_ref[...]), at + 8)
    rows[at : at + 1] = shared_ref[3:4]
    rows[at + 1 : at + 4] = shared_ref[0:3]
    at = line(total(ffn_ref[...]), at + 4)
    at = line(total(out_sum_ref[...]), at)
    core, x = bits[0], bits[1]
    tensor = i0.shape[-1] // 256
    for low, high in ((v0, v1), (r0, r1)):
        for k, ref in enumerate((low, high)):
            for t in range(tensor):
                own, other = (ref[:, (q * tensor + t) * 64 : (q * tensor + t + 1) * 64] for q in (0, 1))
                row = jnp.where(
                    x == 0, jnp.concatenate([own, other], axis=1), jnp.concatenate([other, own], axis=1)
                )
                rows[pl.ds(at + 2 * t + (core ^ k), 1), :] = row
        at += 2 * tensor
    for k, ref in enumerate((i0, i1)):
        for q in (0, 1):
            for t in range(tensor):
                row = ref[:, (q * tensor + t) * 128 : (q * tensor + t + 1) * 128]
                rows[pl.ds(at + 4 * t + 2 * (core ^ k) + (x ^ q), 1), :] = row
    at += 4 * tensor
    rows[at:] = jnp.zeros((rows.shape[0] - at, 128), F32)
    packed_ref[...] = rows[...].astype(BF16)


def run_pack(bits, token, sums, count):
    vmem = pl.BlockSpec(memory_space=pltpu.VMEM)
    return pl.pallas_call(
        pack_kernel,
        in_specs=[pl.BlockSpec(memory_space=pltpu.SMEM), pl.BlockSpec(memory_space=pl.ANY)] + [vmem] * len(sums),
        out_specs=vmem,
        out_shape=shape_of(count, 128, dtype=BF16),
        scratch_shapes=[pltpu.VMEM((count, 128), F32)],
        cost_estimate=cost(4),
    )(bits, token, *sums)


def join_kernel(place, left_ref, right_ref, out_ref, token_ref):
    token_ref[...] = jnp.zeros((8, 128), F32)
    n = left_ref.shape[1]
    out_ref[:, :n] = left_ref[...].astype(F32)
    part = right_ref.shape[1]
    count = out_ref.shape[0] // part
    for k in range(count):
        v = right_ref[place[pl.program_id(0) * count + k]]
        out_ref[k * part : (k + 1) * part, n:] = v.astype(F32)


def join(place, left, right):
    rows, n = left.shape
    block = 256
    return pl.pallas_call(
        join_kernel,
        grid_spec=pltpu.PrefetchScalarGridSpec(
            num_scalar_prefetch=1,
            grid=(rows // block,),
            in_specs=[pl.BlockSpec((block, n), lambda i, p: (i, 0)), pl.BlockSpec(right.shape, lambda i, p: (0, 0, 0))],
            out_specs=[
                pl.BlockSpec((block, n + right.shape[2]), lambda i, p: (i, 0)), pl.BlockSpec((8, 128), lambda i, p: (0, 0))
            ],
        ),
        out_shape=[shape_of(rows, n + right.shape[2]), shape_of(8, 128)],
        cost_estimate=cost(50),
    )(place, left, right)


def sum_flat(grid, packed, hold, last_hold, end_hold):
    held = packed.astype(F32)
    masks = [grid.core, *grid.tensor, *grid.xs]
    for mask in masks:
        if mask == masks[-1]:
            held = tied(held, last_hold)
        low = packed if mask == masks[0] else held.astype(BF16)
        held = low.astype(F32) + grid.swap(low, mask).astype(F32)
        if mask == masks[0]:
            held = tied(held, hold)
    return tied(held, end_hold).reshape(-1)


def every_part(grid, part):
    parts = part
    masks = [grid.core, *grid.tensor, *grid.xs]
    for mask in masks:
        parts = jnp.concatenate([parts, grid.swap(parts, mask)])
    return parts.reshape(grid.count, *part.shape), grid.place


def tied(v, token):
    return (v.reshape(-1, 8, 128) + token.astype(v.dtype)).reshape(v.shape)


def padded(v, size):
    return jnp.concatenate([v, jnp.zeros(-v.size % size, F32)])


def local(
    inputs, resets, cotangent, norm_gain, ema_alpha, ema_damp, ema_beta, ema_eta, ema_omega,
    w_gates, b_gates, qk_gain, q_bias, w_value, b_value, w_reset, b_reset, w_branch, ffn_gain,
    w_in, b_in, w_out, b_out,
):
    grid = Grid()
    micros, rows, width = inputs.shape
    total = micros * rows
    heads = ema_alpha.shape[1]
    rank = lax.axis_index("tensor")
    units_v, units_f = w_value.shape[1], w_in.shape[1]
    n_x = 1 << len(grid.xs)
    split_x = n_x == 2
    core, x_at = grid.bit(grid.core), lax.axis_index("dp") // 2

    half_v, half_f = units_v // 2, units_f // 2

    def chunks(w, half, axis, whole):
        size = half // n_x
        picks = range(n_x) if whole else range(1)
        return jnp.concatenate(
            [lax.dynamic_slice_in_dim(w, core * half + (x_at ^ r) * size, size, axis) for r in picks],
            axis=axis,
        )

    n_tensor = lax.axis_size("tensor")
    part_f, part_v = half_f // n_x, half_v // n_x
    own = lambda w, half, axis: chunks(w, half, axis, False)
    bias = jnp.concatenate([own(b_value, half_v, 0), own(b_reset, half_v, 0), own(b_in, half_f, 0)])
    bias = jnp.zeros((8, width), BF16).at[0, : bias.size].set(bias)
    seed = jnp.concatenate(
        [
            own(w_in, half_f, 1).T, own(w_value, half_v, 1).T, own(w_reset, half_v, 1).T, own(w_branch, half_v, 0),
            bias,
        ]
    )
    gathered = lax.all_gather(seed, AXES, axis=0)
    gathered_out = lax.all_gather(own(w_out, half_f, 0), AXES, axis=0)
    which = [
        jnp.stack([(x_at ^ r) * 2 + c for r in range(n_x)]).astype(jnp.int32) for c in (core, 1 - core)
    ]
    pieces = [Pieces(gathered, gathered_out, w, n_tensor, part_f, part_v) for w in which]
    table = gathered[:, part_f + 3 * part_v].astype(F32).reshape(2 * n_x, n_tensor, width)
    tables = [jnp.stack([lax.dynamic_index_in_dim(table, w[r], 0, False) for r in range(n_x)]) for w in which]
    bias_v = [t[..., :part_v].reshape(1, -1) for t in tables]
    bias_r = [t[..., part_v : 2 * part_v].reshape(1, -1) for t in tables]
    bias_i = [t[..., 2 * part_v : 2 * part_v + part_f].reshape(1, -1) for t in tables]
    dims = [*grid.xs[::-1], *grid.tensor[::-1]]
    still = grid.tensor

    def in_place(low, high):
        d = [grid.core, *dims]
        v = jnp.stack([low, high]).reshape(*[2] * len(d), -1)
        for axis, mask in enumerate(d):
            if mask not in still:
                v = jnp.where(grid.bit(mask) == 1, jnp.flip(v, axis), v)
        want = [*grid.tensor[::-1], grid.core, *grid.xs[::-1]]
        return v.transpose(*[d.index(m) for m in want], len(d)).reshape(-1)

    offsets = rank * rows + jnp.arange(rows)
    flags = jnp.where(offsets[None] == 0, 1, resets).astype(jnp.int32)
    sel = jnp.stack([grid.bit(m) ^ i for m in [*grid.tensor, *grid.xs] for i in (0, 1)]).astype(jnp.int32)
    places = [jnp.stack([2 * x + c for x in range(n_x)]).astype(jnp.int32) for c in (core, 1 - core)]
    devices = jnp.arange(grid.count) ^ grid.index
    place = sum(
        ((devices // mask) % 2) << k for k, mask in enumerate([grid.core, *grid.tensor, *grid.xs])
    ).astype(jnp.int32)
    turns = jnp.stack([core, x_at % 2]).astype(jnp.int32)
    flags, grid.sel, places, which, grid.place, grid.turns = lax.optimization_barrier(
        (flags, sel, places, which, place, turns)
    )
    for p, w in zip(pieces, which):
        p.which = w
    tile = lambda a: a.T.reshape(heads, 8, 128)
    decay = tile(1.0 - ema_alpha * ema_damp)
    feed = tile(ema_alpha * ema_beta)
    tell = tile(ema_eta)
    whole = jnp.exp(rows * jnp.log(decay))[None]
    clear = (jnp.sum(flags, axis=1) == 0).astype(F32)
    source_low = inputs.reshape(total, width)
    laid = jax.ShapeDtypeStruct((total * 8, 128), F32)
    wide = jax.ShapeDtypeStruct((total, width), F32)
    wide_low = jax.ShapeDtypeStruct((total, width), BF16)
    states = jax.ShapeDtypeStruct((micros, heads, 8, 128), F32)
    sums = jax.ShapeDtypeStruct((heads, 8, 128), F32)
    normed_laid, normed_low, final = call(
        norm_kernel, (laid, wide_low, states), [], 1,
        flags, source_low, norm_gain[None], decay, feed,
    )
    start = scan_carry(grid, final, clear, whole, False)
    blended, mixed_low = call(
        blend_kernel, (wide, wide_low), [pltpu.VMEM((total * 8, 128), F32)], 1,
        flags, normed_laid, start, decay, feed, tell, ema_omega.reshape(8, 128),
    )

    source = source_low.astype(F32)
    gate_pre = dot_plain(mixed_low, w_gates) + b_gates
    update = jax.nn.sigmoid(gate_pre[:, :width])
    direct = gate_pre[:, width : 2 * width]
    shared_pre = gate_pre[:, 2 * width :]
    shared = rounded(jax.nn.silu(shared_pre))
    query = (shared * qk_gain[0] + q_bias).astype(BF16)
    key = (shared * qk_gain[1]).astype(BF16)
    blocks = total // BLOCK
    doc = jnp.cumsum(flags.reshape(blocks, BLOCK), axis=1)
    order = jnp.arange(BLOCK)
    allowed = (doc[:, :, None] == doc[:, None, :]) & (order[:, None] >= order[None, :])[None]
    score_scale = query.shape[-1] ** (-0.5)
    query_b, key_b = query.reshape(blocks, BLOCK, -1), key.reshape(blocks, BLOCK, -1)
    scores = jnp.einsum("cik,cjk->cij", query_b, key_b, preferred_element_type=F32) * score_scale
    scores = jnp.where(allowed, scores, -1000000000.0)
    probs = jax.nn.softmax(scores, axis=-1)
    probs_low = probs.astype(BF16)

    both = Pieces(gathered, gathered_out, jnp.concatenate(which), n_tensor, part_f, part_v)
    bias_v, bias_r = jnp.concatenate(bias_v, axis=1), jnp.concatenate(bias_r, axis=1)
    *kept, branch = run_value(both, bias_v, normed_low, mixed_low, probs_low, bias_v, bias_r)
    mixed_out, ffn_low = run_middle(gate_pre, branch, source_low, ffn_gain)
    grad_low = cotangent.reshape(total, width)

    inner = [None, None]
    inner[1] = run_inner(pieces[1], bias_i[1], ffn_low, grad_low, bias_i[1])
    r_out = Reduce(grid, inner[1][2], dims, still)
    inner[0] = run_inner(pieces[0], inner[1][1], ffn_low, grad_low, bias_i[0])
    r_out.add_low(inner[0][2])
    token, gathered_out = point(grid, [], r_out, behind=gathered_out)
    for p in pieces:
        p.outer = gathered_out
    sum_in = [None, None]
    d_high, sum_in[1], feed_out, grad_ffn = run_outer(
        pieces[1], token, ffn_low, grad_low, inner[1][0], inner[1][1]
    )
    r_in = Reduce(grid, d_high, dims, still)
    token = point(grid, [sum_in[1]], r_out)
    d_low, sum_in[0], feed_out, grad_ffn = run_outer(
        pieces[0], token, ffn_low, grad_low, inner[0][0], inner[0][1], feed_out, grad_ffn
    )
    r_in.add_low(d_low)
    token = point(grid, [], r_out, r_in)
    output, grad_source, grad_gates_low, sum_ffn_gain, sum_out, sum_gates = run_middle_back(
        token, gate_pre, branch, source_low, ffn_gain, b_out, mixed_out, feed_out, grad_low, grad_ffn
    )
    bits = [*grid.xs[::-1], grid.core, *grid.tensor[::-1]]
    dims_g = [m for m in bits if m != grid.core]
    if width // (2 * n_x) % 128 == 0:
        d_gates = [None, None]
        d_gates[1] = run_gates(places[1], sum_gates, mixed_low, grad_gates_low)
        r_gates = Reduce(grid, d_gates[1], dims_g, dims_g)
        d_gates[0] = run_gates(places[0], d_gates[1], mixed_low, grad_gates_low)
        r_gates.add_low(d_gates[0])
        token = d_gates[0]
    else:
        c_axis = bits.index(grid.core)
        d_gates = [
            dot_over_rows(mixed_low, side).astype(BF16).reshape(*[2] * len(bits), -1, width)
            for side in (grad_gates_low[:, :width], grad_gates_low[:, width:])
        ]
        half_of = lambda i: jnp.stack(
            [lax.dynamic_index_in_dim(d, i, c_axis, False).reshape(1, width // 2, width) for d in d_gates]
        )
        r_gates = Reduce(grid, half_of(1 - core), dims_g, dims_g)
        r_gates.add_low(half_of(core))
        token = sum_gates

    def run_vb(k, token):
        return run_value_back(
            pieces[k], k, 200 if k == 0 else 1, token, grad_gates_low, normed_low, mixed_low, probs_low, kept
        )

    back = [None, None]
    back[1] = run_vb(1, token)
    r_v = Reduce(grid, back[1][0], dims, still)
    token = point(grid, [back[1][1], *r_out.raw], r_in, r_gates)
    back[0] = run_vb(0, token)
    r_v.add_low(back[0][0])
    token = point(grid, [back[0][1]], r_v, r_gates, r_in)
    grad_laid, left, grad_shared_low, sums_shared = run_shared(
        token, flags, back[0][5], back[1][5], probs, query, key, shared, shared_pre, qk_gain, grad_gates_low, w_gates,
        back[0][3], back[1][3], blended, decay, tell,
    )
    token = point(grid, [left, *r_in.raw], r_gates)
    left = left + token
    d_shared = dot_over_rows(mixed_low, tied(grad_shared_low, token))
    d_shared = d_shared.reshape(*[2] * len(bits), -1, d_shared.shape[-1])

    def fold(v, mask):
        axis, here = bits.index(mask), grid.bit(mask)
        got = grid.swap(lax.dynamic_slice_in_dim(v, 1 - here, 1, axis).astype(BF16), mask)
        return lax.dynamic_slice_in_dim(v, here, 1, axis) + got.astype(F32)

    right = scan_carry(grid, left, clear, whole, True)
    t_first, *t_rest = grid.tensor
    for mask in [grid.core, *grid.xs, t_first]:
        d_shared = fold(d_shared, mask)
    token = point(grid, [right], r_v, r_gates, r_in, r_out)
    d_shared = fold(tied(d_shared, token) if d_shared.shape[-2] % 8 == 0 else d_shared, t_rest[0])
    column = shape_of(8, 128)
    results = []
    for m in range(micros):
        part = slice(m * rows, (m + 1) * rows)
        laid_part = slice(m * rows * 8, (m + 1) * rows * 8)
        results.append(
            run_back(
                m, token, flags, normed_laid, grad_laid, start, right, decay, feed, tell, ema_omega.reshape(8, 128),
                back[0][4], back[1][4], source_low, grad_source, norm_gain[None],
            )
        )
        if m == 0:
            token, *done = ends(point(grid, [results[0][1]], r_gates, r_in, r_out, r_v))
            d_shared = tied(d_shared, token) if d_shared.shape[-2] % 8 == 0 else d_shared
            for mask in t_rest[1:]:
                d_shared = fold(d_shared, mask)
    done_gates = finish(grid, [token], r_gates, *done[:1])
    done_in = finish(grid, [token], r_in, *done[1:2])
    done_out = finish(grid, [token], r_out, *done[2:])
    token_v = point(grid, [results[-1][1]], r_v)
    token_w, *done_v = ends(point(grid, [token_v], r_v))
    done_v = finish(grid, [token_w], r_v, *done_v)
    grad_w_out, grad_w_in = share_and_place(grid, [done_out, done_in], [(False,), (True,)], None)
    grad_w_out, grad_w_in = grad_w_out[0], grad_w_in[0]
    grad_w_gates = lax.all_gather(
        done_gates.reshape(width // grid.count, 2 * width), AXES, axis=0, tiled=True
    )

    z = token_v[0, 0]
    part = d_shared.reshape(width // grid.count, -1)
    part = tied(part, token_w) if part.shape[0] % 8 == 0 else part
    sizes_late = [heads * width] * 3 + [width, width]
    sizes_early = [2 * width + 128, 256, 128, width, width, units_v * n_tensor, units_v * n_tensor, units_f * n_tensor]
    count = -(-sum(sizes_late + sizes_early) // 2048) * 16
    if (part_v, part_f, n_x) == (64, 128, 2):
        by_kind = [r[k] for k in range(1, 4) for r in results]
        packed = run_pack(
            grid.turns, token_v,
            [
                *by_kind, *[r[4] for r in results], *[r[5] for r in results], sum_gates, sums_shared, sum_ffn_gain, sum_out,
                back[0][2], back[1][2], back[0][1], back[1][1], *sum_in,
            ],
            count,
        )
    else:
        spread_in = lambda k: in_place(back[0][k] + z, back[1][k] + z)
        both = [sum(r[k] + z for r in results) for k in range(1, 6)]
        small = [
            *[v.reshape(-1) for v in both[:3]], jnp.sum(both[4], axis=0), both[3].reshape(-1), jnp.sum(sum_gates + z, axis=0),
            sums_shared[3] + z, sums_shared[:2].reshape(-1) + z, sums_shared[2] + z, jnp.sum(sum_ffn_gain + z, axis=0),
            jnp.sum(sum_out + z, axis=0), spread_in(2), spread_in(1), in_place(sum_in[0] + z, sum_in[1] + z),
        ]
        packed = padded(jnp.concatenate(small), count * 128).reshape(-1, 128).astype(BF16)

    def cut_like(v, sizes):
        out, first = [], 0
        for n in sizes:
            out.append(v[first : first + n])
            first += n
        return out

    ((grad_w_branch, grad_w_reset, grad_w_value, *placed),) = share_and_place(grid, [done_v], [(False, True, True)], None)
    parts, place = every_part(grid, part.astype(BF16))
    grad_w_gates, token_j = join(place, grad_w_gates, parts)
    summed = sum_flat(grid, packed, token_w, placed[0] if placed else token_w, token_j)
    last, cut = cut_like(summed, sizes_late), cut_like(summed[sum(sizes_late) :], sizes_early)
    untile = lambda v: v.reshape(heads, width).T
    eta, one, two = (untile(v) for v in last[:3])
    mine = lambda v, n: lax.dynamic_slice_in_dim(v, rank * n, n, 0)
    return (
        output.reshape(inputs.shape),
        jnp.stack([r[0] + z for r in results]),
        last[3],
        ema_beta * one - ema_damp * two,
        -ema_alpha * two,
        ema_alpha * one,
        eta,
        last[4],
        grad_w_gates,
        cut[0],
        cut[1].reshape(2, -1),
        cut[2],
        grad_w_value,
        mine(cut[5], units_v),
        grad_w_reset,
        mine(cut[6], units_v),
        grad_w_branch,
        cut[3],
        grad_w_in,
        mine(cut[7], units_f),
        grad_w_out,
        cut[4],
    )


def solution(mesh):
    rows = P(None, AXES, None)
    col, row, vec, rep = P(None, "tensor"), P("tensor", None), P("tensor"), P()
    return jax.shard_map(
        local,
        mesh=mesh,
        in_specs=(
            rows, P(None, AXES), rows, rep, rep, rep, rep, rep, rep, rep, rep, rep, rep,
            col, vec, col, vec, row, rep, col, vec, row, rep,
        ),
        out_specs=(
            rows, rows, rep, rep, rep, rep, rep, rep, rep, rep, rep, rep,
            col, vec, col, vec, row, rep, col, vec, row, rep,
        ),
        check_vma=False,
    )
```
